32 devices in a mesh: seq: 4 (over z), mp: 8 (over y, x, core).
Axes of the slice: x: 2, y: 2, z: 4, core: 2. Of those that a mesh axis runs over, the one named last changes fastest.
Arguments:
- enc_rows: bfloat16 [1024, 1024], P('seq', 'mp'), may hold values from -6 to 6
- ffn_in: bfloat16 [1024, 65536], P('seq', 'mp'), may hold values from -0.1875 to 0.1875
- ffn_out: bfloat16 [65536, 1024], P('mp', 'seq'), may hold values from -0.03125 to 0.03125
- enc_gain: float32 [1024], replicated, may hold values from 0.25 to 1.75
- final_gain: float32 [1024], replicated, may hold values from 0.25 to 1.75
- sent_lengths: int32 [4, 4], replicated, may hold values from 1 to 128, 256 in all within a row
- group_table: int32 [4, 4], replicated, may hold values from 0 to 3, as said below
- dec_rows: bfloat16 [1024, 1024], P('seq', 'mp'), may hold values from -6 to 6
- dec_gain: float32 [2, 1024], replicated, may hold values from 0.25 to 1.75
- w_query: bfloat16 [2, 1024, 8192], P(None, None, 'mp'), may hold values from -0.1875 to 0.1875
- w_key: bfloat16 [2, 1024, 8192], P(None, None, 'mp'), may hold values from -0.1875 to 0.1875
- w_value: bfloat16 [2, 1024, 8192], P(None, None, 'mp'), may hold values from -0.1875 to 0.1875
- w_output: bfloat16 [2, 8192, 1024], P(None, 'mp'), may hold values from -0.0625 to 0.0625
Outputs:
- dec_out: bfloat16 [1024, 1024], P('seq', 'mp')
The draws below stay inside these ranges and needn't reach their ends.
Inputs may be any that keep to these rules, and one draw needn't show every extreme that they name: `sent_lengths`: each row sums to 256; each row has an entry equal to 128. `group_table`: every row and every column holds each group number exactly once.
All inputs are finite; a program needn't handle non-finite values.
Results may differ from the reference program's by a relative error of at most 0.014.
Values may be sent and summed in bfloat16 or wider, within the bound.
A program may use at most 128 MiB of HBM per device.

```python
import math
import jax
import jax.numpy as jnp
import numpy as np
from jax import lax

D = 1024
FF = 65536
DH = 128
HEADS = 64
LAYERS = 2
ROWS_DEV = 256
TGT_GRP = 256
ENC_ROWS = 1024
SENT_DEV = 4
MAXLEN = 128
TGT_ALL = 1024
HD = 8192
N_SEQ = 4


def draw_group_table(key, part):
    row_perm = jax.random.permutation(jax.random.fold_in(key, 11), N_SEQ)
    col_perm = jax.random.permutation(jax.random.fold_in(key, 12), N_SEQ)
    return ((row_perm[:, None] + col_perm[None, :]) % N_SEQ).astype(jnp.int32)


def draw_w_query(key, part):
    full_shape = (LAYERS, D, HEADS * DH)
    return (jnp.clip(jax.random.normal(key, full_shape, jnp.float32), -6.0, 6.0) * D ** (-0.5)).astype(jnp.bfloat16)


def levels(key, extent, cuts, least, high):
    level, own = 1.0, jax.random.fold_in(key, 6)
    for dim, parts in cuts:
        steps = jnp.exp(jax.random.uniform(jax.random.fold_in(own, dim), (parts,), jnp.float32, least / len(cuts), high / len(cuts)))
        level = level * jnp.repeat(steps, extent[dim] // parts).reshape([-1 if axis == dim else 1 for axis in range(len(extent))])
    return level


def profile(amount, total, reach, skew):
    loads = [(1 << 20) // math.isqrt(standing ** skew) + 1 for standing in range(2, amount + 1)]
    spare, holding = total - reach - (amount - 1), [1] * (amount - 1)
    while spare > 0:
        candidates = [i for i in range(amount - 1) if holding[i] < reach]
        mass, remaining = sum([loads[i] for i in candidates]), spare
        for i in candidates:
            addition = min(reach - holding[i], max(1, remaining * loads[i] // mass), spare)
            holding[i] = holding[i] + addition
            spare = spare - addition
    return np.array([reach] + holding)


def uneven(stream_key, count, total, reach, lean):
    if count == 2:
        one = jax.random.randint(stream_key, (), max(1, total - reach), min(reach, total - 1) + 1)
        return jnp.stack([one, total - one])
    tallies = jnp.asarray(profile(count, total, reach, lean), jnp.int32)
    twos = (count - 1) // 2
    source_of, taker = tallies[1:1 + 2 * twos:2], tallies[2:2 + 2 * twos:2]
    slack = jnp.minimum(source_of - 1, reach - taker)
    shifted = jax.random.randint(jax.random.fold_in(stream_key, 1), (twos,), 0, 1 << 20) % (slack + 1)
    tallies = tallies.at[1:1 + 2 * twos:2].set(source_of - shifted).at[2:2 + 2 * twos:2].set(taker + shifted)
    return tallies[jax.random.permutation(jax.random.fold_in(stream_key, 2), count)]


def centred(own_key, shape, deviation, most, pieces=(), held_as=jnp.bfloat16):
    result = jax.random.normal(own_key, shape, jnp.float32) * deviation
    if len(pieces) > 0:
        result = levels(own_key, shape, pieces, -0.22, 0.18) * result
    return jnp.clip(result, min=-most, max=most).astype(held_as)


def setup_inputs(seed: int = 0) -> dict:
    splits = jax.random.split(jax.random.key(seed), 14)
    return {
        "enc_rows": centred(splits[0], (ENC_ROWS, D), 1.0, 6.0, ((0, 4), (1, 8))),
        "ffn_in": centred(splits[1], (D, FF), D ** -0.5, 0.1875, ((0, 4), (1, 8))),
        "ffn_out": centred(splits[2], (FF, D), (FF // 2) ** -0.5, 0.03125, ((0, 8), (1, 4))),
        "enc_gain": jnp.clip(1.0 + 0.15 * jax.random.normal(splits[3], (D,), jnp.float32), 0.25, 1.75),
        "final_gain": jnp.clip(1.0 + 0.15 * jax.random.normal(splits[4], (D,), jnp.float32), 0.25, 1.75),
        "sent_lengths": jax.vmap(lambda own: uneven(own, SENT_DEV, ROWS_DEV, MAXLEN, 2))(jax.random.split(splits[5], N_SEQ)).reshape((N_SEQ, SENT_DEV)).astype(jnp.int32),
        "group_table": draw_group_table(jax.random.fold_in(splits[13], 71), 0),
        "dec_rows": centred(splits[7], (TGT_ALL, D), 1.0, 6.0, ((0, 4), (1, 8))),
        "dec_gain": jnp.clip(1.0 + 0.15 * jax.random.normal(splits[8], (LAYERS, D), jnp.float32), 0.25, 1.75),
        "w_query": draw_w_query(jax.random.fold_in(splits[13], 71), 0),
        "w_key": centred(splits[10], (LAYERS, D, HD), D ** -0.5, 0.1875, ((2, 8),)),
        "w_value": centred(splits[11], (LAYERS, D, HD), D ** -0.5, 0.1875, ((2, 8),)),
        "w_output": centred(splits[12], (LAYERS, HD, D), HD ** -0.5, 0.0625, ((1, 8),)),
    }


epsilon = 1e-06

def rms_scale(values, gain_row):
    mean_square = lax.optimization_barrier(jnp.mean(values * values, axis=-1, keepdims=True))
    return values * lax.rsqrt(mean_square + epsilon) * gain_row

def reference(enc_rows, ffn_in, ffn_out, enc_gain, final_gain, sent_lengths, group_table, dec_rows, dec_gain, w_query, w_key, w_value, w_output):

    def encode_block(block_rows):
        block_float = block_rows.astype(jnp.float32)
        normed = rms_scale(block_float, enc_gain).astype(jnp.bfloat16)
        hidden = jnp.maximum(jnp.dot(normed, ffn_in, preferred_element_type=jnp.float32), 0.0).astype(jnp.bfloat16)
        encoded = block_float + jnp.dot(hidden, ffn_out, preferred_element_type=jnp.float32)
        return rms_scale(encoded, final_gain).astype(jnp.bfloat16)
    memory = lax.map(encode_block, enc_rows.reshape(N_SEQ, ROWS_DEV, D)).reshape(N_SEQ * ROWS_DEV, D)
    group_ids = jnp.arange(N_SEQ, dtype=jnp.int32)
    starts = (jnp.cumsum(sent_lengths, axis=1) - sent_lengths).astype(jnp.int32)
    matches = group_table[None, :, :] == group_ids[:, None, None]
    chosen_len = lax.optimization_barrier(jnp.sum(jnp.where(matches, sent_lengths[None], 0), axis=2)).astype(jnp.int32)
    chosen_start = lax.optimization_barrier(jnp.sum(jnp.where(matches, starts[None], 0), axis=2)).astype(jnp.int32)
    positions = jnp.arange(MAXLEN, dtype=jnp.int32)
    row_index = (group_ids[None, :, None] * ROWS_DEV + jnp.minimum(chosen_start[:, :, None] + positions[None, None, :], ROWS_DEV - 1)).astype(jnp.int32)
    padded_memory = memory[row_index]
    live_mask = positions[None, None, :] < chosen_len[:, :, None]
    states = dec_rows.astype(jnp.float32).reshape(N_SEQ, N_SEQ, TGT_GRP // N_SEQ, D)

    def decode_group(inputs):
        group_memory, group_mask, state = inputs
        q_rows = state.shape[1]
        for layer_index in range(LAYERS):
            state_half = lax.optimization_barrier(state.astype(jnp.bfloat16))
            normed = rms_scale(state_half.astype(jnp.float32), dec_gain[layer_index]).astype(jnp.bfloat16)
            queries = (jnp.dot(normed, w_query[layer_index], preferred_element_type=jnp.float32) * DH ** (-0.5)).astype(jnp.bfloat16)
            key_rows = jnp.dot(group_memory, w_key[layer_index], preferred_element_type=jnp.float32).astype(jnp.bfloat16)
            value_rows = jnp.dot(group_memory, w_value[layer_index], preferred_element_type=jnp.float32).astype(jnp.bfloat16)
            queries, key_rows, value_rows = lax.optimization_barrier((queries, key_rows, value_rows))
            query_heads = queries.reshape(N_SEQ, q_rows, HEADS, DH).astype(jnp.float32)
            key_heads = key_rows.reshape(N_SEQ, MAXLEN, HEADS, DH).astype(jnp.float32)
            value_heads = value_rows.reshape(N_SEQ, MAXLEN, HEADS, DH).astype(jnp.float32)
            scores = jnp.einsum('sqhd,sthd->shqt', query_heads, key_heads)
            scores = jnp.where(group_mask[:, None, None, :], scores, -jnp.inf)
            weights = lax.optimization_barrier(jax.nn.softmax(scores, axis=-1).astype(jnp.bfloat16))
            attended = jnp.einsum('shqt,sthd->sqhd', weights.astype(jnp.float32), value_heads).astype(jnp.bfloat16)
            attended = attended.reshape(N_SEQ, q_rows, HEADS * DH)
            state = state + jnp.dot(attended, w_output[layer_index], preferred_element_type=jnp.float32)
        return state.astype(jnp.bfloat16)
    outputs = lax.map(decode_group, (padded_memory, live_mask, states))
    return outputs.reshape(N_SEQ * TGT_GRP, D)
```

```python
import functools

import jax
import jax.numpy as jnp
from jax import lax
from jax.experimental import pallas as pl
from jax.experimental.pallas import tpu as pltpu
from jax.sharding import PartitionSpec as P

MESH = pl.DeviceIdType.MESH

D = 1024
DH = 128
LAYERS = 2


epsilon = 1e-06


def rms_scale(values, gain_row):
    mean_square = jnp.mean(values * values, axis=-1, keepdims=True)
    return values * lax.rsqrt(mean_square + epsilon) * gain_row


def flip(index, bits):
    out = index
    for power in (1, 2, 4, 8, 16, 32):
        if bits & power:
            out = out + power - 2 * power * ((out // power) % 2)
    return out


def z_order(count):
    return sorted(range(1, count), key=lambda bits: (bits == 1, bits))


def column_order(n_seq, per_block):
    inner = [block * per_block + j for block in range(1, n_seq - 1) for j in range(per_block)]
    outer = [block * per_block + j for j in range(per_block) for block in (0, n_seq - 1)]
    return inner + outer


def ffn_kernel(
    n_seq,
    n_mp,
    enc_ref,
    gain_ref,
    final_gain_ref,
    lengths_ref,
    table_ref,
    dec_ref,
    dec_gain_ref,
    fin_ref,
    fout_ref,
    wq_ref,
    wk_ref,
    wv_ref,
    wo_ref,
    out_ref,
    enc_all,
    normed,
    win,
    wout,
    hidden,
    part_out,
    part_in,
    tree_out,
    tree_in,
    late_out,
    late_in,
    enc_a,
    enc_b,
    enc_c,
    enc_zs,
    enc_zr,
    enc_ps,
    enc_pr,
    in_s,
    in_r,
    out_s,
    out_r,
    rs_s,
    rs_r,
    tree_s,
    tree_r,
    late_s,
    late_r,
    ag_s,
    ag_r,
    local_sem,
    wq,
    wk,
    wv,
    wo,
    w_sem,
    dec_all,
    dec_normed,
    queries,
    memory,
    square,
    kv_acc,
    keys,
    values,
    attended,
    att_out,
    att_in,
    dec_ps,
    dec_pr,
    att_ps,
    att_pr,
    sel,
    mask,
    own_out_sem,
):
    s = lax.axis_index("seq")
    m = lax.axis_index("mp")
    rows, width = enc_ref.shape
    depth = fin_ref.shape[0]
    units = fin_ref.shape[1] // n_seq
    out_width = fout_ref.shape[1]
    total_rows = rows * n_seq
    per_block = out_width // width

    order = column_order(n_seq, per_block)
    early = (n_seq - 2) * per_block

    barrier = pltpu.get_barrier_semaphore()
    for bits in range(1, n_seq):
        pl.semaphore_signal(barrier, inc=1, device_id=(flip(s, bits), m), device_id_type=MESH)
    for bits in range(1, n_mp):
        pl.semaphore_signal(barrier, inc=1, device_id=(s, flip(m, bits)), device_id_type=MESH)
    pl.semaphore_wait(barrier, n_seq + n_mp - 2)

    my_rows = pl.ds(pl.multiple_of(s * rows, rows), rows)

    def plane_gather(buf, send_sem, recv_sem):
        def copy(slot, bits, peer):
            return pltpu.make_async_remote_copy(
                src_ref=buf.at[slot],
                dst_ref=buf.at[slot],
                send_sem=send_sem.at[bits],
                recv_sem=recv_sem.at[bits],
                device_id=(s, peer),
                device_id_type=MESH,
            )

        across = [bits for bits in range(n_mp - 2, 1, -2)]
        direct = {bits: copy(m, bits, flip(m, bits)) for bits in across + [1]}
        for bits in across + [1]:
            direct[bits].start()

        def finish():
            onward = []
            for bits in reversed(across):
                direct[bits].wait_recv()
                forward = copy(flip(m, bits), bits + 1, flip(m, 1))
                forward.start()
                onward.append(forward)
            direct[1].wait_recv()
            for forward in onward:
                forward.wait()
            for bits in across + [1]:
                direct[bits].wait_send()

        return finish

    def normalise(buf, dst, count, gain, gain_row):
        step = min(256, count)

        def body(i, carry):
            span = pl.ds(pl.multiple_of(i * step, step), step)
            squares = jnp.zeros((step, 1), jnp.float32)
            for k in range(n_mp):
                value = buf[k, span, :].astype(jnp.float32)
                squares = squares + jnp.sum(value * value, axis=1, keepdims=True)
            scale = lax.rsqrt(squares / (n_mp * width) + epsilon)
            for k in range(n_mp):
                cols = pl.ds(k * width, width)
                value = buf[k, span, :].astype(jnp.float32)
                dst[span, cols] = (value * scale * gain[pl.ds(gain_row, 1), cols]).astype(
                    jnp.bfloat16
                )
            return carry

        lax.fori_loop(0, count // step, body, 0)

    def product(left, right, layer, store):
        columns = right.shape[2]
        step = min(256, columns)

        def body(i, carry):
            cols = pl.ds(pl.multiple_of(i * step, step), step)
            store(
                cols, jnp.dot(left[...], right[layer, :, cols], preferred_element_type=jnp.float32)
            )
            return carry

        lax.fori_loop(0, columns // step, body, 0)

    def project_queries(layer):
        def store(cols, value):
            queries[:, cols] = (value * DH ** (-0.5)).astype(jnp.bfloat16)

        product(dec_normed, wq, layer, store)

    def project_part(cols0, count, first):
        step = min(256, wk.shape[2])
        part = pl.ds(cols0, count)

        def body(i, carry):
            cols = pl.ds(pl.multiple_of(i * step, step), step)
            for index, weight in enumerate((wk, wv)):
                value = jnp.dot(
                    memory[:, part], weight[0, part, cols], preferred_element_type=jnp.float32
                )
                if not first:
                    value = value + kv_acc[index, :, cols]
                kv_acc[index, :, cols] = value
            return carry

        lax.fori_loop(0, wk.shape[2] // step, body, 0)

    def row_scale():
        squares = jnp.sum(square[...], axis=1, keepdims=True)
        return lax.rsqrt(squares / (n_mp * width) + epsilon)

    def project_last(cols0, count):
        step = min(256, wk.shape[2])
        part = pl.ds(cols0, count)
        scale = row_scale()

        def body(i, carry):
            cols = pl.ds(pl.multiple_of(i * step, step), step)
            for index, (weight, dst) in enumerate(((wk, keys), (wv, values))):
                value = kv_acc[index, :, cols] + jnp.dot(
                    memory[:, part], weight[0, part, cols], preferred_element_type=jnp.float32
                )
                dst[:, cols] = (value * scale).astype(jnp.bfloat16)
            return carry

        lax.fori_loop(0, wk.shape[2] // step, body, 0)

    def project_memory(layer):
        scale = row_scale()

        def store_key(cols, value):
            keys[:, cols] = (value * scale).astype(jnp.bfloat16)

        def store_value(cols, value):
            values[:, cols] = (value * scale).astype(jnp.bfloat16)

        product(memory, wk, layer, store_key)
        product(memory, wv, layer, store_value)

    slot_rows = sel.shape[1]
    targets = dec_ref.shape[0]
    per_sentence = targets // n_seq
    layers = wq_ref.shape[0]
    heads = wq_ref.shape[2] // DH

    def attend():
        def body(i, carry):
            span = pl.ds(pl.multiple_of(i * per_sentence, per_sentence), per_sentence)
            slot_span = pl.ds(pl.multiple_of(i * slot_rows, slot_rows), slot_rows)
            live = mask[i] > 0.5
            columns = [pl.ds(head * DH, DH) for head in range(heads)]
            scores = [
                lax.dot_general(
                    queries[span, cols],
                    keys[slot_span, cols],
                    (((1,), (1,)), ((), ())),
                    preferred_element_type=jnp.float32,
                )
                for cols in columns
            ]
            scores = [jnp.where(live, score, -jnp.inf) for score in scores]
            tops = [jnp.max(score, axis=1, keepdims=True) for score in scores]
            powers = [jnp.exp(score - top) for score, top in zip(scores, tops)]
            sums = [jnp.sum(power, axis=1, keepdims=True) for power in powers]
            weights = [(power / total).astype(jnp.bfloat16) for power, total in zip(powers, sums)]
            for cols, weight in zip(columns, weights):
                attended[span, cols] = jnp.dot(
                    weight, values[slot_span, cols], preferred_element_type=jnp.float32
                ).astype(jnp.bfloat16)
            return carry

        lax.fori_loop(0, n_seq, body, 0, unroll=n_seq <= 4)

    def att_copy(layer, slot, source):
        return pltpu.make_async_remote_copy(
            src_ref=att_out.at[layer, slot],
            dst_ref=att_in.at[layer, source],
            send_sem=att_ps.at[layer, slot],
            recv_sem=att_pr.at[layer, source],
            device_id=(s, slot),
            device_id_type=MESH,
        )

    def scatter_output(layer):
        step = max(width, 256)

        def body(i, carry):
            chip = (i + m // (step // width) + 1) % (n_mp * width // step)
            cols = pl.ds(pl.multiple_of(chip * step, step), step)
            value = jnp.dot(
                attended[...], wo[layer, :, cols], preferred_element_type=jnp.float32
            ).astype(jnp.bfloat16)
            for j in range(step // width):
                slot = chip * (step // width) + j
                att_out[layer, slot] = value[:, j * width : (j + 1) * width]

                @pl.when(slot != m)
                def _():
                    att_copy(layer, slot, m).start()

            return carry

        lax.fori_loop(0, n_mp * width // step, body, 0)

    def collect_output(layer):
        total = att_out[layer, m].astype(jnp.float32)
        for bits in range(1, n_mp):
            peer = flip(m, bits)
            att_copy(layer, peer, peer).wait_recv()
            total = total + att_in[layer, peer].astype(jnp.float32)
        for bits in range(1, n_mp):
            att_copy(layer, flip(m, bits), m).wait_send()
        return total

    own_enc = pltpu.make_async_copy(enc_ref, enc_all.at[m, my_rows], local_sem.at[0])
    own_enc.start()
    enc_z = []
    for bits in z_order(n_seq):
        copy = pltpu.make_async_remote_copy(
            src_ref=enc_ref,
            dst_ref=enc_all.at[m, my_rows],
            send_sem=enc_zs.at[bits],
            recv_sem=enc_zr.at[bits],
            device_id=(flip(s, bits), m),
            device_id_type=MESH,
        )
        copy.start()
        enc_z.append(copy)

    own_in = pltpu.make_async_copy(
        fin_ref.at[:, pl.ds(pl.multiple_of(s * units, units), units)], win.at[s], local_sem.at[1]
    )
    own_in.start()
    own_out = [
        pltpu.make_async_copy(
            fout_ref.at[
                pl.ds(pl.multiple_of(s * units, units), units), pl.ds(j * width, width)
            ],
            wout.at[s, j],
            own_out_sem.at[j],
        )
        for j in range(per_block)
    ]
    for copy in own_out:
        copy.start()
    in_copies = []
    for bits in z_order(n_seq):
        peer = flip(s, bits)
        copy = pltpu.make_async_remote_copy(
            src_ref=fin_ref.at[:, pl.ds(pl.multiple_of(peer * units, units), units)],
            dst_ref=win.at[s],
            send_sem=in_s.at[bits],
            recv_sem=in_r.at[bits],
            device_id=(peer, m),
            device_id_type=MESH,
        )
        copy.start()
        in_copies.append(copy)
    piece = units // 2

    def out_copy(bits, j, k):
        peer = flip_any(bits)
        return pltpu.make_async_remote_copy(
            src_ref=fout_ref.at[
                pl.ds(pl.multiple_of(peer * units + k * piece, piece), piece),
                pl.ds(j * width, width),
            ],
            dst_ref=wout.at[s, j, pl.ds(k * piece, piece)],
            send_sem=out_s.at[bits, j, k],
            recv_sem=out_r.at[bits, j, k],
            device_id=(peer, m),
            device_id_type=MESH,
        )

    inner = (s % 2 + s // 2) % 2

    def flip_any(bits):
        if isinstance(bits, int):
            return flip(s, bits)
        return flip(s, 2) * (3 - bits) + flip(s, 3) * (bits - 2)

    def across_out(j):
        for k in range(2):
            for bits in (2, 3):
                out_copy(bits, j, k).start()

    for j in range(per_block):
        for k in range(2):
            out_copy(1, j, k).start()

    @pl.when(inner == 1)
    def _():
        for j in range(per_block):
            across_out(j)

    weight_copies = []
    for index, (src, dst) in enumerate(((wq_ref, wq), (wo_ref, wo))):
        copy = pltpu.make_async_copy(src, dst, w_sem.at[index])
        copy.start()
        weight_copies.append(copy)
    for index, (src, dst) in enumerate(((wk_ref, wk), (wv_ref, wv))):
        for slot, source in enumerate(order):
            copy = pltpu.make_async_copy(
                src.at[:, pl.ds(source * width, width)],
                dst.at[:, pl.ds(slot * width, width)],
                w_sem.at[2 + index * n_mp + slot],
            )
            copy.start()
            weight_copies.append(copy)
    own_dec = pltpu.make_async_copy(dec_ref, dec_all.at[0, m], local_sem.at[3])
    own_dec.start()
    own_dec.wait()
    finish_dec = plane_gather(dec_all.at[0], dec_ps.at[0], dec_pr.at[0])

    own_enc.wait()
    for copy in enc_z:
        copy.wait()

    plane_gather(enc_all, enc_ps, enc_pr)()

    chunk = min(256, rows)

    normalise(enc_all, normed, total_rows, gain_ref, 0)

    for source in range(n_seq):
        start = jnp.int32(0)
        before = jnp.int32(0)
        for j in range(n_seq):
            start = start + jnp.where(table_ref[source, j] == s, before, 0)
            before = before + lengths_ref[source, j]
        slot_row = lax.broadcasted_iota(jnp.int32, (slot_rows, rows), 0)
        column = lax.broadcasted_iota(jnp.int32, (slot_rows, rows), 1)
        wanted = jnp.minimum(slot_row + start, rows - 1)
        sel[source] = jnp.where(wanted == column, 1.0, 0.0).astype(jnp.bfloat16)
    for source in range(n_seq):
        length = jnp.int32(0)
        for j in range(n_seq):
            length = length + jnp.where(table_ref[source, j] == s, lengths_ref[source, j], 0)
        slot = lax.broadcasted_iota(jnp.int32, (1, slot_rows), 1)
        mask[source] = jnp.where(slot < length, 1.0, 0.0)

    finish_dec()
    normalise(dec_all.at[0], dec_normed, targets, dec_gain_ref, 0)
    for copy in weight_copies:
        copy.wait()
    project_queries(0)

    own_in.wait()
    for copy in in_copies:
        copy.wait()

    tile = min(256, units)

    def hidden_chunk(i, carry):
        cols = pl.ds(pl.multiple_of((i % (units // tile)) * tile, tile), tile)
        span = pl.ds(pl.multiple_of((i // (units // tile)) * chunk, chunk), chunk)
        acc = jnp.zeros((chunk, tile), jnp.float32)
        for k in range(n_seq):
            acc = acc + jnp.dot(
                normed[span, pl.ds(k * depth, depth)],
                win[k, :, cols],
                preferred_element_type=jnp.float32,
            )
        hidden[span, cols] = jnp.maximum(acc, 0.0).astype(jnp.bfloat16)
        return carry

    lax.fori_loop(0, (total_rows // chunk) * (units // tile), hidden_chunk, 0)

    share = total_rows // n_mp
    per_chunk = chunk // share
    per_source = rows // share
    my_share = pl.ds(pl.multiple_of(m * share, share), share)

    def position(block, j):
        within = (block % 2 + block // 2) % 2
        outside = early + block // (n_seq - 1) + 2 * j
        return within * ((block - 1) * per_block + j) + (1 - within) * outside

    def rs_copy(p, peer, source):
        return pltpu.make_async_remote_copy(
            src_ref=part_out.at[p, pl.ds(pl.multiple_of(peer * share, share), share)],
            dst_ref=part_in.at[p, source],
            send_sem=rs_s.at[p, peer],
            recv_sem=rs_r.at[p, source],
            device_id=(s, peer),
            device_id_type=MESH,
        )

    def send_block(block, j):
        p = position(block, j)

        def rows_chunk(i, carry):
            c = (i + m // per_chunk + 1) % (total_rows // chunk)
            span = pl.ds(pl.multiple_of(c * chunk, chunk), chunk)
            part_out[p, span, :] = jnp.dot(
                hidden[span, :], wout[block, j], preferred_element_type=jnp.float32
            ).astype(jnp.bfloat16)
            for t in range(per_chunk):
                peer = c * per_chunk + t

                @pl.when(peer != m)
                def _():
                    rs_copy(p, peer, m).start()

            return carry

        lax.fori_loop(0, total_rows // chunk, rows_chunk, 0)

    def receive_block(bits, block, j):
        for k in range(2):
            out_copy(bits, j, k).wait_recv()
        send_block(block, j)

    def plane_sum(p):
        total = part_out[p, my_share, :].astype(jnp.float32)
        for bits in range(1, n_mp):
            peer = flip(m, bits)
            rs_copy(p, peer, peer).wait_recv()
            total = total + part_in[p, peer].astype(jnp.float32)
        return total

    def tree_copy(step, p0, count, peer):
        return pltpu.make_async_remote_copy(
            src_ref=tree_out.at[step, pl.ds(p0, count)],
            dst_ref=tree_in.at[step, pl.ds(p0, count)],
            send_sem=tree_s.at[step, p0],
            recv_sem=tree_r.at[step, p0],
            device_id=(peer, m),
            device_id_type=MESH,
        )

    def down_copy(enc_buf, p0):
        return pltpu.make_async_remote_copy(
            src_ref=enc_buf.at[m],
            dst_ref=enc_buf.at[m],
            send_sem=tree_s.at[2, p0],
            recv_sem=tree_r.at[2, p0],
            device_id=(flip(s, 1), m),
            device_id_type=MESH,
        )

    def residual(p):
        return enc_all[order[p], my_share, :].astype(jnp.float32)

    def tree_up(p0, count):
        for p in range(p0, p0 + count):
            tree_out[0, p] = plane_sum(p).astype(jnp.bfloat16)

        @pl.when(inner == 0)
        def _():
            tree_copy(0, p0, count, flip(s, 1)).start()

    def tree_across(p0, count):
        @pl.when(inner == 1)
        def _():
            tree_copy(0, p0, count, flip(s, 1)).wait_recv()
            for p in range(p0, p0 + count):
                tree_out[1, p] = (
                    tree_out[0, p].astype(jnp.float32) + tree_in[0, p].astype(jnp.float32)
                ).astype(jnp.bfloat16)
            tree_copy(1, p0, count, flip(s, 3)).start()

    def tree_down(p0, count, enc_buf):
        @pl.when(inner == 1)
        def _():
            tree_copy(1, p0, count, flip(s, 3)).wait_recv()
            for p in range(p0, p0 + count):
                total = tree_out[1, p].astype(jnp.float32) + tree_in[1, p].astype(jnp.float32)
                enc_buf[m, p - p0] = (total + residual(p)).astype(jnp.bfloat16)
            down_copy(enc_buf, p0).start()

    def tree_gather(p0, enc_buf, index):
        @pl.when(inner == 0)
        def _():
            down_copy(enc_buf, p0).wait_recv()

        return plane_gather(enc_buf, ag_s.at[index], ag_r.at[index])

    def tree_finish(p0, count, enc_buf):
        @pl.when(inner == 0)
        def _():
            tree_copy(0, p0, count, flip(s, 1)).wait_send()

        @pl.when(inner == 1)
        def _():
            tree_copy(1, p0, count, flip(s, 3)).wait_send()
            down_copy(enc_buf, p0).wait_send()

    last = early + 2

    def late_copy(slot, bits):
        return pltpu.make_async_remote_copy(
            src_ref=late_out.at[slot],
            dst_ref=late_in.at[slot, bits],
            send_sem=late_s.at[slot, bits],
            recv_sem=late_r.at[slot, bits],
            device_id=(flip(s, bits), m),
            device_id_type=MESH,
        )

    def late_send(slot):
        late_out[slot] = plane_sum(last + slot).astype(jnp.bfloat16)
        for bits in z_order(n_seq):
            late_copy(slot, bits).start()

    def late_sum():
        for slot in range(2):
            total = late_out[slot].astype(jnp.float32)
            for bits in z_order(n_seq):
                late_copy(slot, bits).wait_recv()
                total = total + late_in[slot, bits].astype(jnp.float32)
            enc_c[m, slot] = (total + residual(last + slot)).astype(jnp.bfloat16)

    def absorb(enc_buf, p0, count):
        for source in range(n_seq):
            span = pl.ds(source * slot_rows, slot_rows)
            total = jnp.zeros((slot_rows, width), jnp.float32)
            for q in range(count):
                block = enc_buf[pl.ds(source * per_source, per_source), q].reshape(rows, width)
                slot = jnp.dot(sel[source], block, preferred_element_type=jnp.float32)
                total = total + slot * slot
                memory[span, pl.ds((p0 + q) * width, width)] = (
                    slot * final_gain_ref[:, pl.ds(order[p0 + q] * width, width)]
                ).astype(jnp.bfloat16)
            if p0 == 0:
                square[span, :] = total
            else:
                square[span, :] = square[span, :] + total

    half = s // 2
    near = 2 - half
    far = 3 - 3 * half
    near_bits = 2 + inner
    far_bits = 3 - inner

    for j in range(per_block):
        own_out[j].wait()
        send_block(s, j)
    for j in range(per_block):
        receive_block(1, flip(s, 1), j)
    late_send(half)
    for j in range(per_block - 1):
        receive_block(near_bits, near, j)
    out_copy(near_bits, per_block - 1, 0).wait_recv()

    @pl.when(inner == 0)
    def _():
        across_out(0)

    out_copy(near_bits, per_block - 1, 1).wait_recv()
    send_block(near, per_block - 1)
    tree_up(0, early)

    @pl.when(inner == 0)
    def _():
        for j in range(1, per_block):
            across_out(j)

    tree_across(0, early)
    tree_down(0, early, enc_a)
    finish_a = tree_gather(0, enc_a, 0)
    receive_block(far_bits, far, 0)
    finish_a()
    tree_up(early, 2)
    absorb(enc_a, 0, early)
    project_part(0, early * width, True)
    for j in range(1, per_block):
        receive_block(far_bits, far, j)
    tree_across(early, 2)
    tree_down(early, 2, enc_b)
    finish_b = tree_gather(early, enc_b, 1)
    late_send(1 - half)
    finish_b()
    absorb(enc_b, early, 2)
    project_part(early * width, 2 * width, False)
    late_sum()
    plane_gather(enc_c, ag_s.at[2], ag_r.at[2])()
    absorb(enc_c, last, 2)
    project_last(last * width, 2 * width)

    for p in range(n_mp):
        for bits in range(1, n_mp):
            rs_copy(p, flip(m, bits), m).wait_send()
    tree_finish(0, early, enc_a)
    tree_finish(early, 2, enc_b)
    for slot in range(2):
        for bits in z_order(n_seq):
            late_copy(slot, bits).wait_send()
    for bits in range(1, n_seq):
        for j in range(per_block):
            for k in range(2):
                out_copy(bits, j, k).wait_send()

    state = dec_ref[...].astype(jnp.float32)
    for layer in range(layers):
        if layer > 0:
            dec_all[layer, m] = state.astype(jnp.bfloat16)
            plane_gather(dec_all.at[layer], dec_ps.at[layer], dec_pr.at[layer])()
            normalise(dec_all.at[layer], dec_normed, targets, dec_gain_ref, layer)
            project_queries(layer)
        attend()
        scatter_output(layer)
        if layer + 1 < layers:
            project_memory(layer + 1)
        state = state + collect_output(layer)
    out_ref[...] = state.astype(out_ref.dtype)


def whole_fast(
    enc_rows,
    ffn_in,
    ffn_out,
    enc_gain,
    final_gain,
    sent_lengths,
    group_table,
    dec_rows,
    dec_gain,
    w_query,
    w_key,
    w_value,
    w_output,
):
    n_seq, n_mp = lax.axis_size("seq"), lax.axis_size("mp")
    rows, width = enc_rows.shape
    depth, units = ffn_in.shape[0], ffn_in.shape[1] // n_seq
    out_width = ffn_out.shape[1]
    total = rows * n_seq
    full = width * n_mp
    targets = dec_rows.shape[0]
    layers, _, heads_width = w_query.shape
    slot_total = 2 * rows
    per_block = out_width // width
    share = total // n_mp
    half = jnp.bfloat16
    dma = pltpu.SemaphoreType.DMA
    return pl.pallas_call(
        functools.partial(ffn_kernel, n_seq, n_mp),
        out_shape=jax.ShapeDtypeStruct(dec_rows.shape, dec_rows.dtype),
        in_specs=[pl.BlockSpec(memory_space=pltpu.VMEM)] * 3
        + [pl.BlockSpec(memory_space=pltpu.SMEM)] * 2
        + [pl.BlockSpec(memory_space=pltpu.VMEM)] * 2
        + [pl.BlockSpec(memory_space=pl.ANY)] * 6,
        out_specs=pl.BlockSpec(memory_space=pltpu.VMEM),
        scratch_shapes=[
            pltpu.VMEM((n_mp, total, width), half),
            pltpu.VMEM((total, full), half),
            pltpu.VMEM((n_seq, depth, units), half),
            pltpu.VMEM((n_seq, per_block, units, width), half),
            pltpu.VMEM((total, units), half),
            pltpu.VMEM((n_mp, total, width), half),
            pltpu.VMEM((n_mp, n_mp, share, width), half),
            pltpu.VMEM((2, n_mp, share, width), half),
            pltpu.VMEM((2, n_mp, share, width), half),
            pltpu.VMEM((2, share, width), half),
            pltpu.VMEM((2, n_seq, share, width), half),
            pltpu.VMEM((n_mp, n_mp - 4, share, width), half),
            pltpu.VMEM((n_mp, 2, share, width), half),
            pltpu.VMEM((n_mp, 2, share, width), half),
            dma((n_seq,)),
            dma((n_seq,)),
            dma((n_mp,)),
            dma((n_mp,)),
            dma((n_seq,)),
            dma((n_seq,)),
            dma((n_seq, per_block, 2)),
            dma((n_seq, per_block, 2)),
            dma((n_mp, n_mp)),
            dma((n_mp, n_mp)),
            dma((3, n_mp)),
            dma((3, n_mp)),
            dma((2, n_seq)),
            dma((2, n_seq)),
            dma((3, n_mp)),
            dma((3, n_mp)),
            dma((4,)),
            pltpu.VMEM(w_query.shape, half),
            pltpu.VMEM(w_key.shape, half),
            pltpu.VMEM(w_value.shape, half),
            pltpu.VMEM(w_output.shape, half),
            dma((2 + 2 * n_mp,)),
            pltpu.VMEM((layers, n_mp, targets, width), half),
            pltpu.VMEM((targets, full), half),
            pltpu.VMEM((targets, heads_width), half),
            pltpu.VMEM((slot_total, full), half),
            pltpu.VMEM((slot_total, width), jnp.float32),
            pltpu.VMEM((2, slot_total, heads_width), jnp.float32),
            pltpu.VMEM((slot_total, heads_width), half),
            pltpu.VMEM((slot_total, heads_width), half),
            pltpu.VMEM((targets, heads_width), half),
            pltpu.VMEM((layers, n_mp, targets, width), half),
            pltpu.VMEM((layers, n_mp, targets, width), half),
            dma((layers, n_mp)),
            dma((layers, n_mp)),
            dma((layers, n_mp)),
            dma((layers, n_mp)),
            pltpu.VMEM((n_seq, slot_total // n_seq, rows), half),
            pltpu.VMEM((n_seq, 1, slot_total // n_seq), jnp.float32),
            dma((per_block,)),
        ],
        compiler_params=pltpu.CompilerParams(
            collective_id=0, has_side_effects=True, vmem_limit_bytes=60 * 1024 * 1024
        ),
    )(
        enc_rows,
        enc_gain.reshape(1, full),
        final_gain.reshape(1, full),
        sent_lengths,
        group_table,
        dec_rows,
        dec_gain,
        ffn_in,
        ffn_out,
        w_query,
        w_key,
        w_value,
        w_output,
    )


def fast_shapes(enc_rows, ffn_in, ffn_out, dec_rows, w_query):
    n_seq, n_mp = lax.axis_size("seq"), lax.axis_size("mp")
    power = n_seq == 4 and n_mp == 8 and ffn_out.shape[1] == 2 * enc_rows.shape[1]
    aligned = (
        enc_rows.shape[1] % 128 == 0
        and ffn_in.shape[0] % 128 == 0
        and (ffn_in.shape[1] // n_seq) % 256 == 0
        and ffn_out.shape[1] % enc_rows.shape[1] == 0
        and enc_rows.shape[0] % 256 == 0
        and dec_rows.shape[0] % 256 == 0
        and (2 * enc_rows.shape[0] // n_seq) % 128 == 0
        and w_query.shape[2] % 256 == 0
        and w_query.shape[1] % 256 == 0
    )
    return power and aligned


def shards(
    enc_rows,
    ffn_in,
    ffn_out,
    enc_gain,
    final_gain,
    sent_lengths,
    group_table,
    dec_rows,
    dec_gain,
    w_query,
    w_key,
    w_value,
    w_output,
):
    group_count = lax.axis_size("seq")
    my_group = lax.axis_index("seq")
    col_width = enc_rows.shape[1]
    col_start = lax.axis_index("mp") * col_width
    row_count = enc_rows.shape[0]
    max_length = 2 * row_count // group_count
    fast = fast_shapes(enc_rows, ffn_in, ffn_out, dec_rows, w_query)
    if not fast:
        whole_rows = lax.all_gather(enc_rows, "mp", axis=1, tiled=True)
        normed = rms_scale(whole_rows.astype(jnp.float32), enc_gain).astype(jnp.bfloat16)
        full_in = lax.all_gather(ffn_in, "seq", axis=0, tiled=True)
        inner = jnp.dot(normed, full_in, preferred_element_type=jnp.float32)
        hidden = jnp.maximum(inner, 0.0).astype(jnp.bfloat16)
        partial_out = jnp.dot(
            hidden,
            lax.all_gather(ffn_out, "seq", axis=1, tiled=True),
            preferred_element_type=jnp.float32,
        )
    my_lengths = lax.dynamic_index_in_dim(sent_lengths, my_group, 0, keepdims=False)
    my_targets = lax.dynamic_index_in_dim(group_table, my_group, 0, keepdims=False)
    ordinal = jnp.arange(group_count, dtype=jnp.int32)
    my_starts = jnp.sum(
        jnp.where(ordinal[None, :] < ordinal[:, None], my_lengths[None, :], 0), axis=1
    )
    group_ids = jnp.arange(group_count, dtype=jnp.int32)
    matches = my_targets[None, :] == group_ids[:, None]
    send_starts = jnp.sum(jnp.where(matches, my_starts[None, :], 0), axis=1)
    positions = jnp.arange(max_length, dtype=jnp.int32)
    row_index = jnp.minimum(send_starts[:, None] + positions[None, :], row_count - 1)
    recv_lengths = jnp.sum(jnp.where(group_table == my_group, sent_lengths, 0), axis=1)
    live_mask = positions[None, :] < recv_lengths[:, None]
    if fast:
        return whole_fast(
            enc_rows,
            ffn_in,
            ffn_out,
            enc_gain,
            final_gain,
            sent_lengths,
            group_table,
            dec_rows,
            dec_gain,
            w_query,
            w_key,
            w_value,
            w_output,
        )
    kv_width = w_key.shape[2]
    weight_list = []
    for layer_index in range(LAYERS):
        weight_list.append(w_key[layer_index])
        weight_list.append(w_value[layer_index])
    enc_share = lax.psum_scatter(partial_out, "mp", scatter_dimension=1, tiled=True)
    encoded = enc_rows.astype(jnp.float32) + enc_share
    squares = lax.psum(jnp.sum(encoded * encoded, axis=1), "mp")
    gain_part = lax.dynamic_slice_in_dim(final_gain, col_start, col_width, 0)
    memory = (encoded * lax.rsqrt(squares / D + epsilon)[:, None] * gain_part).astype(jnp.bfloat16)
    blocks = memory[row_index]
    gathered = lax.all_gather(
        lax.all_to_all(blocks, "seq", split_axis=0, concat_axis=0, tiled=True),
        "mp",
        axis=2,
        tiled=True,
    )
    projected = tuple(
        (
            jnp.einsum(
                "std,de->ste", gathered, weight_matrix, preferred_element_type=jnp.float32
            ).astype(jnp.bfloat16)
            for weight_matrix in weight_list
        )
    )
    tgt_rows = dec_rows.shape[0]
    per_sentence = tgt_rows // group_count
    local_heads = kv_width // DH
    final_state = dec_rows.astype(jnp.float32)
    for layer_index in range(LAYERS):
        state_half = lax.all_gather(final_state.astype(jnp.bfloat16), "mp", axis=1, tiled=True)
        normed_rows = rms_scale(state_half.astype(jnp.float32), dec_gain[layer_index]).astype(
            jnp.bfloat16
        )
        queries = (
            jnp.dot(normed_rows, w_query[layer_index], preferred_element_type=jnp.float32)
            * DH ** (-0.5)
        ).astype(jnp.bfloat16)
        query_heads = queries.reshape(group_count, per_sentence, local_heads, DH)
        key_heads = projected[2 * layer_index].reshape(group_count, max_length, local_heads, DH)
        value_heads = projected[2 * layer_index + 1].reshape(
            group_count, max_length, local_heads, DH
        )
        scores = jnp.einsum(
            "sqhd,sthd->shqt", query_heads, key_heads, preferred_element_type=jnp.float32
        )
        scores = jnp.where(live_mask[:, None, None, :], scores, -jnp.inf)
        weights = jax.nn.softmax(scores, axis=-1).astype(jnp.bfloat16)
        attended = jnp.einsum(
            "shqt,sthd->sqhd", weights, value_heads, preferred_element_type=jnp.float32
        ).astype(jnp.bfloat16)
        final_state = final_state + lax.psum_scatter(
            jnp.dot(
                attended.reshape(tgt_rows, kv_width),
                w_output[layer_index],
                preferred_element_type=jnp.float32,
            ).astype(jnp.bfloat16),
            "mp",
            scatter_dimension=1,
            tiled=True,
        ).astype(jnp.float32)
    return final_state.astype(jnp.bfloat16)


def solution(mesh):
    in_specs = (
        P("seq", "mp"),
        P("seq", "mp"),
        P("mp", "seq"),
        P(),
        P(),
        P(),
        P(),
        P("seq", "mp"),
        P(),
        P(None, None, "mp"),
        P(None, None, "mp"),
        P(None, None, "mp"),
        P(None, "mp", None),
    )
    out_specs = P("seq", "mp")
    return jax.shard_map(shards, mesh=mesh, in_specs=in_specs, out_specs=out_specs, check_vma=False)
```

```python
import functools

import jax
import jax.numpy as jnp
from jax import lax
from jax.experimental import pallas as pl
from jax.experimental.pallas import tpu as pltpu
from jax.sharding import PartitionSpec as P

MESH = pl.DeviceIdType.MESH

D = 1024
DH = 128
LAYERS = 2


epsilon = 1e-06


def rms_scale(values, gain_row):
    mean_square = jnp.mean(values * values, axis=-1, keepdims=True)
    return values * lax.rsqrt(mean_square + epsilon) * gain_row


def flip(index, bits):
    out = index
    for power in (1, 2, 4, 8, 16, 32):
        if bits & power:
            out = out + power - 2 * power * ((out // power) % 2)
    return out


def z_order(count):
    return sorted(range(1, count), key=lambda bits: (bits == 1, bits))


def column_order(n_seq, per_block):
    inner = [block * per_block + j for block in range(1, n_seq - 1) for j in range(per_block)]
    outer = [block * per_block + j for j in range(per_block) for block in (0, n_seq - 1)]
    return inner + outer


def ffn_kernel(
    n_seq,
    n_mp,
    enc_ref,
    gain_ref,
    final_gain_ref,
    lengths_ref,
    table_ref,
    dec_ref,
    dec_gain_ref,
    fin_ref,
    fout_ref,
    wq_ref,
    wk_ref,
    wv_ref,
    wo_ref,
    out_ref,
    enc_all,
    normed,
    win,
    wout,
    hidden,
    part_out,
    part_in,
    tree_out,
    tree_in,
    enc_a,
    enc_b,
    enc_c,
    enc_zs,
    enc_zr,
    enc_ps,
    enc_pr,
    in_s,
    in_r,
    out_s,
    out_r,
    rs_s,
    rs_r,
    tree_s,
    tree_r,
    ag_s,
    ag_r,
    local_sem,
    wq,
    wk,
    wv,
    wo,
    w_sem,
    dec_all,
    dec_normed,
    queries,
    memory,
    square,
    kv_acc,
    keys,
    values,
    attended,
    att_out,
    att_in,
    dec_ps,
    dec_pr,
    att_ps,
    att_pr,
    sel,
    mask,
    own_out_sem,
):
    s = lax.axis_index("seq")
    m = lax.axis_index("mp")
    rows, width = enc_ref.shape
    depth = fin_ref.shape[0]
    units = fin_ref.shape[1] // n_seq
    out_width = fout_ref.shape[1]
    total_rows = rows * n_seq
    per_block = out_width // width

    order = column_order(n_seq, per_block)
    early = (n_seq - 2) * per_block

    barrier = pltpu.get_barrier_semaphore()
    for bits in range(1, n_seq):
        pl.semaphore_signal(barrier, inc=1, device_id=(flip(s, bits), m), device_id_type=MESH)
    for bits in range(1, n_mp):
        pl.semaphore_signal(barrier, inc=1, device_id=(s, flip(m, bits)), device_id_type=MESH)
    pl.semaphore_wait(barrier, n_seq + n_mp - 2)

    my_rows = pl.ds(pl.multiple_of(s * rows, rows), rows)

    def plane_gather(buf, send_sem, recv_sem):
        def copy(slot, bits, peer):
            return pltpu.make_async_remote_copy(
                src_ref=buf.at[slot],
                dst_ref=buf.at[slot],
                send_sem=send_sem.at[bits],
                recv_sem=recv_sem.at[bits],
                device_id=(s, peer),
                device_id_type=MESH,
            )

        across = [bits for bits in range(n_mp - 2, 1, -2)]
        direct = {bits: copy(m, bits, flip(m, bits)) for bits in across + [1]}
        for bits in across + [1]:
            direct[bits].start()

        def finish():
            onward = []
            for bits in reversed(across):
                direct[bits].wait_recv()
                forward = copy(flip(m, bits), bits + 1, flip(m, 1))
                forward.start()
                onward.append(forward)
            direct[1].wait_recv()
            for forward in onward:
                forward.wait()
            for bits in across + [1]:
                direct[bits].wait_send()

        return finish

    def normalise(buf, dst, count, gain, gain_row):
        step = min(256, count)

        def body(i, carry):
            span = pl.ds(pl.multiple_of(i * step, step), step)
            squares = jnp.zeros((step, 1), jnp.float32)
            for k in range(n_mp):
                value = buf[k, span, :].astype(jnp.float32)
                squares = squares + jnp.sum(value * value, axis=1, keepdims=True)
            scale = lax.rsqrt(squares / (n_mp * width) + epsilon)
            for k in range(n_mp):
                cols = pl.ds(k * width, width)
                value = buf[k, span, :].astype(jnp.float32)
                dst[span, cols] = (value * scale * gain[pl.ds(gain_row, 1), cols]).astype(
                    jnp.bfloat16
                )
            return carry

        lax.fori_loop(0, count // step, body, 0)

    def product(left, right, layer, store):
        columns = right.shape[2]
        step = min(256, columns)

        def body(i, carry):
            cols = pl.ds(pl.multiple_of(i * step, step), step)
            store(
                cols, jnp.dot(left[...], right[layer, :, cols], preferred_element_type=jnp.float32)
            )
            return carry

        lax.fori_loop(0, columns // step, body, 0)

    def project_queries(layer):
        def store(cols, value):
            queries[:, cols] = (value * DH ** (-0.5)).astype(jnp.bfloat16)

        product(dec_normed, wq, layer, store)

    def project_part(cols0, count, first):
        step = min(256, wk.shape[2])
        part = pl.ds(cols0, count)

        def body(i, carry):
            cols = pl.ds(pl.multiple_of(i * step, step), step)
            for index, weight in enumerate((wk, wv)):
                value = jnp.dot(
                    memory[:, part], weight[0, part, cols], preferred_element_type=jnp.float32
                )
                if not first:
                    value = value + kv_acc[index, :, cols]
                kv_acc[index, :, cols] = value
            return carry

        lax.fori_loop(0, wk.shape[2] // step, body, 0)

    def row_scale():
        squares = jnp.sum(square[...], axis=1, keepdims=True)
        return lax.rsqrt(squares / (n_mp * width) + epsilon)

    def project_last(cols0, count):
        step = min(256, wk.shape[2])
        part = pl.ds(cols0, count)
        scale = row_scale()

        def body(i, carry):
            cols = pl.ds(pl.multiple_of(i * step, step), step)
            for index, (weight, dst) in enumerate(((wk, keys), (wv, values))):
                value = kv_acc[index, :, cols] + jnp.dot(
                    memory[:, part], weight[0, part, cols], preferred_element_type=jnp.float32
                )
                dst[:, cols] = (value * scale).astype(jnp.bfloat16)
            return carry

        lax.fori_loop(0, wk.shape[2] // step, body, 0)

    def project_memory(layer):
        scale = row_scale()

        def store_key(cols, value):
            keys[:, cols] = (value * scale).astype(jnp.bfloat16)

        def store_value(cols, value):
            values[:, cols] = (value * scale).astype(jnp.bfloat16)

        product(memory, wk, layer, store_key)
        product(memory, wv, layer, store_value)

    slot_rows = sel.shape[1]
    targets = dec_ref.shape[0]
    per_sentence = targets // n_seq
    layers = wq_ref.shape[0]
    heads = wq_ref.shape[2] // DH

    def attend():
        def body(i, carry):
            span = pl.ds(pl.multiple_of(i * per_sentence, per_sentence), per_sentence)
            slot_span = pl.ds(pl.multiple_of(i * slot_rows, slot_rows), slot_rows)
            live = mask[i] > 0.5
            columns = [pl.ds(head * DH, DH) for head in range(heads)]
            scores = [
                lax.dot_general(
                    queries[span, cols],
                    keys[slot_span, cols],
                    (((1,), (1,)), ((), ())),
                    preferred_element_type=jnp.float32,
                )
                for cols in columns
            ]
            scores = [jnp.where(live, score, -jnp.inf) for score in scores]
            tops = [jnp.max(score, axis=1, keepdims=True) for score in scores]
            powers = [jnp.exp(score - top) for score, top in zip(scores, tops)]
            sums = [jnp.sum(power, axis=1, keepdims=True) for power in powers]
            weights = [(power / total).astype(jnp.bfloat16) for power, total in zip(powers, sums)]
            for cols, weight in zip(columns, weights):
                attended[span, cols] = jnp.dot(
                    weight, values[slot_span, cols], preferred_element_type=jnp.float32
                ).astype(jnp.bfloat16)
            return carry

        lax.fori_loop(0, n_seq, body, 0, unroll=n_seq <= 4)

    def att_copy(layer, slot, source):
        return pltpu.make_async_remote_copy(
            src_ref=att_out.at[layer, slot],
            dst_ref=att_in.at[layer, source],
            send_sem=att_ps.at[layer, slot],
            recv_sem=att_pr.at[layer, source],
            device_id=(s, slot),
            device_id_type=MESH,
        )

    def scatter_output(layer):
        step = max(width, 256)

        def body(i, carry):
            chip = (i + m // (step // width) + 1) % (n_mp * width // step)
            cols = pl.ds(pl.multiple_of(chip * step, step), step)
            value = jnp.dot(
                attended[...], wo[layer, :, cols], preferred_element_type=jnp.float32
            ).astype(jnp.bfloat16)
            for j in range(step // width):
                slot = chip * (step // width) + j
                att_out[layer, slot] = value[:, j * width : (j + 1) * width]

                @pl.when(slot != m)
                def _():
                    att_copy(layer, slot, m).start()

            return carry

        lax.fori_loop(0, n_mp * width // step, body, 0)

    def collect_output(layer):
        total = att_out[layer, m].astype(jnp.float32)
        for bits in range(1, n_mp):
            peer = flip(m, bits)
            att_copy(layer, peer, peer).wait_recv()
            total = total + att_in[layer, peer].astype(jnp.float32)
        for bits in range(1, n_mp):
            att_copy(layer, flip(m, bits), m).wait_send()
        return total

    own_enc = pltpu.make_async_copy(enc_ref, enc_all.at[m, my_rows], local_sem.at[0])
    own_enc.start()
    enc_z = []
    for bits in z_order(n_seq):
        copy = pltpu.make_async_remote_copy(
            src_ref=enc_ref,
            dst_ref=enc_all.at[m, my_rows],
            send_sem=enc_zs.at[bits],
            recv_sem=enc_zr.at[bits],
            device_id=(flip(s, bits), m),
            device_id_type=MESH,
        )
        copy.start()
        enc_z.append(copy)

    own_in = pltpu.make_async_copy(
        fin_ref.at[:, pl.ds(pl.multiple_of(s * units, units), units)], win.at[s], local_sem.at[1]
    )
    own_in.start()
    own_out = [
        pltpu.make_async_copy(
            fout_ref.at[
                pl.ds(pl.multiple_of(s * units, units), units), pl.ds(j * width, width)
            ],
            wout.at[s, j],
            own_out_sem.at[j],
        )
        for j in range(per_block)
    ]
    for copy in own_out:
        copy.start()
    in_copies = []
    for bits in z_order(n_seq):
        peer = flip(s, bits)
        copy = pltpu.make_async_remote_copy(
            src_ref=fin_ref.at[:, pl.ds(pl.multiple_of(peer * units, units), units)],
            dst_ref=win.at[s],
            send_sem=in_s.at[bits],
            recv_sem=in_r.at[bits],
            device_id=(peer, m),
            device_id_type=MESH,
        )
        copy.start()
        in_copies.append(copy)
    piece = units // 2

    def out_copy(bits, j, k):
        peer = flip_any(bits)
        return pltpu.make_async_remote_copy(
            src_ref=fout_ref.at[
                pl.ds(pl.multiple_of(peer * units + k * piece, piece), piece),
                pl.ds(j * width, width),
            ],
            dst_ref=wout.at[s, j, pl.ds(k * piece, piece)],
            send_sem=out_s.at[bits, j, k],
            recv_sem=out_r.at[bits, j, k],
            device_id=(peer, m),
            device_id_type=MESH,
        )

    inner = (s % 2 + s // 2) % 2

    def flip_any(bits):
        if isinstance(bits, int):
            return flip(s, bits)
        return flip(s, 2) * (3 - bits) + flip(s, 3) * (bits - 2)

    def across_out(j, k):
        for bits in (3, 2):
            out_copy(bits, j, k).start()

    for j in range(per_block):
        for k in range(2):
            out_copy(1, j, k).start()

    @pl.when(inner == 1)
    def _():
        for j in range(per_block):
            for k in range(2):
                across_out(j, k)

    weight_copies = []
    for index, (src, dst) in enumerate(((wq_ref, wq), (wo_ref, wo))):
        copy = pltpu.make_async_copy(src, dst, w_sem.at[index])
        copy.start()
        weight_copies.append(copy)
    for index, (src, dst) in enumerate(((wk_ref, wk), (wv_ref, wv))):
        for slot, source in enumerate(order):
            copy = pltpu.make_async_copy(
                src.at[:, pl.ds(source * width, width)],
                dst.at[:, pl.ds(slot * width, width)],
                w_sem.at[2 + index * n_mp + slot],
            )
            copy.start()
            weight_copies.append(copy)
    own_dec = pltpu.make_async_copy(dec_ref, dec_all.at[0, m], local_sem.at[3])
    own_dec.start()
    own_dec.wait()
    finish_dec = plane_gather(dec_all.at[0], dec_ps.at[0], dec_pr.at[0])

    own_enc.wait()
    for copy in enc_z:
        copy.wait()

    plane_gather(enc_all, enc_ps, enc_pr)()

    chunk = min(256, rows)

    normalise(enc_all, normed, total_rows, gain_ref, 0)

    for source in range(n_seq):
        start = jnp.int32(0)
        before = jnp.int32(0)
        for j in range(n_seq):
            start = start + jnp.where(table_ref[source, j] == s, before, 0)
            before = before + lengths_ref[source, j]
        slot_row = lax.broadcasted_iota(jnp.int32, (slot_rows, rows), 0)
        column = lax.broadcasted_iota(jnp.int32, (slot_rows, rows), 1)
        wanted = jnp.minimum(slot_row + start, rows - 1)
        sel[source] = jnp.where(wanted == column, 1.0, 0.0).astype(jnp.bfloat16)
    for source in range(n_seq):
        length = jnp.int32(0)
        for j in range(n_seq):
            length = length + jnp.where(table_ref[source, j] == s, lengths_ref[source, j], 0)
        slot = lax.broadcasted_iota(jnp.int32, (1, slot_rows), 1)
        mask[source] = jnp.where(slot < length, 1.0, 0.0)

    finish_dec()
    normalise(dec_all.at[0], dec_normed, targets, dec_gain_ref, 0)
    for copy in weight_copies:
        copy.wait()
    project_queries(0)

    own_in.wait()
    for copy in in_copies:
        copy.wait()

    tile = min(256, units)

    def hidden_chunk(i, carry):
        cols = pl.ds(pl.multiple_of((i % (units // tile)) * tile, tile), tile)
        span = pl.ds(pl.multiple_of((i // (units // tile)) * chunk, chunk), chunk)
        acc = jnp.zeros((chunk, tile), jnp.float32)
        for k in range(n_seq):
            acc = acc + jnp.dot(
                normed[span, pl.ds(k * depth, depth)],
                win[k, :, cols],
                preferred_element_type=jnp.float32,
            )
        hidden[span, cols] = jnp.maximum(acc, 0.0).astype(jnp.bfloat16)
        return carry

    lax.fori_loop(0, (total_rows // chunk) * (units // tile), hidden_chunk, 0)

    share = total_rows // n_mp
    per_chunk = chunk // share
    per_source = rows // share
    my_share = pl.ds(pl.multiple_of(m * share, share), share)

    def position(block, j):
        within = (block % 2 + block // 2) % 2
        outside = early + block // (n_seq - 1) + 2 * j
        return within * ((block - 1) * per_block + j) + (1 - within) * outside

    def rs_copy(p, peer, source):
        return pltpu.make_async_remote_copy(
            src_ref=part_out.at[p, pl.ds(pl.multiple_of(peer * share, share), share)],
            dst_ref=part_in.at[p, source],
            send_sem=rs_s.at[p, peer],
            recv_sem=rs_r.at[p, source],
            device_id=(s, peer),
            device_id_type=MESH,
        )

    def send_block(block, j):
        p = position(block, j)

        def rows_chunk(i, carry):
            c = (i + m // per_chunk + 1) % (total_rows // chunk)
            span = pl.ds(pl.multiple_of(c * chunk, chunk), chunk)
            part_out[p, span, :] = jnp.dot(
                hidden[span, :], wout[block, j], preferred_element_type=jnp.float32
            ).astype(jnp.bfloat16)
            for t in range(per_chunk):
                peer = c * per_chunk + t

                @pl.when(peer != m)
                def _():
                    rs_copy(p, peer, m).start()

            return carry

        lax.fori_loop(0, total_rows // chunk, rows_chunk, 0)

    def receive_block(bits, block, j):
        for k in range(2):
            out_copy(bits, j, k).wait_recv()
        send_block(block, j)

    def plane_sum(p):
        total = part_out[p, my_share, :].astype(jnp.float32)
        for bits in range(1, n_mp):
            peer = flip(m, bits)
            rs_copy(p, peer, peer).wait_recv()
            total = total + part_in[p, peer].astype(jnp.float32)
        return total

    def tree_copy(bits, p0, count):
        return pltpu.make_async_remote_copy(
            src_ref=tree_out.at[min(bits, 1), pl.ds(p0, count)],
            dst_ref=tree_in.at[min(bits, 2), pl.ds(p0, count)],
            send_sem=tree_s.at[bits, p0],
            recv_sem=tree_r.at[min(bits, 2), p0],
            device_id=(flip(s, max(bits, 1)), m),
            device_id_type=MESH,
        )

    def residual(p):
        return enc_all[order[p], my_share, :].astype(jnp.float32)

    def tree_up(p0, count):
        for p in range(p0, p0 + count):
            tree_out[0, p] = plane_sum(p).astype(jnp.bfloat16)

        @pl.when(inner == 1)
        def _():
            tree_copy(0, p0, count).start()

    def tree_across(p0, count):
        @pl.when(inner == 0)
        def _():
            tree_copy(0, p0, count).wait_recv()
            for p in range(p0, p0 + count):
                tree_out[1, p] = (
                    tree_out[0, p].astype(jnp.float32) + tree_in[0, p].astype(jnp.float32)
                ).astype(jnp.bfloat16)
            for bits in z_order(n_seq):
                tree_copy(bits, p0, count).start()

    def tree_down(p0, count, enc_buf):
        def combine(own):
            for p in range(p0, p0 + count):
                total = own[p].astype(jnp.float32) + tree_in[2, p].astype(jnp.float32)
                enc_buf[m, p - p0] = (total + residual(p)).astype(jnp.bfloat16)

        tree_copy(2, p0, count).wait_recv()

        @pl.when(inner == 0)
        def _():
            combine(tree_out.at[1])

        @pl.when(inner == 1)
        def _():
            tree_copy(1, p0, count).wait_recv()
            combine(tree_in.at[1])

    def tree_finish(p0, count):
        @pl.when(inner == 1)
        def _():
            tree_copy(0, p0, count).wait_send()

        @pl.when(inner == 0)
        def _():
            for bits in z_order(n_seq):
                tree_copy(bits, p0, count).wait_send()

    last = early + 2

    def absorb(enc_buf, p0, count):
        for source in range(n_seq):
            span = pl.ds(source * slot_rows, slot_rows)
            total = jnp.zeros((slot_rows, width), jnp.float32)
            for q in range(count):
                block = enc_buf[pl.ds(source * per_source, per_source), q].reshape(rows, width)
                slot = jnp.dot(sel[source], block, preferred_element_type=jnp.float32)
                total = total + slot * slot
                memory[span, pl.ds((p0 + q) * width, width)] = (
                    slot * final_gain_ref[:, pl.ds(order[p0 + q] * width, width)]
                ).astype(jnp.bfloat16)
            if p0 == 0:
                square[span, :] = total
            else:
                square[span, :] = square[span, :] + total

    last = early + 2
    near = 2 - s // 2
    far = 3 - 3 * (s // 2)
    near_bits = 2 + inner

    for j in range(per_block):
        own_out[j].wait()
        send_block(s, j)
    for j in range(per_block):
        receive_block(1, flip(s, 1), j)
    for j in range(per_block - 1):
        receive_block(near_bits, near, j)
    out_copy(near_bits, per_block - 1, 0).wait_recv()

    @pl.when(inner == 0)
    def _():
        out_copy(2, 0, 0).start()

    out_copy(near_bits, per_block - 1, 1).wait_recv()

    @pl.when(inner == 0)
    def _():
        out_copy(2, 0, 1).start()
        for k in range(2):
            out_copy(2, 1, k).start()

    send_block(near, per_block - 1)
    tree_up(0, early)
    tree_across(0, early)

    @pl.when(inner == 0)
    def _():
        for j in range(per_block):
            for k in range(2):
                out_copy(3, j, k).start()

    @pl.when(inner == 1)
    def _():
        receive_block(2, far, 0)
        tree_up(early, 2)
        receive_block(2, far, 1)
        tree_up(last, 2)

    tree_down(0, early, enc_a)
    plane_gather(enc_a, ag_s.at[0], ag_r.at[0])()
    absorb(enc_a, 0, early)
    project_part(0, early * width, True)

    @pl.when(inner == 0)
    def _():
        receive_block(3, far, 0)
        tree_up(early, 2)
        tree_across(early, 2)
        receive_block(3, far, 1)

    tree_down(early, 2, enc_b)
    finish_b = plane_gather(enc_b, ag_s.at[1], ag_r.at[1])

    @pl.when(inner == 0)
    def _():
        tree_up(last, 2)
        tree_across(last, 2)

    finish_b()
    absorb(enc_b, early, 2)
    project_part(early * width, 2 * width, False)
    tree_down(last, 2, enc_c)
    plane_gather(enc_c, ag_s.at[2], ag_r.at[2])()
    absorb(enc_c, last, 2)
    project_last(last * width, 2 * width)

    for p in range(n_mp):
        for bits in range(1, n_mp):
            rs_copy(p, flip(m, bits), m).wait_send()
    tree_finish(0, early)
    tree_finish(early, 2)
    tree_finish(last, 2)
    for bits in range(1, n_seq):
        for j in range(per_block):
            for k in range(2):
                out_copy(bits, j, k).wait_send()

    state = dec_ref[...].astype(jnp.float32)
    for layer in range(layers):
        if layer > 0:
            dec_all[layer, m] = state.astype(jnp.bfloat16)
            plane_gather(dec_all.at[layer], dec_ps.at[layer], dec_pr.at[layer])()
            normalise(dec_all.at[layer], dec_normed, targets, dec_gain_ref, layer)
            project_queries(layer)
        attend()
        scatter_output(layer)
        if layer + 1 < layers:
            project_memory(layer + 1)
        state = state + collect_output(layer)
    out_ref[...] = state.astype(out_ref.dtype)


def whole_fast(
    enc_rows,
    ffn_in,
    ffn_out,
    enc_gain,
    final_gain,
    sent_lengths,
    group_table,
    dec_rows,
    dec_gain,
    w_query,
    w_key,
    w_value,
    w_output,
):
    n_seq, n_mp = lax.axis_size("seq"), lax.axis_size("mp")
    rows, width = enc_rows.shape
    depth, units = ffn_in.shape[0], ffn_in.shape[1] // n_seq
    out_width = ffn_out.shape[1]
    total = rows * n_seq
    full = width * n_mp
    targets = dec_rows.shape[0]
    layers, _, heads_width = w_query.shape
    slot_total = 2 * rows
    per_block = out_width // width
    share = total // n_mp
    half = jnp.bfloat16
    dma = pltpu.SemaphoreType.DMA
    return pl.pallas_call(
        functools.partial(ffn_kernel, n_seq, n_mp),
        out_shape=jax.ShapeDtypeStruct(dec_rows.shape, dec_rows.dtype),
        in_specs=[pl.BlockSpec(memory_space=pltpu.VMEM)] * 3
        + [pl.BlockSpec(memory_space=pltpu.SMEM)] * 2
        + [pl.BlockSpec(memory_space=pltpu.VMEM)] * 2
        + [pl.BlockSpec(memory_space=pl.ANY)] * 6,
        out_specs=pl.BlockSpec(memory_space=pltpu.VMEM),
        scratch_shapes=[
            pltpu.VMEM((n_mp, total, width), half),
            pltpu.VMEM((total, full), half),
            pltpu.VMEM((n_seq, depth, units), half),
            pltpu.VMEM((n_seq, per_block, units, width), half),
            pltpu.VMEM((total, units), half),
            pltpu.VMEM((n_mp, total, width), half),
            pltpu.VMEM((n_mp, n_mp, share, width), half),
            pltpu.VMEM((2, n_mp, share, width), half),
            pltpu.VMEM((3, n_mp, share, width), half),
            pltpu.VMEM((n_mp, n_mp - 4, share, width), half),
            pltpu.VMEM((n_mp, 2, share, width), half),
            pltpu.VMEM((n_mp, 2, share, width), half),
            dma((n_seq,)),
            dma((n_seq,)),
            dma((n_mp,)),
            dma((n_mp,)),
            dma((n_seq,)),
            dma((n_seq,)),
            dma((n_seq, per_block, 2)),
            dma((n_seq, per_block, 2)),
            dma((n_mp, n_mp)),
            dma((n_mp, n_mp)),
            dma((4, n_mp)),
            dma((3, n_mp)),
            dma((3, n_mp)),
            dma((3, n_mp)),
            dma((4,)),
            pltpu.VMEM(w_query.shape, half),
            pltpu.VMEM(w_key.shape, half),
            pltpu.VMEM(w_value.shape, half),
            pltpu.VMEM(w_output.shape, half),
            dma((2 + 2 * n_mp,)),
            pltpu.VMEM((layers, n_mp, targets, width), half),
            pltpu.VMEM((targets, full), half),
            pltpu.VMEM((targets, heads_width), half),
            pltpu.VMEM((slot_total, full), half),
            pltpu.VMEM((slot_total, width), jnp.float32),
            pltpu.VMEM((2, slot_total, heads_width), jnp.float32),
            pltpu.VMEM((slot_total, heads_width), half),
            pltpu.VMEM((slot_total, heads_width), half),
            pltpu.VMEM((targets, heads_width), half),
            pltpu.VMEM((layers, n_mp, targets, width), half),
            pltpu.VMEM((layers, n_mp, targets, width), half),
            dma((layers, n_mp)),
            dma((layers, n_mp)),
            dma((layers, n_mp)),
            dma((layers, n_mp)),
            pltpu.VMEM((n_seq, slot_total // n_seq, rows), half),
            pltpu.VMEM((n_seq, 1, slot_total // n_seq), jnp.float32),
            dma((per_block,)),
        ],
        compiler_params=pltpu.CompilerParams(
            collective_id=0, has_side_effects=True, vmem_limit_bytes=60 * 1024 * 1024
        ),
    )(
        enc_rows,
        enc_gain.reshape(1, full),
        final_gain.reshape(1, full),
        sent_lengths,
        group_table,
        dec_rows,
        dec_gain,
        ffn_in,
        ffn_out,
        w_query,
        w_key,
        w_value,
        w_output,
    )


def fast_shapes(enc_rows, ffn_in, ffn_out, dec_rows, w_query):
    n_seq, n_mp = lax.axis_size("seq"), lax.axis_size("mp")
    power = n_seq == 4 and n_mp == 8 and ffn_out.shape[1] == 2 * enc_rows.shape[1]
    aligned = (
        enc_rows.shape[1] % 128 == 0
        and ffn_in.shape[0] % 128 == 0
        and (ffn_in.shape[1] // n_seq) % 256 == 0
        and ffn_out.shape[1] % enc_rows.shape[1] == 0
        and enc_rows.shape[0] % 256 == 0
        and dec_rows.shape[0] % 256 == 0
        and (2 * enc_rows.shape[0] // n_seq) % 128 == 0
        and w_query.shape[2] % 256 == 0
        and w_query.shape[1] % 256 == 0
    )
    return power and aligned


def shards(
    enc_rows,
    ffn_in,
    ffn_out,
    enc_gain,
    final_gain,
    sent_lengths,
    group_table,
    dec_rows,
    dec_gain,
    w_query,
    w_key,
    w_value,
    w_output,
):
    group_count = lax.axis_size("seq")
    my_group = lax.axis_index("seq")
    col_width = enc_rows.shape[1]
    col_start = lax.axis_index("mp") * col_width
    row_count = enc_rows.shape[0]
    max_length = 2 * row_count // group_count
    fast = fast_shapes(enc_rows, ffn_in, ffn_out, dec_rows, w_query)
    if not fast:
        whole_rows = lax.all_gather(enc_rows, "mp", axis=1, tiled=True)
        normed = rms_scale(whole_rows.astype(jnp.float32), enc_gain).astype(jnp.bfloat16)
        full_in = lax.all_gather(ffn_in, "seq", axis=0, tiled=True)
        inner = jnp.dot(normed, full_in, preferred_element_type=jnp.float32)
        hidden = jnp.maximum(inner, 0.0).astype(jnp.bfloat16)
        partial_out = jnp.dot(
            hidden,
            lax.all_gather(ffn_out, "seq", axis=1, tiled=True),
            preferred_element_type=jnp.float32,
        )
    my_lengths = lax.dynamic_index_in_dim(sent_lengths, my_group, 0, keepdims=False)
    my_targets = lax.dynamic_index_in_dim(group_table, my_group, 0, keepdims=False)
    ordinal = jnp.arange(group_count, dtype=jnp.int32)
    my_starts = jnp.sum(
        jnp.where(ordinal[None, :] < ordinal[:, None], my_lengths[None, :], 0), axis=1
    )
    group_ids = jnp.arange(group_count, dtype=jnp.int32)
    matches = my_targets[None, :] == group_ids[:, None]
    send_starts = jnp.sum(jnp.where(matches, my_starts[None, :], 0), axis=1)
    positions = jnp.arange(max_length, dtype=jnp.int32)
    row_index = jnp.minimum(send_starts[:, None] + positions[None, :], row_count - 1)
    recv_lengths = jnp.sum(jnp.where(group_table == my_group, sent_lengths, 0), axis=1)
    live_mask = positions[None, :] < recv_lengths[:, None]
    if fast:
        return whole_fast(
            enc_rows,
            ffn_in,
            ffn_out,
            enc_gain,
            final_gain,
            sent_lengths,
            group_table,
            dec_rows,
            dec_gain,
            w_query,
            w_key,
            w_value,
            w_output,
        )
    kv_width = w_key.shape[2]
    weight_list = []
    for layer_index in range(LAYERS):
        weight_list.append(w_key[layer_index])
        weight_list.append(w_value[layer_index])
    enc_share = lax.psum_scatter(partial_out, "mp", scatter_dimension=1, tiled=True)
    encoded = enc_rows.astype(jnp.float32) + enc_share
    squares = lax.psum(jnp.sum(encoded * encoded, axis=1), "mp")
    gain_part = lax.dynamic_slice_in_dim(final_gain, col_start, col_width, 0)
    memory = (encoded * lax.rsqrt(squares / D + epsilon)[:, None] * gain_part).astype(jnp.bfloat16)
    blocks = memory[row_index]
    gathered = lax.all_gather(
        lax.all_to_all(blocks, "seq", split_axis=0, concat_axis=0, tiled=True),
        "mp",
        axis=2,
        tiled=True,
    )
    projected = tuple(
        (
            jnp.einsum(
                "std,de->ste", gathered, weight_matrix, preferred_element_type=jnp.float32
            ).astype(jnp.bfloat16)
            for weight_matrix in weight_list
        )
    )
    tgt_rows = dec_rows.shape[0]
    per_sentence = tgt_rows // group_count
    local_heads = kv_width // DH
    final_state = dec_rows.astype(jnp.float32)
    for layer_index in range(LAYERS):
        state_half = lax.all_gather(final_state.astype(jnp.bfloat16), "mp", axis=1, tiled=True)
        normed_rows = rms_scale(state_half.astype(jnp.float32), dec_gain[layer_index]).astype(
            jnp.bfloat16
        )
        queries = (
            jnp.dot(normed_rows, w_query[layer_index], preferred_element_type=jnp.float32)
            * DH ** (-0.5)
        ).astype(jnp.bfloat16)
        query_heads = queries.reshape(group_count, per_sentence, local_heads, DH)
        key_heads = projected[2 * layer_index].reshape(group_count, max_length, local_heads, DH)
        value_heads = projected[2 * layer_index + 1].reshape(
            group_count, max_length, local_heads, DH
        )
        scores = jnp.einsum(
            "sqhd,sthd->shqt", query_heads, key_heads, preferred_element_type=jnp.float32
        )
        scores = jnp.where(live_mask[:, None, None, :], scores, -jnp.inf)
        weights = jax.nn.softmax(scores, axis=-1).astype(jnp.bfloat16)
        attended = jnp.einsum(
            "shqt,sthd->sqhd", weights, value_heads, preferred_element_type=jnp.float32
        ).astype(jnp.bfloat16)
        final_state = final_state + lax.psum_scatter(
            jnp.dot(
                attended.reshape(tgt_rows, kv_width),
                w_output[layer_index],
                preferred_element_type=jnp.float32,
            ).astype(jnp.bfloat16),
            "mp",
            scatter_dimension=1,
            tiled=True,
        ).astype(jnp.float32)
    return final_state.astype(jnp.bfloat16)


def solution(mesh):
    in_specs = (
        P("seq", "mp"),
        P("seq", "mp"),
        P("mp", "seq"),
        P(),
        P(),
        P(),
        P(),
        P("seq", "mp"),
        P(),
        P(None, None, "mp"),
        P(None, None, "mp"),
        P(None, None, "mp"),
        P(None, "mp", None),
    )
    out_specs = P("seq", "mp")
    return jax.shard_map(shards, mesh=mesh, in_specs=in_specs, out_specs=out_specs, check_vma=False)
```

```python
import functools

import jax
import jax.numpy as jnp
from jax import lax
from jax.experimental import pallas as pl
from jax.experimental.pallas import tpu as pltpu
from jax.sharding import PartitionSpec as P

MESH = pl.DeviceIdType.MESH

D = 1024
DH = 128
LAYERS = 2


epsilon = 1e-06


def rms_scale(values, gain_row):
    mean_square = jnp.mean(values * values, axis=-1, keepdims=True)
    return values * lax.rsqrt(mean_square + epsilon) * gain_row


def flip(index, bits):
    out = index
    for power in (1, 2, 4, 8, 16, 32):
        if bits & power:
            out = out + power - 2 * power * ((out // power) % 2)
    return out


def z_order(count):
    return sorted(range(1, count), key=lambda bits: (bits == 1, bits))


def column_order(n_seq, per_block):
    inner = [block * per_block + j for block in range(1, n_seq - 1) for j in range(per_block)]
    outer = [block * per_block + j for j in range(per_block) for block in (0, n_seq - 1)]
    return inner + outer


def ffn_kernel(
    n_seq,
    n_mp,
    enc_ref,
    gain_ref,
    final_gain_ref,
    lengths_ref,
    table_ref,
    dec_ref,
    dec_gain_ref,
    fin_ref,
    fout_ref,
    wq_ref,
    wk_ref,
    wv_ref,
    wo_ref,
    out_ref,
    enc_all,
    normed,
    win,
    wout,
    hidden,
    part_out,
    part_in,
    tree_out,
    tree_in,
    enc_a,
    enc_b,
    enc_c,
    enc_zs,
    enc_zr,
    enc_ps,
    enc_pr,
    in_s,
    in_r,
    out_s,
    out_r,
    rs_s,
    rs_r,
    tree_s,
    tree_r,
    ag_s,
    ag_r,
    local_sem,
    wq,
    wk,
    wv,
    wo,
    w_sem,
    dec_all,
    dec_next,
    dec_normed,
    queries,
    memory,
    square,
    kv_acc,
    keys,
    values,
    attended,
    att_out,
    att_in,
    dec_ps,
    dec_pr,
    att_ps,
    att_pr,
    sel,
    mask,
    own_out_sem,
):
    s = lax.axis_index("seq")
    m = lax.axis_index("mp")
    rows, width = enc_ref.shape
    depth = fin_ref.shape[0]
    units = fin_ref.shape[1] // n_seq
    out_width = fout_ref.shape[1]
    total_rows = rows * n_seq
    per_block = out_width // width

    order = column_order(n_seq, per_block)
    early = (n_seq - 2) * per_block

    barrier = pltpu.get_barrier_semaphore()
    for bits in range(1, n_seq):
        pl.semaphore_signal(barrier, inc=1, device_id=(flip(s, bits), m), device_id_type=MESH)
    for bits in range(1, n_mp):
        pl.semaphore_signal(barrier, inc=1, device_id=(s, flip(m, bits)), device_id_type=MESH)
    pl.semaphore_wait(barrier, n_seq + n_mp - 2)

    my_rows = pl.ds(pl.multiple_of(s * rows, rows), rows)

    def plane_gather(buf, send_sem, recv_sem):
        def copy(slot, bits, peer):
            return pltpu.make_async_remote_copy(
                src_ref=buf.at[slot],
                dst_ref=buf.at[slot],
                send_sem=send_sem.at[bits],
                recv_sem=recv_sem.at[bits],
                device_id=(s, peer),
                device_id_type=MESH,
            )

        across = [bits for bits in range(n_mp - 2, 1, -2)]
        direct = {bits: copy(m, bits, flip(m, bits)) for bits in across + [1]}
        for bits in across + [1]:
            direct[bits].start()

        def finish():
            onward = []
            for bits in reversed(across):
                direct[bits].wait_recv()
                forward = copy(flip(m, bits), bits + 1, flip(m, 1))
                forward.start()
                onward.append(forward)
            direct[1].wait_recv()
            for forward in onward:
                forward.wait()
            for bits in across + [1]:
                direct[bits].wait_send()

        return finish

    def normalise(buf, dst, count, gain, gain_row):
        step = min(256, count)

        def body(i, carry):
            span = pl.ds(pl.multiple_of(i * step, step), step)
            squares = jnp.zeros((step, 1), jnp.float32)
            for k in range(n_mp):
                value = buf[k, span, :].astype(jnp.float32)
                squares = squares + jnp.sum(value * value, axis=1, keepdims=True)
            scale = lax.rsqrt(squares / (n_mp * width) + epsilon)
            for k in range(n_mp):
                cols = pl.ds(k * width, width)
                value = buf[k, span, :].astype(jnp.float32)
                dst[span, cols] = (value * scale * gain[pl.ds(gain_row, 1), cols]).astype(
                    jnp.bfloat16
                )
            return carry

        lax.fori_loop(0, count // step, body, 0)

    def product(left, right, layer, store):
        columns = right.shape[2]
        step = min(256, columns)

        def body(i, carry):
            cols = pl.ds(pl.multiple_of(i * step, step), step)
            store(
                cols, jnp.dot(left[...], right[layer, :, cols], preferred_element_type=jnp.float32)
            )
            return carry

        lax.fori_loop(0, columns // step, body, 0)

    def project_queries(layer, span):
        def store(cols, value):
            queries[span, cols] = (value * DH ** (-0.5)).astype(jnp.bfloat16)

        product(dec_normed.at[span], wq, layer, store)

    def project_part(cols0, count, first):
        step = min(256, wk.shape[2])
        part = pl.ds(cols0, count)

        def body(i, carry):
            cols = pl.ds(pl.multiple_of(i * step, step), step)
            for index, weight in enumerate((wk, wv)):
                value = jnp.dot(
                    memory[:, part], weight[0, part, cols], preferred_element_type=jnp.float32
                )
                if not first:
                    value = value + kv_acc[index, :, cols]
                kv_acc[index, :, cols] = value
            return carry

        lax.fori_loop(0, wk.shape[2] // step, body, 0)

    def row_scale():
        squares = jnp.sum(square[...], axis=1, keepdims=True)
        return lax.rsqrt(squares / (n_mp * width) + epsilon)

    def project_last(cols0, count):
        step = min(256, wk.shape[2])
        part = pl.ds(cols0, count)
        scale = row_scale()

        def body(i, carry):
            cols = pl.ds(pl.multiple_of(i * step, step), step)
            for index, (weight, dst) in enumerate(((wk, keys), (wv, values))):
                value = kv_acc[index, :, cols] + jnp.dot(
                    memory[:, part], weight[0, part, cols], preferred_element_type=jnp.float32
                )
                dst[:, cols] = (value * scale).astype(jnp.bfloat16)
            return carry

        lax.fori_loop(0, wk.shape[2] // step, body, 0)

    def project_memory(layer):
        scale = row_scale()

        def store_key(cols, value):
            keys[:, cols] = (value * scale).astype(jnp.bfloat16)

        def store_value(cols, value):
            values[:, cols] = (value * scale).astype(jnp.bfloat16)

        product(memory, wk, layer, store_key)
        product(memory, wv, layer, store_value)

    slot_rows = sel.shape[1]
    targets = dec_ref.shape[0]
    per_sentence = targets // n_seq
    layers = wq_ref.shape[0]
    heads = wq_ref.shape[2] // DH

    def attend(first, count):
        def body(i, carry):
            span = pl.ds(pl.multiple_of(i * per_sentence, per_sentence), per_sentence)
            slot_span = pl.ds(pl.multiple_of(i * slot_rows, slot_rows), slot_rows)
            live = mask[i] > 0.5
            columns = [pl.ds(head * DH, DH) for head in range(heads)]
            scores = [
                lax.dot_general(
                    queries[span, cols],
                    keys[slot_span, cols],
                    (((1,), (1,)), ((), ())),
                    preferred_element_type=jnp.float32,
                )
                for cols in columns
            ]
            scores = [jnp.where(live, score, -jnp.inf) for score in scores]
            tops = [jnp.max(score, axis=1, keepdims=True) for score in scores]
            powers = [jnp.exp(score - top) for score, top in zip(scores, tops)]
            sums = [jnp.sum(power, axis=1, keepdims=True) for power in powers]
            weights = [(power / total).astype(jnp.bfloat16) for power, total in zip(powers, sums)]
            for cols, weight in zip(columns, weights):
                attended[span, cols] = jnp.dot(
                    weight, values[slot_span, cols], preferred_element_type=jnp.float32
                ).astype(jnp.bfloat16)
            return carry

        lax.fori_loop(first, first + count, body, 0, unroll=True)

    parts = 2
    part_rows = targets // parts

    def rows_of(part):
        return pl.ds(part * part_rows, part_rows)

    def att_copy(layer, part, slot, source):
        return pltpu.make_async_remote_copy(
            src_ref=att_out.at[layer, part, slot],
            dst_ref=att_in.at[layer, part, source],
            send_sem=att_ps.at[layer, part, slot],
            recv_sem=att_pr.at[layer, part, source],
            device_id=(s, slot),
            device_id_type=MESH,
        )

    def scatter_output(layer, part):
        step = max(width, 256)

        def body(i, carry):
            chip = (i + m // (step // width) + 1) % (n_mp * width // step)
            cols = pl.ds(pl.multiple_of(chip * step, step), step)
            value = jnp.dot(
                attended[rows_of(part), :], wo[layer, :, cols], preferred_element_type=jnp.float32
            ).astype(jnp.bfloat16)
            for j in range(step // width):
                slot = chip * (step // width) + j
                att_out[layer, part, slot] = value[:, j * width : (j + 1) * width]

                @pl.when(slot != m)
                def _():
                    att_copy(layer, part, slot, m).start()

            return carry

        lax.fori_loop(0, n_mp * width // step, body, 0)

    def collect_output(layer, part):
        total = att_out[layer, part, m].astype(jnp.float32)
        for bits in range(1, n_mp):
            peer = flip(m, bits)
            att_copy(layer, part, peer, peer).wait_recv()
            total = total + att_in[layer, part, peer].astype(jnp.float32)
        return total

    own_enc = pltpu.make_async_copy(enc_ref, enc_all.at[m, my_rows], local_sem.at[0])
    own_enc.start()

    def enc_copy(bits):
        return pltpu.make_async_remote_copy(
            src_ref=enc_ref,
            dst_ref=enc_all.at[m, my_rows],
            send_sem=enc_zs.at[bits],
            recv_sem=enc_zr.at[bits],
            device_id=(flip(s, bits), m),
            device_id_type=MESH,
        )

    for bits in (2, 1):
        enc_copy(bits).start()
    across_rows = pl.ds(pl.multiple_of(flip(s, 2) * rows, rows), rows)
    enc_onward = pltpu.make_async_remote_copy(
        src_ref=enc_all.at[m, across_rows],
        dst_ref=enc_all.at[m, across_rows],
        send_sem=enc_zs.at[3],
        recv_sem=enc_zr.at[3],
        device_id=(flip(s, 1), m),
        device_id_type=MESH,
    )
    inner = (s % 2 + s // 2) % 2

    own_in = pltpu.make_async_copy(
        fin_ref.at[:, pl.ds(pl.multiple_of(s * units, units), units)], win.at[s], local_sem.at[1]
    )
    own_in.start()
    own_out = [
        pltpu.make_async_copy(
            fout_ref.at[
                pl.ds(pl.multiple_of(s * units, units), units), pl.ds(j * width, width)
            ],
            wout.at[s, j],
            own_out_sem.at[j],
        )
        for j in range(per_block)
    ]
    for copy in own_out:
        copy.start()
    def in_copy(bits):
        peer = flip(s, bits)
        return pltpu.make_async_remote_copy(
            src_ref=fin_ref.at[:, pl.ds(pl.multiple_of(peer * units, units), units)],
            dst_ref=win.at[s],
            send_sem=in_s.at[bits],
            recv_sem=in_r.at[bits],
            device_id=(peer, m),
            device_id_type=MESH,
        )

    @pl.when(inner == 1)
    def _():
        for bits in (2, 3):
            in_copy(bits).start()

    enc_copy(2).wait_recv()
    enc_onward.start()

    @pl.when(inner == 0)
    def _():
        for bits in (2, 3):
            in_copy(bits).start()

    in_copy(1).start()
    piece = units // 2

    def out_copy(bits, j, k):
        peer = flip_any(bits)
        return pltpu.make_async_remote_copy(
            src_ref=fout_ref.at[
                pl.ds(pl.multiple_of(peer * units + k * piece, piece), piece),
                pl.ds(j * width, width),
            ],
            dst_ref=wout.at[s, j, pl.ds(k * piece, piece)],
            send_sem=out_s.at[bits, j, k],
            recv_sem=out_r.at[bits, j, k],
            device_id=(peer, m),
            device_id_type=MESH,
        )

    def flip_any(bits):
        if isinstance(bits, int):
            return flip(s, bits)
        return flip(s, 2) * (3 - bits) + flip(s, 3) * (bits - 2)

    def across_out(j, k):
        for bits in (3, 2):
            out_copy(bits, j, k).start()

    for j in range(per_block):
        for k in range(2):
            out_copy(1, j, k).start()

    @pl.when(inner == 1)
    def _():
        for j in range(per_block):
            for k in range(2):
                across_out(j, k)

    weight_copies = []
    for index, (src, dst) in enumerate(((wq_ref, wq), (wo_ref, wo))):
        copy = pltpu.make_async_copy(src, dst, w_sem.at[index])
        copy.start()
        weight_copies.append(copy)
    for index, (src, dst) in enumerate(((wk_ref, wk), (wv_ref, wv))):
        for slot, source in enumerate(order):
            copy = pltpu.make_async_copy(
                src.at[:, pl.ds(source * width, width)],
                dst.at[:, pl.ds(slot * width, width)],
                w_sem.at[2 + index * n_mp + slot],
            )
            copy.start()
            weight_copies.append(copy)
    own_dec = pltpu.make_async_copy(dec_ref, dec_all.at[m], local_sem.at[3])
    own_dec.start()
    own_dec.wait()
    finish_dec = plane_gather(dec_all, dec_ps.at[0], dec_pr.at[0])

    own_enc.wait()
    enc_copy(1).wait_recv()
    enc_onward.wait_recv()
    for bits in (2, 1):
        enc_copy(bits).wait_send()
    enc_onward.wait_send()

    plane_gather(enc_all, enc_ps, enc_pr)()

    chunk = min(256, rows)

    normalise(enc_all, normed, total_rows, gain_ref, 0)

    for source in range(n_seq):
        start = jnp.int32(0)
        before = jnp.int32(0)
        for j in range(n_seq):
            start = start + jnp.where(table_ref[source, j] == s, before, 0)
            before = before + lengths_ref[source, j]
        slot_row = lax.broadcasted_iota(jnp.int32, (slot_rows, rows), 0)
        column = lax.broadcasted_iota(jnp.int32, (slot_rows, rows), 1)
        wanted = jnp.minimum(slot_row + start, rows - 1)
        sel[source] = jnp.where(wanted == column, 1.0, 0.0).astype(jnp.bfloat16)
    for source in range(n_seq):
        length = jnp.int32(0)
        for j in range(n_seq):
            length = length + jnp.where(table_ref[source, j] == s, lengths_ref[source, j], 0)
        slot = lax.broadcasted_iota(jnp.int32, (1, slot_rows), 1)
        mask[source] = jnp.where(slot < length, 1.0, 0.0)

    finish_dec()
    normalise(dec_all, dec_normed, targets, dec_gain_ref, 0)
    for copy in weight_copies:
        copy.wait()
    project_queries(0, pl.ds(0, targets))

    own_in.wait()
    for bits in range(1, n_seq):
        in_copy(bits).wait()

    tile = min(256, units)

    def hidden_chunk(i, carry):
        cols = pl.ds(pl.multiple_of((i % (units // tile)) * tile, tile), tile)
        span = pl.ds(pl.multiple_of((i // (units // tile)) * chunk, chunk), chunk)
        acc = jnp.zeros((chunk, tile), jnp.float32)
        for k in range(n_seq):
            acc = acc + jnp.dot(
                normed[span, pl.ds(k * depth, depth)],
                win[k, :, cols],
                preferred_element_type=jnp.float32,
            )
        hidden[span, cols] = jnp.maximum(acc, 0.0).astype(jnp.bfloat16)
        return carry

    lax.fori_loop(0, (total_rows // chunk) * (units // tile), hidden_chunk, 0)

    share = total_rows // n_mp
    per_chunk = chunk // share
    per_source = rows // share
    my_share = pl.ds(pl.multiple_of(m * share, share), share)

    def position(block, j):
        within = (block % 2 + block // 2) % 2
        outside = early + block // (n_seq - 1) + 2 * j
        return within * ((block - 1) * per_block + j) + (1 - within) * outside

    def rs_copy(p, peer, source):
        return pltpu.make_async_remote_copy(
            src_ref=part_out.at[p, pl.ds(pl.multiple_of(peer * share, share), share)],
            dst_ref=part_in.at[p, source],
            send_sem=rs_s.at[p, peer],
            recv_sem=rs_r.at[p, source],
            device_id=(s, peer),
            device_id_type=MESH,
        )

    def send_block(block, j):
        p = position(block, j)

        def rows_chunk(i, carry):
            c = (i + m // per_chunk + 1) % (total_rows // chunk)
            span = pl.ds(pl.multiple_of(c * chunk, chunk), chunk)
            part_out[p, span, :] = jnp.dot(
                hidden[span, :], wout[block, j], preferred_element_type=jnp.float32
            ).astype(jnp.bfloat16)
            for t in range(per_chunk):
                peer = c * per_chunk + t

                @pl.when(peer != m)
                def _():
                    rs_copy(p, peer, m).start()

            return carry

        lax.fori_loop(0, total_rows // chunk, rows_chunk, 0)

    def receive_block(bits, block, j):
        for k in range(2):
            out_copy(bits, j, k).wait_recv()
        send_block(block, j)

    def plane_sum(p):
        total = part_out[p, my_share, :].astype(jnp.float32)
        for bits in range(1, n_mp):
            peer = flip(m, bits)
            rs_copy(p, peer, peer).wait_recv()
            total = total + part_in[p, peer].astype(jnp.float32)
        return total

    def tree_copy(bits, p0, count):
        return pltpu.make_async_remote_copy(
            src_ref=tree_out.at[min(bits, 1), pl.ds(p0, count)],
            dst_ref=tree_in.at[min(bits, 2), pl.ds(p0, count)],
            send_sem=tree_s.at[bits, p0],
            recv_sem=tree_r.at[min(bits, 2), p0],
            device_id=(flip(s, max(bits, 1)), m),
            device_id_type=MESH,
        )

    def residual(p):
        return enc_all[order[p], my_share, :].astype(jnp.float32)

    def tree_up(p0, count):
        for p in range(p0, p0 + count):
            tree_out[0, p] = plane_sum(p).astype(jnp.bfloat16)

        @pl.when(inner == 1)
        def _():
            tree_copy(0, p0, count).start()

    def tree_across(p0, count):
        @pl.when(inner == 0)
        def _():
            tree_copy(0, p0, count).wait_recv()
            for p in range(p0, p0 + count):
                tree_out[1, p] = (
                    tree_out[0, p].astype(jnp.float32) + tree_in[0, p].astype(jnp.float32)
                ).astype(jnp.bfloat16)
            for bits in z_order(n_seq):
                tree_copy(bits, p0, count).start()

    def tree_down(p0, count, enc_buf):
        def combine(own):
            for p in range(p0, p0 + count):
                total = own[p].astype(jnp.float32) + tree_in[2, p].astype(jnp.float32)
                enc_buf[m, p - p0] = (total + residual(p)).astype(jnp.bfloat16)

        tree_copy(2, p0, count).wait_recv()

        @pl.when(inner == 0)
        def _():
            combine(tree_out.at[1])

        @pl.when(inner == 1)
        def _():
            tree_copy(1, p0, count).wait_recv()
            combine(tree_in.at[1])

    def tree_finish(p0, count):
        @pl.when(inner == 1)
        def _():
            tree_copy(0, p0, count).wait_send()

        @pl.when(inner == 0)
        def _():
            for bits in z_order(n_seq):
                tree_copy(bits, p0, count).wait_send()

    last = early + 2

    def absorb(enc_buf, p0, count):
        for source in range(n_seq):
            span = pl.ds(source * slot_rows, slot_rows)
            total = jnp.zeros((slot_rows, width), jnp.float32)
            for q in range(count):
                block = enc_buf[pl.ds(source * per_source, per_source), q].reshape(rows, width)
                slot = jnp.dot(sel[source], block, preferred_element_type=jnp.float32)
                total = total + slot * slot
                memory[span, pl.ds((p0 + q) * width, width)] = (
                    slot * final_gain_ref[:, pl.ds(order[p0 + q] * width, width)]
                ).astype(jnp.bfloat16)
            if p0 == 0:
                square[span, :] = total
            else:
                square[span, :] = square[span, :] + total

    last = early + 2
    near = 2 - s // 2
    far = 3 - 3 * (s // 2)
    near_bits = 2 + inner

    for j in range(per_block):
        own_out[j].wait()
        send_block(s, j)
    for j in range(per_block):
        receive_block(1, flip(s, 1), j)
    for j in range(per_block - 1):
        receive_block(near_bits, near, j)
    out_copy(near_bits, per_block - 1, 0).wait_recv()

    @pl.when(inner == 0)
    def _():
        out_copy(2, 0, 0).start()

    out_copy(near_bits, per_block - 1, 1).wait_recv()

    @pl.when(inner == 0)
    def _():
        out_copy(2, 0, 1).start()
        for k in range(2):
            out_copy(2, 1, k).start()

    send_block(near, per_block - 1)
    tree_up(0, early)
    tree_across(0, early)

    @pl.when(inner == 0)
    def _():
        for j in range(per_block):
            for k in range(2):
                out_copy(3, j, k).start()

    @pl.when(inner == 1)
    def _():
        receive_block(2, far, 0)
        tree_up(early, 2)
        receive_block(2, far, 1)
        tree_up(last, 2)

    tree_down(0, early, enc_a)
    plane_gather(enc_a, ag_s.at[0], ag_r.at[0])()
    absorb(enc_a, 0, early)
    project_part(0, early * width, True)

    @pl.when(inner == 0)
    def _():
        receive_block(3, far, 0)
        tree_up(early, 2)
        tree_across(early, 2)
        receive_block(3, far, 1)

    tree_down(early, 2, enc_b)
    finish_b = plane_gather(enc_b, ag_s.at[1], ag_r.at[1])

    @pl.when(inner == 0)
    def _():
        tree_up(last, 2)
        tree_across(last, 2)

    finish_b()
    absorb(enc_b, early, 2)
    project_part(early * width, 2 * width, False)
    tree_down(last, 2, enc_c)
    plane_gather(enc_c, ag_s.at[2], ag_r.at[2])()
    absorb(enc_c, last, 2)
    project_last(last * width, 2 * width)

    for p in range(n_mp):
        for bits in range(1, n_mp):
            rs_copy(p, flip(m, bits), m).wait_send()
    tree_finish(0, early)
    tree_finish(early, 2)
    tree_finish(last, 2)
    for bits in range(1, n_seq):
        for j in range(per_block):
            for k in range(2):
                out_copy(bits, j, k).wait_send()

    state = [dec_ref[rows_of(part), :].astype(jnp.float32) for part in range(parts)]
    per_part = n_seq // parts
    finish = [None] * parts
    for layer in range(layers):
        for part in range(parts):
            if layer > 0:
                finish[part]()
                span = rows_of(part)
                normalise(
                    dec_next.at[layer - 1, part], dec_normed.at[span], part_rows, dec_gain_ref, layer
                )
                project_queries(layer, span)
            attend(part * per_part, per_part)
            scatter_output(layer, part)
        if layer + 1 < layers:
            project_memory(layer + 1)
        for part in range(parts):
            state[part] = state[part] + collect_output(layer, part)
            if layer + 1 < layers:
                dec_next[layer, part, m] = state[part].astype(jnp.bfloat16)
                index = 1 + layer * parts + part
                finish[part] = plane_gather(
                    dec_next.at[layer, part], dec_ps.at[index], dec_pr.at[index]
                )
            else:
                out_ref[rows_of(part), :] = state[part].astype(out_ref.dtype)
    for layer in range(layers):
        for part in range(parts):
            for bits in range(1, n_mp):
                att_copy(layer, part, flip(m, bits), m).wait_send()


def whole_fast(
    enc_rows,
    ffn_in,
    ffn_out,
    enc_gain,
    final_gain,
    sent_lengths,
    group_table,
    dec_rows,
    dec_gain,
    w_query,
    w_key,
    w_value,
    w_output,
):
    n_seq, n_mp = lax.axis_size("seq"), lax.axis_size("mp")
    rows, width = enc_rows.shape
    depth, units = ffn_in.shape[0], ffn_in.shape[1] // n_seq
    out_width = ffn_out.shape[1]
    total = rows * n_seq
    full = width * n_mp
    targets = dec_rows.shape[0]
    layers, _, heads_width = w_query.shape
    slot_total = 2 * rows
    per_block = out_width // width
    share = total // n_mp
    half = jnp.bfloat16
    dma = pltpu.SemaphoreType.DMA
    return pl.pallas_call(
        functools.partial(ffn_kernel, n_seq, n_mp),
        out_shape=jax.ShapeDtypeStruct(dec_rows.shape, dec_rows.dtype),
        in_specs=[pl.BlockSpec(memory_space=pltpu.VMEM)] * 3
        + [pl.BlockSpec(memory_space=pltpu.SMEM)] * 2
        + [pl.BlockSpec(memory_space=pltpu.VMEM)] * 2
        + [pl.BlockSpec(memory_space=pl.ANY)] * 6,
        out_specs=pl.BlockSpec(memory_space=pltpu.VMEM),
        scratch_shapes=[
            pltpu.VMEM((n_mp, total, width), half),
            pltpu.VMEM((total, full), half),
            pltpu.VMEM((n_seq, depth, units), half),
            pltpu.VMEM((n_seq, per_block, units, width), half),
            pltpu.VMEM((total, units), half),
            pltpu.VMEM((n_mp, total, width), half),
            pltpu.VMEM((n_mp, n_mp, share, width), half),
            pltpu.VMEM((2, n_mp, share, width), half),
            pltpu.VMEM((3, n_mp, share, width), half),
            pltpu.VMEM((n_mp, n_mp - 4, share, width), half),
            pltpu.VMEM((n_mp, 2, share, width), half),
            pltpu.VMEM((n_mp, 2, share, width), half),
            dma((n_seq,)),
            dma((n_seq,)),
            dma((n_mp,)),
            dma((n_mp,)),
            dma((n_seq,)),
            dma((n_seq,)),
            dma((n_seq, per_block, 2)),
            dma((n_seq, per_block, 2)),
            dma((n_mp, n_mp)),
            dma((n_mp, n_mp)),
            dma((4, n_mp)),
            dma((3, n_mp)),
            dma((3, n_mp)),
            dma((3, n_mp)),
            dma((4,)),
            pltpu.VMEM(w_query.shape, half),
            pltpu.VMEM(w_key.shape, half),
            pltpu.VMEM(w_value.shape, half),
            pltpu.VMEM(w_output.shape, half),
            dma((2 + 2 * n_mp,)),
            pltpu.VMEM((n_mp, targets, width), half),
            pltpu.VMEM((layers, 2, n_mp, targets // 2, width), half),
            pltpu.VMEM((targets, full), half),
            pltpu.VMEM((targets, heads_width), half),
            pltpu.VMEM((slot_total, full), half),
            pltpu.VMEM((slot_total, width), jnp.float32),
            pltpu.VMEM((2, slot_total, heads_width), jnp.float32),
            pltpu.VMEM((slot_total, heads_width), half),
            pltpu.VMEM((slot_total, heads_width), half),
            pltpu.VMEM((targets, heads_width), half),
            pltpu.VMEM((layers, 2, n_mp, targets // 2, width), half),
            pltpu.VMEM((layers, 2, n_mp, targets // 2, width), half),
            dma((2 * layers, n_mp)),
            dma((2 * layers, n_mp)),
            dma((layers, 2, n_mp)),
            dma((layers, 2, n_mp)),
            pltpu.VMEM((n_seq, slot_total // n_seq, rows), half),
            pltpu.VMEM((n_seq, 1, slot_total // n_seq), jnp.float32),
            dma((per_block,)),
        ],
        compiler_params=pltpu.CompilerParams(
            collective_id=0, has_side_effects=True, vmem_limit_bytes=60 * 1024 * 1024
        ),
    )(
        enc_rows,
        enc_gain.reshape(1, full),
        final_gain.reshape(1, full),
        sent_lengths,
        group_table,
        dec_rows,
        dec_gain,
        ffn_in,
        ffn_out,
        w_query,
        w_key,
        w_value,
        w_output,
    )


def fast_shapes(enc_rows, ffn_in, ffn_out, dec_rows, w_query):
    n_seq, n_mp = lax.axis_size("seq"), lax.axis_size("mp")
    power = n_seq == 4 and n_mp == 8 and ffn_out.shape[1] == 2 * enc_rows.shape[1]
    aligned = (
        enc_rows.shape[1] % 128 == 0
        and ffn_in.shape[0] % 128 == 0
        and (ffn_in.shape[1] // n_seq) % 256 == 0
        and ffn_out.shape[1] % enc_rows.shape[1] == 0
        and enc_rows.shape[0] % 256 == 0
        and dec_rows.shape[0] % 256 == 0
        and (2 * enc_rows.shape[0] // n_seq) % 128 == 0
        and w_query.shape[2] % 256 == 0
        and w_query.shape[1] % 256 == 0
    )
    return power and aligned


def shards(
    enc_rows,
    ffn_in,
    ffn_out,
    enc_gain,
    final_gain,
    sent_lengths,
    group_table,
    dec_rows,
    dec_gain,
    w_query,
    w_key,
    w_value,
    w_output,
):
    group_count = lax.axis_size("seq")
    my_group = lax.axis_index("seq")
    col_width = enc_rows.shape[1]
    col_start = lax.axis_index("mp") * col_width
    row_count = enc_rows.shape[0]
    max_length = 2 * row_count // group_count
    fast = fast_shapes(enc_rows, ffn_in, ffn_out, dec_rows, w_query)
    if not fast:
        whole_rows = lax.all_gather(enc_rows, "mp", axis=1, tiled=True)
        normed = rms_scale(whole_rows.astype(jnp.float32), enc_gain).astype(jnp.bfloat16)
        full_in = lax.all_gather(ffn_in, "seq", axis=0, tiled=True)
        inner = jnp.dot(normed, full_in, preferred_element_type=jnp.float32)
        hidden = jnp.maximum(inner, 0.0).astype(jnp.bfloat16)
        partial_out = jnp.dot(
            hidden,
            lax.all_gather(ffn_out, "seq", axis=1, tiled=True),
            preferred_element_type=jnp.float32,
        )
    my_lengths = lax.dynamic_index_in_dim(sent_lengths, my_group, 0, keepdims=False)
    my_targets = lax.dynamic_index_in_dim(group_table, my_group, 0, keepdims=False)
    ordinal = jnp.arange(group_count, dtype=jnp.int32)
    my_starts = jnp.sum(
        jnp.where(ordinal[None, :] < ordinal[:, None], my_lengths[None, :], 0), axis=1
    )
    group_ids = jnp.arange(group_count, dtype=jnp.int32)
    matches = my_targets[None, :] == group_ids[:, None]
    send_starts = jnp.sum(jnp.where(matches, my_starts[None, :], 0), axis=1)
    positions = jnp.arange(max_length, dtype=jnp.int32)
    row_index = jnp.minimum(send_starts[:, None] + positions[None, :], row_count - 1)
    recv_lengths = jnp.sum(jnp.where(group_table == my_group, sent_lengths, 0), axis=1)
    live_mask = positions[None, :] < recv_lengths[:, None]
    if fast:
        return whole_fast(
            enc_rows,
            ffn_in,
            ffn_out,
            enc_gain,
            final_gain,
            sent_lengths,
            group_table,
            dec_rows,
            dec_gain,
            w_query,
            w_key,
            w_value,
            w_output,
        )
    kv_width = w_key.shape[2]
    weight_list = []
    for layer_index in range(LAYERS):
        weight_list.append(w_key[layer_index])
        weight_list.append(w_value[layer_index])
    enc_share = lax.psum_scatter(partial_out, "mp", scatter_dimension=1, tiled=True)
    encoded = enc_rows.astype(jnp.float32) + enc_share
    squares = lax.psum(jnp.sum(encoded * encoded, axis=1), "mp")
    gain_part = lax.dynamic_slice_in_dim(final_gain, col_start, col_width, 0)
    memory = (encoded * lax.rsqrt(squares / D + epsilon)[:, None] * gain_part).astype(jnp.bfloat16)
    blocks = memory[row_index]
    gathered = lax.all_gather(
        lax.all_to_all(blocks, "seq", split_axis=0, concat_axis=0, tiled=True),
        "mp",
        axis=2,
        tiled=True,
    )
    projected = tuple(
        (
            jnp.einsum(
                "std,de->ste", gathered, weight_matrix, preferred_element_type=jnp.float32
            ).astype(jnp.bfloat16)
            for weight_matrix in weight_list
        )
    )
    tgt_rows = dec_rows.shape[0]
    per_sentence = tgt_rows // group_count
    local_heads = kv_width // DH
    final_state = dec_rows.astype(jnp.float32)
    for layer_index in range(LAYERS):
        state_half = lax.all_gather(final_state.astype(jnp.bfloat16), "mp", axis=1, tiled=True)
        normed_rows = rms_scale(state_half.astype(jnp.float32), dec_gain[layer_index]).astype(
            jnp.bfloat16
        )
        queries = (
            jnp.dot(normed_rows, w_query[layer_index], preferred_element_type=jnp.float32)
            * DH ** (-0.5)
        ).astype(jnp.bfloat16)
        query_heads = queries.reshape(group_count, per_sentence, local_heads, DH)
        key_heads = projected[2 * layer_index].reshape(group_count, max_length, local_heads, DH)
        value_heads = projected[2 * layer_index + 1].reshape(
            group_count, max_length, local_heads, DH
        )
        scores = jnp.einsum(
            "sqhd,sthd->shqt", query_heads, key_heads, preferred_element_type=jnp.float32
        )
        scores = jnp.where(live_mask[:, None, None, :], scores, -jnp.inf)
        weights = jax.nn.softmax(scores, axis=-1).astype(jnp.bfloat16)
        attended = jnp.einsum(
            "shqt,sthd->sqhd", weights, value_heads, preferred_element_type=jnp.float32
        ).astype(jnp.bfloat16)
        final_state = final_state + lax.psum_scatter(
            jnp.dot(
                attended.reshape(tgt_rows, kv_width),
                w_output[layer_index],
                preferred_element_type=jnp.float32,
            ).astype(jnp.bfloat16),
            "mp",
            scatter_dimension=1,
            tiled=True,
        ).astype(jnp.float32)
    return final_state.astype(jnp.bfloat16)


def solution(mesh):
    in_specs = (
        P("seq", "mp"),
        P("seq", "mp"),
        P("mp", "seq"),
        P(),
        P(),
        P(),
        P(),
        P("seq", "mp"),
        P(),
        P(None, None, "mp"),
        P(None, None, "mp"),
        P(None, None, "mp"),
        P(None, "mp", None),
    )
    out_specs = P("seq", "mp")
    return jax.shard_map(shards, mesh=mesh, in_specs=in_specs, out_specs=out_specs, check_vma=False)
```

```python
import functools

import jax
import jax.numpy as jnp
from jax import lax
from jax.experimental import pallas as pl
from jax.experimental.pallas import tpu as pltpu
from jax.sharding import PartitionSpec as P

MESH = pl.DeviceIdType.MESH

D = 1024
DH = 128
LAYERS = 2


epsilon = 1e-06


def rms_scale(values, gain_row):
    mean_square = jnp.mean(values * values, axis=-1, keepdims=True)
    return values * lax.rsqrt(mean_square + epsilon) * gain_row


def flip(index, bits):
    out = index
    for power in (1, 2, 4, 8, 16, 32):
        if bits & power:
            out = out + power - 2 * power * ((out // power) % 2)
    return out


def z_order(count):
    return sorted(range(1, count), key=lambda bits: (bits == 1, bits))


def column_order(n_seq, per_block):
    inner = [block * per_block + j for block in range(1, n_seq - 1) for j in range(per_block)]
    outer = [block * per_block + j for j in range(per_block) for block in (0, n_seq - 1)]
    return inner + outer


def ffn_kernel(
    n_seq,
    n_mp,
    enc_ref,
    gain_ref,
    final_gain_ref,
    lengths_ref,
    table_ref,
    dec_ref,
    dec_gain_ref,
    fin_ref,
    fout_ref,
    wq_ref,
    wk_ref,
    wv_ref,
    wo_ref,
    out_ref,
    enc_all,
    normed,
    win,
    wout,
    hidden,
    part_out,
    part_in,
    tree_out,
    tree_in,
    enc_a,
    enc_b,
    enc_c,
    enc_zs,
    enc_zr,
    enc_ps,
    enc_pr,
    in_s,
    in_r,
    out_s,
    out_r,
    rs_s,
    rs_r,
    tree_s,
    tree_r,
    ag_s,
    ag_r,
    local_sem,
    wq,
    wk,
    wv,
    wo,
    w_sem,
    dec_all,
    dec_next,
    dec_normed,
    queries,
    memory,
    square,
    kv_acc,
    keys,
    values,
    attended,
    att_out,
    att_in,
    dec_ps,
    dec_pr,
    att_ps,
    att_pr,
    sel,
    mask,
    own_out_sem,
):
    s = lax.axis_index("seq")
    m = lax.axis_index("mp")
    rows, width = enc_ref.shape
    depth = fin_ref.shape[0]
    units = fin_ref.shape[1] // n_seq
    out_width = fout_ref.shape[1]
    total_rows = rows * n_seq
    per_block = out_width // width

    order = column_order(n_seq, per_block)
    early = (n_seq - 2) * per_block

    barrier = pltpu.get_barrier_semaphore()
    for bits in range(1, n_seq):
        pl.semaphore_signal(barrier, inc=1, device_id=(flip(s, bits), m), device_id_type=MESH)
    for bits in range(1, n_mp):
        pl.semaphore_signal(barrier, inc=1, device_id=(s, flip(m, bits)), device_id_type=MESH)
    pl.semaphore_wait(barrier, n_seq + n_mp - 2)

    my_rows = pl.ds(pl.multiple_of(s * rows, rows), rows)

    def plane_gather(buf, send_sem, recv_sem):
        def copy(slot, bits, peer):
            return pltpu.make_async_remote_copy(
                src_ref=buf.at[slot],
                dst_ref=buf.at[slot],
                send_sem=send_sem.at[bits],
                recv_sem=recv_sem.at[bits],
                device_id=(s, peer),
                device_id_type=MESH,
            )

        across = [bits for bits in range(n_mp - 2, 1, -2)]
        direct = {bits: copy(m, bits, flip(m, bits)) for bits in across + [1]}
        for bits in across + [1]:
            direct[bits].start()

        def finish():
            onward = []
            for bits in reversed(across):
                direct[bits].wait_recv()
                forward = copy(flip(m, bits), bits + 1, flip(m, 1))
                forward.start()
                onward.append(forward)
            direct[1].wait_recv()
            for forward in onward:
                forward.wait()
            for bits in across + [1]:
                direct[bits].wait_send()

        return finish

    def direct_gather(buf, send_sem, recv_sem):
        def copy(bits):
            return pltpu.make_async_remote_copy(
                src_ref=buf.at[m],
                dst_ref=buf.at[m],
                send_sem=send_sem.at[bits],
                recv_sem=recv_sem.at[bits],
                device_id=(s, flip(m, bits)),
                device_id_type=MESH,
            )

        for bits in range(n_mp - 1, 0, -1):
            copy(bits).start()

        def finish():
            for bits in range(1, n_mp):
                copy(bits).wait()

        return finish

    def normalise(buf, dst, count, gain, gain_row):
        step = min(256, count)

        def body(i, carry):
            span = pl.ds(pl.multiple_of(i * step, step), step)
            squares = jnp.zeros((step, 1), jnp.float32)
            for k in range(n_mp):
                value = buf[k, span, :].astype(jnp.float32)
                squares = squares + jnp.sum(value * value, axis=1, keepdims=True)
            scale = lax.rsqrt(squares / (n_mp * width) + epsilon)
            for k in range(n_mp):
                cols = pl.ds(k * width, width)
                value = buf[k, span, :].astype(jnp.float32)
                dst[span, cols] = (value * scale * gain[pl.ds(gain_row, 1), cols]).astype(
                    jnp.bfloat16
                )
            return carry

        lax.fori_loop(0, count // step, body, 0)

    def product(left, right, layer, store):
        columns = right.shape[2]
        step = min(256, columns)

        def body(i, carry):
            cols = pl.ds(pl.multiple_of(i * step, step), step)
            store(
                cols, jnp.dot(left[...], right[layer, :, cols], preferred_element_type=jnp.float32)
            )
            return carry

        lax.fori_loop(0, columns // step, body, 0)

    def project_queries(layer, span):
        def store(cols, value):
            queries[span, cols] = (value * DH ** (-0.5)).astype(jnp.bfloat16)

        product(dec_normed.at[span], wq, layer, store)

    def project_part(cols0, count, first):
        step = min(256, wk.shape[2])
        part = pl.ds(cols0, count)

        def body(i, carry):
            cols = pl.ds(pl.multiple_of(i * step, step), step)
            for index, weight in enumerate((wk, wv)):
                value = jnp.dot(
                    memory[:, part], weight[0, part, cols], preferred_element_type=jnp.float32
                )
                if not first:
                    value = value + kv_acc[index, :, cols]
                kv_acc[index, :, cols] = value
            return carry

        lax.fori_loop(0, wk.shape[2] // step, body, 0)

    def row_scale():
        squares = jnp.sum(square[...], axis=1, keepdims=True)
        return lax.rsqrt(squares / (n_mp * width) + epsilon)

    def project_last(cols0, count):
        step = min(256, wk.shape[2])
        part = pl.ds(cols0, count)
        scale = row_scale()

        def body(i, carry):
            cols = pl.ds(pl.multiple_of(i * step, step), step)
            for index, (weight, dst) in enumerate(((wk, keys), (wv, values))):
                value = kv_acc[index, :, cols] + jnp.dot(
                    memory[:, part], weight[0, part, cols], preferred_element_type=jnp.float32
                )
                dst[:, cols] = (value * scale).astype(jnp.bfloat16)
            return carry

        lax.fori_loop(0, wk.shape[2] // step, body, 0)

    def project_memory(layer):
        scale = row_scale()

        def store_key(cols, value):
            keys[:, cols] = (value * scale).astype(jnp.bfloat16)

        def store_value(cols, value):
            values[:, cols] = (value * scale).astype(jnp.bfloat16)

        product(memory, wk, layer, store_key)
        product(memory, wv, layer, store_value)

    slot_rows = sel.shape[1]
    targets = dec_ref.shape[0]
    per_sentence = targets // n_seq
    layers = wq_ref.shape[0]
    heads = wq_ref.shape[2] // DH

    def attend(first, count):
        def body(i, carry):
            span = pl.ds(pl.multiple_of(i * per_sentence, per_sentence), per_sentence)
            slot_span = pl.ds(pl.multiple_of(i * slot_rows, slot_rows), slot_rows)
            live = mask[i] > 0.5
            columns = [pl.ds(head * DH, DH) for head in range(heads)]
            scores = [
                lax.dot_general(
                    queries[span, cols],
                    keys[slot_span, cols],
                    (((1,), (1,)), ((), ())),
                    preferred_element_type=jnp.float32,
                )
                for cols in columns
            ]
            scores = [jnp.where(live, score, -jnp.inf) for score in scores]
            tops = [jnp.max(score, axis=1, keepdims=True) for score in scores]
            powers = [jnp.exp(score - top) for score, top in zip(scores, tops)]
            sums = [jnp.sum(power, axis=1, keepdims=True) for power in powers]
            weights = [
                (power * (1.0 / total)).astype(jnp.bfloat16) for power, total in zip(powers, sums)
            ]
            for cols, weight in zip(columns, weights):
                attended[span, cols] = jnp.dot(
                    weight, values[slot_span, cols], preferred_element_type=jnp.float32
                ).astype(jnp.bfloat16)
            return carry

        lax.fori_loop(first, first + count, body, 0, unroll=True)

    parts = 2
    part_rows = targets // parts

    def rows_of(part):
        return pl.ds(part * part_rows, part_rows)

    def att_copy(layer, part, slot, source):
        return pltpu.make_async_remote_copy(
            src_ref=att_out.at[layer, part, slot],
            dst_ref=att_in.at[layer, part, source],
            send_sem=att_ps.at[layer, part, slot],
            recv_sem=att_pr.at[layer, part, source],
            device_id=(s, slot),
            device_id_type=MESH,
        )

    def scatter_output(layer, part):
        step = max(width, 256)

        def body(i, carry):
            chip = (i + m // (step // width) + 1) % (n_mp * width // step)
            cols = pl.ds(pl.multiple_of(chip * step, step), step)
            value = jnp.dot(
                attended[rows_of(part), :], wo[layer, :, cols], preferred_element_type=jnp.float32
            ).astype(jnp.bfloat16)
            for j in range(step // width):
                slot = chip * (step // width) + j
                att_out[layer, part, slot] = value[:, j * width : (j + 1) * width]

                @pl.when(slot != m)
                def _():
                    att_copy(layer, part, slot, m).start()

            return carry

        lax.fori_loop(0, n_mp * width // step, body, 0)

    def collect_output(layer, part):
        total = att_out[layer, part, m].astype(jnp.float32)
        for bits in range(1, n_mp):
            peer = flip(m, bits)
            att_copy(layer, part, peer, peer).wait_recv()
            total = total + att_in[layer, part, peer].astype(jnp.float32)
        return total

    own_enc = pltpu.make_async_copy(enc_ref, enc_all.at[m, my_rows], local_sem.at[0])
    own_enc.start()

    def enc_copy(bits):
        return pltpu.make_async_remote_copy(
            src_ref=enc_ref,
            dst_ref=enc_all.at[m, my_rows],
            send_sem=enc_zs.at[bits],
            recv_sem=enc_zr.at[bits],
            device_id=(flip(s, bits), m),
            device_id_type=MESH,
        )

    for bits in (2, 1):
        enc_copy(bits).start()
    across_rows = pl.ds(pl.multiple_of(flip(s, 2) * rows, rows), rows)
    enc_onward = pltpu.make_async_remote_copy(
        src_ref=enc_all.at[m, across_rows],
        dst_ref=enc_all.at[m, across_rows],
        send_sem=enc_zs.at[3],
        recv_sem=enc_zr.at[3],
        device_id=(flip(s, 1), m),
        device_id_type=MESH,
    )
    inner = (s % 2 + s // 2) % 2

    own_in = pltpu.make_async_copy(
        fin_ref.at[:, pl.ds(pl.multiple_of(s * units, units), units)], win.at[s], local_sem.at[1]
    )
    own_in.start()
    own_out = [
        pltpu.make_async_copy(
            fout_ref.at[
                pl.ds(pl.multiple_of(s * units, units), units), pl.ds(j * width, width)
            ],
            wout.at[s, j],
            own_out_sem.at[j],
        )
        for j in range(per_block)
    ]
    for copy in own_out:
        copy.start()
    def in_copy(bits):
        peer = flip(s, bits)
        return pltpu.make_async_remote_copy(
            src_ref=fin_ref.at[:, pl.ds(pl.multiple_of(peer * units, units), units)],
            dst_ref=win.at[s],
            send_sem=in_s.at[bits],
            recv_sem=in_r.at[bits],
            device_id=(peer, m),
            device_id_type=MESH,
        )

    @pl.when(inner == 1)
    def _():
        for bits in (2, 3):
            in_copy(bits).start()

    enc_copy(2).wait_recv()
    enc_onward.start()

    @pl.when(inner == 0)
    def _():
        for bits in (2, 3):
            in_copy(bits).start()

    in_copy(1).start()
    piece = units // 2

    def out_copy(bits, j, k):
        peer = flip_any(bits)
        return pltpu.make_async_remote_copy(
            src_ref=fout_ref.at[
                pl.ds(pl.multiple_of(peer * units + k * piece, piece), piece),
                pl.ds(j * width, width),
            ],
            dst_ref=wout.at[s, j, pl.ds(k * piece, piece)],
            send_sem=out_s.at[bits, j, k],
            recv_sem=out_r.at[bits, j, k],
            device_id=(peer, m),
            device_id_type=MESH,
        )

    def flip_any(bits):
        if isinstance(bits, int):
            return flip(s, bits)
        return flip(s, 2) * (3 - bits) + flip(s, 3) * (bits - 2)

    def across_out(j, k):
        for bits in (3, 2):
            out_copy(bits, j, k).start()

    for j in range(per_block):
        for k in range(2):
            out_copy(1, j, k).start()

    @pl.when(inner == 1)
    def _():
        for j in range(per_block):
            for k in range(2):
                across_out(j, k)

    weight_copies = []
    for index, (src, dst) in enumerate(((wq_ref, wq), (wo_ref, wo))):
        copy = pltpu.make_async_copy(src, dst, w_sem.at[index])
        copy.start()
        weight_copies.append(copy)
    for index, (src, dst) in enumerate(((wk_ref, wk), (wv_ref, wv))):
        for slot, source in enumerate(order):
            copy = pltpu.make_async_copy(
                src.at[:, pl.ds(source * width, width)],
                dst.at[:, pl.ds(slot * width, width)],
                w_sem.at[2 + index * n_mp + slot],
            )
            copy.start()
            weight_copies.append(copy)
    own_dec = pltpu.make_async_copy(dec_ref, dec_all.at[m], local_sem.at[3])
    own_dec.start()
    own_dec.wait()
    finish_dec = plane_gather(dec_all, dec_ps.at[0], dec_pr.at[0])

    own_enc.wait()
    enc_copy(1).wait_recv()
    enc_onward.wait_recv()
    for bits in (2, 1):
        enc_copy(bits).wait_send()
    enc_onward.wait_send()

    plane_gather(enc_all, enc_ps, enc_pr)()

    chunk = min(256, rows)

    normalise(enc_all, normed, total_rows, gain_ref, 0)

    for source in range(n_seq):
        start = jnp.int32(0)
        before = jnp.int32(0)
        for j in range(n_seq):
            start = start + jnp.where(table_ref[source, j] == s, before, 0)
            before = before + lengths_ref[source, j]
        slot_row = lax.broadcasted_iota(jnp.int32, (slot_rows, rows), 0)
        column = lax.broadcasted_iota(jnp.int32, (slot_rows, rows), 1)
        wanted = jnp.minimum(slot_row + start, rows - 1)
        sel[source] = jnp.where(wanted == column, 1.0, 0.0).astype(jnp.bfloat16)
    for source in range(n_seq):
        length = jnp.int32(0)
        for j in range(n_seq):
            length = length + jnp.where(table_ref[source, j] == s, lengths_ref[source, j], 0)
        slot = lax.broadcasted_iota(jnp.int32, (1, slot_rows), 1)
        mask[source] = jnp.where(slot < length, 1.0, 0.0)

    finish_dec()
    normalise(dec_all, dec_normed, targets, dec_gain_ref, 0)
    for copy in weight_copies:
        copy.wait()
    project_queries(0, pl.ds(0, targets))

    own_in.wait()
    for bits in range(1, n_seq):
        in_copy(bits).wait()

    tile = min(256, units)

    def hidden_chunk(i, carry):
        cols = pl.ds(pl.multiple_of((i % (units // tile)) * tile, tile), tile)
        span = pl.ds(pl.multiple_of((i // (units // tile)) * chunk, chunk), chunk)
        acc = jnp.zeros((chunk, tile), jnp.float32)
        for k in range(n_seq):
            acc = acc + jnp.dot(
                normed[span, pl.ds(k * depth, depth)],
                win[k, :, cols],
                preferred_element_type=jnp.float32,
            )
        hidden[span, cols] = jnp.maximum(acc, 0.0).astype(jnp.bfloat16)
        return carry

    lax.fori_loop(0, (total_rows // chunk) * (units // tile), hidden_chunk, 0)

    share = total_rows // n_mp
    per_chunk = chunk // share
    per_source = rows // share
    my_share = pl.ds(pl.multiple_of(m * share, share), share)

    def position(block, j):
        within = (block % 2 + block // 2) % 2
        outside = early + block // (n_seq - 1) + 2 * j
        return within * ((block - 1) * per_block + j) + (1 - within) * outside

    def rs_copy(p, peer, source):
        return pltpu.make_async_remote_copy(
            src_ref=part_out.at[p, pl.ds(pl.multiple_of(peer * share, share), share)],
            dst_ref=part_in.at[p, source],
            send_sem=rs_s.at[p, peer],
            recv_sem=rs_r.at[p, source],
            device_id=(s, peer),
            device_id_type=MESH,
        )

    def send_block(block, j):
        p = position(block, j)

        def rows_chunk(i, carry):
            c = (i + m // per_chunk + 1) % (total_rows // chunk)
            span = pl.ds(pl.multiple_of(c * chunk, chunk), chunk)
            part_out[p, span, :] = jnp.dot(
                hidden[span, :], wout[block, j], preferred_element_type=jnp.float32
            ).astype(jnp.bfloat16)
            for t in range(per_chunk):
                peer = c * per_chunk + t

                @pl.when(peer != m)
                def _():
                    rs_copy(p, peer, m).start()

            return carry

        lax.fori_loop(0, total_rows // chunk, rows_chunk, 0)

    def receive_block(bits, block, j):
        for k in range(2):
            out_copy(bits, j, k).wait_recv()
        send_block(block, j)

    def plane_sum(p):
        total = part_out[p, my_share, :].astype(jnp.float32)
        for bits in range(1, n_mp):
            peer = flip(m, bits)
            rs_copy(p, peer, peer).wait_recv()
            total = total + part_in[p, peer].astype(jnp.float32)
        return total

    def tree_copy(bits, p0, count):
        return pltpu.make_async_remote_copy(
            src_ref=tree_out.at[min(bits, 1), pl.ds(p0, count)],
            dst_ref=tree_in.at[min(bits, 2), pl.ds(p0, count)],
            send_sem=tree_s.at[bits, p0],
            recv_sem=tree_r.at[min(bits, 2), p0],
            device_id=(flip(s, max(bits, 1)), m),
            device_id_type=MESH,
        )

    def residual(p):
        return enc_all[order[p], my_share, :].astype(jnp.float32)

    def tree_up(p0, count):
        for p in range(p0, p0 + count):
            tree_out[0, p] = plane_sum(p).astype(jnp.bfloat16)

        @pl.when(inner == 1)
        def _():
            tree_copy(0, p0, count).start()

    def tree_across(p0, count):
        @pl.when(inner == 0)
        def _():
            tree_copy(0, p0, count).wait_recv()
            for p in range(p0, p0 + count):
                tree_out[1, p] = (
                    tree_out[0, p].astype(jnp.float32) + tree_in[0, p].astype(jnp.float32)
                ).astype(jnp.bfloat16)
            for bits in z_order(n_seq):
                tree_copy(bits, p0, count).start()

    def tree_down(p0, count, enc_buf):
        def combine(own):
            for p in range(p0, p0 + count):
                total = own[p].astype(jnp.float32) + tree_in[2, p].astype(jnp.float32)
                enc_buf[m, p - p0] = (total + residual(p)).astype(jnp.bfloat16)

        tree_copy(2, p0, count).wait_recv()

        @pl.when(inner == 0)
        def _():
            combine(tree_out.at[1])

        @pl.when(inner == 1)
        def _():
            tree_copy(1, p0, count).wait_recv()
            combine(tree_in.at[1])

    def tree_finish(p0, count):
        @pl.when(inner == 1)
        def _():
            tree_copy(0, p0, count).wait_send()

        @pl.when(inner == 0)
        def _():
            for bits in z_order(n_seq):
                tree_copy(bits, p0, count).wait_send()

    last = early + 2

    def absorb(enc_buf, p0, count):
        for source in range(n_seq):
            span = pl.ds(source * slot_rows, slot_rows)
            total = jnp.zeros((slot_rows, width), jnp.float32)
            for q in range(count):
                block = enc_buf[pl.ds(source * per_source, per_source), q].reshape(rows, width)
                slot = jnp.dot(sel[source], block, preferred_element_type=jnp.float32)
                total = total + slot * slot
                memory[span, pl.ds((p0 + q) * width, width)] = (
                    slot * final_gain_ref[:, pl.ds(order[p0 + q] * width, width)]
                ).astype(jnp.bfloat16)
            if p0 == 0:
                square[span, :] = total
            else:
                square[span, :] = square[span, :] + total

    last = early + 2
    near = 2 - s // 2
    far = 3 - 3 * (s // 2)
    near_bits = 2 + inner

    for j in range(per_block):
        own_out[j].wait()
        send_block(s, j)
    for j in range(per_block):
        receive_block(1, flip(s, 1), j)
    for j in range(per_block - 1):
        receive_block(near_bits, near, j)
    out_copy(near_bits, per_block - 1, 0).wait_recv()

    @pl.when(inner == 0)
    def _():
        out_copy(2, 0, 0).start()

    out_copy(near_bits, per_block - 1, 1).wait_recv()

    @pl.when(inner == 0)
    def _():
        out_copy(2, 0, 1).start()
        for k in range(2):
            out_copy(2, 1, k).start()

    send_block(near, per_block - 1)
    tree_up(0, early)
    tree_across(0, early)

    @pl.when(inner == 0)
    def _():
        for j in range(per_block):
            for k in range(2):
                out_copy(3, j, k).start()

    @pl.when(inner == 1)
    def _():
        receive_block(2, far, 0)
        tree_up(early, 2)
        receive_block(2, far, 1)
        tree_up(last, 2)

    tree_down(0, early, enc_a)
    plane_gather(enc_a, ag_s.at[0], ag_r.at[0])()
    absorb(enc_a, 0, early)
    project_part(0, early * width, True)

    @pl.when(inner == 0)
    def _():
        receive_block(3, far, 0)
        tree_up(early, 2)
        tree_across(early, 2)
        receive_block(3, far, 1)
        tree_up(last, 2)
        tree_across(last, 2)

    tree_down(early, 2, enc_b)
    finish_b = plane_gather(enc_b, ag_s.at[1], ag_r.at[1])
    tree_down(last, 2, enc_c)
    finish_c = plane_gather(enc_c, ag_s.at[2], ag_r.at[2])
    finish_b()
    absorb(enc_b, early, 2)
    project_part(early * width, 2 * width, False)
    finish_c()
    absorb(enc_c, last, 2)
    project_last(last * width, 2 * width)

    for p in range(n_mp):
        for bits in range(1, n_mp):
            rs_copy(p, flip(m, bits), m).wait_send()
    tree_finish(0, early)
    tree_finish(early, 2)
    tree_finish(last, 2)
    for bits in range(1, n_seq):
        for j in range(per_block):
            for k in range(2):
                out_copy(bits, j, k).wait_send()

    state = [dec_ref[rows_of(part), :].astype(jnp.float32) for part in range(parts)]
    per_part = n_seq // parts
    finish = [None] * parts
    for layer in range(layers):
        for part in range(parts):
            if layer > 0:
                finish[part]()
                span = rows_of(part)
                normalise(
                    dec_next.at[layer - 1, part], dec_normed.at[span], part_rows, dec_gain_ref, layer
                )
                project_queries(layer, span)
            attend(part * per_part, per_part)
            scatter_output(layer, part)
        for part in range(parts):
            state[part] = state[part] + collect_output(layer, part)
            if layer + 1 < layers:
                dec_next[layer, part, m] = state[part].astype(jnp.bfloat16)
                index = 1 + layer * parts + part
                finish[part] = direct_gather(
                    dec_next.at[layer, part], dec_ps.at[index], dec_pr.at[index]
                )
                if part == 0:
                    project_memory(layer + 1)
            else:
                out_ref[rows_of(part), :] = state[part].astype(out_ref.dtype)
    for layer in range(layers):
        for part in range(parts):
            for bits in range(1, n_mp):
                att_copy(layer, part, flip(m, bits), m).wait_send()


def whole_fast(
    enc_rows,
    ffn_in,
    ffn_out,
    enc_gain,
    final_gain,
    sent_lengths,
    group_table,
    dec_rows,
    dec_gain,
    w_query,
    w_key,
    w_value,
    w_output,
):
    n_seq, n_mp = lax.axis_size("seq"), lax.axis_size("mp")
    rows, width = enc_rows.shape
    depth, units = ffn_in.shape[0], ffn_in.shape[1] // n_seq
    out_width = ffn_out.shape[1]
    total = rows * n_seq
    full = width * n_mp
    targets = dec_rows.shape[0]
    layers, _, heads_width = w_query.shape
    slot_total = 2 * rows
    per_block = out_width // width
    share = total // n_mp
    half = jnp.bfloat16
    dma = pltpu.SemaphoreType.DMA
    return pl.pallas_call(
        functools.partial(ffn_kernel, n_seq, n_mp),
        out_shape=jax.ShapeDtypeStruct(dec_rows.shape, dec_rows.dtype),
        in_specs=[pl.BlockSpec(memory_space=pltpu.VMEM)] * 3
        + [pl.BlockSpec(memory_space=pltpu.SMEM)] * 2
        + [pl.BlockSpec(memory_space=pltpu.VMEM)] * 2
        + [pl.BlockSpec(memory_space=pl.ANY)] * 6,
        out_specs=pl.BlockSpec(memory_space=pltpu.VMEM),
        scratch_shapes=[
            pltpu.VMEM((n_mp, total, width), half),
            pltpu.VMEM((total, full), half),
            pltpu.VMEM((n_seq, depth, units), half),
            pltpu.VMEM((n_seq, per_block, units, width), half),
            pltpu.VMEM((total, units), half),
            pltpu.VMEM((n_mp, total, width), half),
            pltpu.VMEM((n_mp, n_mp, share, width), half),
            pltpu.VMEM((2, n_mp, share, width), half),
            pltpu.VMEM((3, n_mp, share, width), half),
            pltpu.VMEM((n_mp, n_mp - 4, share, width), half),
            pltpu.VMEM((n_mp, 2, share, width), half),
            pltpu.VMEM((n_mp, 2, share, width), half),
            dma((n_seq,)),
            dma((n_seq,)),
            dma((n_mp,)),
            dma((n_mp,)),
            dma((n_seq,)),
            dma((n_seq,)),
            dma((n_seq, per_block, 2)),
            dma((n_seq, per_block, 2)),
            dma((n_mp, n_mp)),
            dma((n_mp, n_mp)),
            dma((4, n_mp)),
            dma((3, n_mp)),
            dma((3, n_mp)),
            dma((3, n_mp)),
            dma((4,)),
            pltpu.VMEM(w_query.shape, half),
            pltpu.VMEM(w_key.shape, half),
            pltpu.VMEM(w_value.shape, half),
            pltpu.VMEM(w_output.shape, half),
            dma((2 + 2 * n_mp,)),
            pltpu.VMEM((n_mp, targets, width), half),
            pltpu.VMEM((layers, 2, n_mp, targets // 2, width), half),
            pltpu.VMEM((targets, full), half),
            pltpu.VMEM((targets, heads_width), half),
            pltpu.VMEM((slot_total, full), half),
            pltpu.VMEM((slot_total, width), jnp.float32),
            pltpu.VMEM((2, slot_total, heads_width), jnp.float32),
            pltpu.VMEM((slot_total, heads_width), half),
            pltpu.VMEM((slot_total, heads_width), half),
            pltpu.VMEM((targets, heads_width), half),
            pltpu.VMEM((layers, 2, n_mp, targets // 2, width), half),
            pltpu.VMEM((layers, 2, n_mp, targets // 2, width), half),
            dma((2 * layers, n_mp)),
            dma((2 * layers, n_mp)),
            dma((layers, 2, n_mp)),
            dma((layers, 2, n_mp)),
            pltpu.VMEM((n_seq, slot_total // n_seq, rows), half),
            pltpu.VMEM((n_seq, 1, slot_total // n_seq), jnp.float32),
            dma((per_block,)),
        ],
        compiler_params=pltpu.CompilerParams(
            collective_id=0, has_side_effects=True, vmem_limit_bytes=60 * 1024 * 1024
        ),
    )(
        enc_rows,
        enc_gain.reshape(1, full),
        final_gain.reshape(1, full),
        sent_lengths,
        group_table,
        dec_rows,
        dec_gain,
        ffn_in,
        ffn_out,
        w_query,
        w_key,
        w_value,
        w_output,
    )


def fast_shapes(enc_rows, ffn_in, ffn_out, dec_rows, w_query):
    n_seq, n_mp = lax.axis_size("seq"), lax.axis_size("mp")
    power = n_seq == 4 and n_mp == 8 and ffn_out.shape[1] == 2 * enc_rows.shape[1]
    aligned = (
        enc_rows.shape[1] % 128 == 0
        and ffn_in.shape[0] % 128 == 0
        and (ffn_in.shape[1] // n_seq) % 256 == 0
        and ffn_out.shape[1] % enc_rows.shape[1] == 0
        and enc_rows.shape[0] % 256 == 0
        and dec_rows.shape[0] % 256 == 0
        and (2 * enc_rows.shape[0] // n_seq) % 128 == 0
        and w_query.shape[2] % 256 == 0
        and w_query.shape[1] % 256 == 0
    )
    return power and aligned


def shards(
    enc_rows,
    ffn_in,
    ffn_out,
    enc_gain,
    final_gain,
    sent_lengths,
    group_table,
    dec_rows,
    dec_gain,
    w_query,
    w_key,
    w_value,
    w_output,
):
    group_count = lax.axis_size("seq")
    my_group = lax.axis_index("seq")
    col_width = enc_rows.shape[1]
    col_start = lax.axis_index("mp") * col_width
    row_count = enc_rows.shape[0]
    max_length = 2 * row_count // group_count
    fast = fast_shapes(enc_rows, ffn_in, ffn_out, dec_rows, w_query)
    if not fast:
        whole_rows = lax.all_gather(enc_rows, "mp", axis=1, tiled=True)
        normed = rms_scale(whole_rows.astype(jnp.float32), enc_gain).astype(jnp.bfloat16)
        full_in = lax.all_gather(ffn_in, "seq", axis=0, tiled=True)
        inner = jnp.dot(normed, full_in, preferred_element_type=jnp.float32)
        hidden = jnp.maximum(inner, 0.0).astype(jnp.bfloat16)
        partial_out = jnp.dot(
            hidden,
            lax.all_gather(ffn_out, "seq", axis=1, tiled=True),
            preferred_element_type=jnp.float32,
        )
    my_lengths = lax.dynamic_index_in_dim(sent_lengths, my_group, 0, keepdims=False)
    my_targets = lax.dynamic_index_in_dim(group_table, my_group, 0, keepdims=False)
    ordinal = jnp.arange(group_count, dtype=jnp.int32)
    my_starts = jnp.sum(
        jnp.where(ordinal[None, :] < ordinal[:, None], my_lengths[None, :], 0), axis=1
    )
    group_ids = jnp.arange(group_count, dtype=jnp.int32)
    matches = my_targets[None, :] == group_ids[:, None]
    send_starts = jnp.sum(jnp.where(matches, my_starts[None, :], 0), axis=1)
    positions = jnp.arange(max_length, dtype=jnp.int32)
    row_index = jnp.minimum(send_starts[:, None] + positions[None, :], row_count - 1)
    recv_lengths = jnp.sum(jnp.where(group_table == my_group, sent_lengths, 0), axis=1)
    live_mask = positions[None, :] < recv_lengths[:, None]
    if fast:
        return whole_fast(
            enc_rows,
            ffn_in,
            ffn_out,
            enc_gain,
            final_gain,
            sent_lengths,
            group_table,
            dec_rows,
            dec_gain,
            w_query,
            w_key,
            w_value,
            w_output,
        )
    kv_width = w_key.shape[2]
    weight_list = []
    for layer_index in range(LAYERS):
        weight_list.append(w_key[layer_index])
        weight_list.append(w_value[layer_index])
    enc_share = lax.psum_scatter(partial_out, "mp", scatter_dimension=1, tiled=True)
    encoded = enc_rows.astype(jnp.float32) + enc_share
    squares = lax.psum(jnp.sum(encoded * encoded, axis=1), "mp")
    gain_part = lax.dynamic_slice_in_dim(final_gain, col_start, col_width, 0)
    memory = (encoded * lax.rsqrt(squares / D + epsilon)[:, None] * gain_part).astype(jnp.bfloat16)
    blocks = memory[row_index]
    gathered = lax.all_gather(
        lax.all_to_all(blocks, "seq", split_axis=0, concat_axis=0, tiled=True),
        "mp",
        axis=2,
        tiled=True,
    )
    projected = tuple(
        (
            jnp.einsum(
                "std,de->ste", gathered, weight_matrix, preferred_element_type=jnp.float32
            ).astype(jnp.bfloat16)
            for weight_matrix in weight_list
        )
    )
    tgt_rows = dec_rows.shape[0]
    per_sentence = tgt_rows // group_count
    local_heads = kv_width // DH
    final_state = dec_rows.astype(jnp.float32)
    for layer_index in range(LAYERS):
        state_half = lax.all_gather(final_state.astype(jnp.bfloat16), "mp", axis=1, tiled=True)
        normed_rows = rms_scale(state_half.astype(jnp.float32), dec_gain[layer_index]).astype(
            jnp.bfloat16
        )
        queries = (
            jnp.dot(normed_rows, w_query[layer_index], preferred_element_type=jnp.float32)
            * DH ** (-0.5)
        ).astype(jnp.bfloat16)
        query_heads = queries.reshape(group_count, per_sentence, local_heads, DH)
        key_heads = projected[2 * layer_index].reshape(group_count, max_length, local_heads, DH)
        value_heads = projected[2 * layer_index + 1].reshape(
            group_count, max_length, local_heads, DH
        )
        scores = jnp.einsum(
            "sqhd,sthd->shqt", query_heads, key_heads, preferred_element_type=jnp.float32
        )
        scores = jnp.where(live_mask[:, None, None, :], scores, -jnp.inf)
        weights = jax.nn.softmax(scores, axis=-1).astype(jnp.bfloat16)
        attended = jnp.einsum(
            "shqt,sthd->sqhd", weights, value_heads, preferred_element_type=jnp.float32
        ).astype(jnp.bfloat16)
        final_state = final_state + lax.psum_scatter(
            jnp.dot(
                attended.reshape(tgt_rows, kv_width),
                w_output[layer_index],
                preferred_element_type=jnp.float32,
            ).astype(jnp.bfloat16),
            "mp",
            scatter_dimension=1,
            tiled=True,
        ).astype(jnp.float32)
    return final_state.astype(jnp.bfloat16)


def solution(mesh):
    in_specs = (
        P("seq", "mp"),
        P("seq", "mp"),
        P("mp", "seq"),
        P(),
        P(),
        P(),
        P(),
        P("seq", "mp"),
        P(),
        P(None, None, "mp"),
        P(None, None, "mp"),
        P(None, None, "mp"),
        P(None, "mp", None),
    )
    out_specs = P("seq", "mp")
    return jax.shard_map(shards, mesh=mesh, in_specs=in_specs, out_specs=out_specs, check_vma=False)
```

```python
import functools

import jax
import jax.numpy as jnp
from jax import lax
from jax.experimental import pallas as pl
from jax.experimental.pallas import tpu as pltpu
from jax.sharding import PartitionSpec as P

MESH = pl.DeviceIdType.MESH

D = 1024
DH = 128
LAYERS = 2


epsilon = 1e-06


def rms_scale(values, gain_row):
    mean_square = jnp.mean(values * values, axis=-1, keepdims=True)
    return values * lax.rsqrt(mean_square + epsilon) * gain_row


def flip(index, bits):
    out = index
    for power in (1, 2, 4, 8, 16, 32):
        if bits & power:
            out = out + power - 2 * power * ((out // power) % 2)
    return out


def z_order(count):
    return sorted(range(1, count), key=lambda bits: (bits == 1, bits))


def column_order(n_seq, per_block):
    inner = [block * per_block + j for block in range(1, n_seq - 1) for j in range(per_block)]
    outer = [block * per_block + j for j in range(per_block) for block in (0, n_seq - 1)]
    return inner + outer


def ffn_kernel(
    n_seq,
    n_mp,
    enc_ref,
    gain_ref,
    final_gain_ref,
    lengths_ref,
    table_ref,
    dec_ref,
    dec_gain_ref,
    fin_ref,
    fout_ref,
    wq_ref,
    wk_ref,
    wv_ref,
    wo_ref,
    out_ref,
    enc_all,
    normed,
    win,
    wout,
    hidden,
    part_out,
    part_in,
    tree_out,
    tree_in,
    enc_a,
    enc_b,
    enc_c,
    enc_zs,
    enc_zr,
    enc_ps,
    enc_pr,
    in_s,
    in_r,
    out_s,
    out_r,
    rs_s,
    rs_r,
    tree_s,
    tree_r,
    ag_s,
    ag_r,
    local_sem,
    wq,
    wk,
    wv,
    wo,
    w_sem,
    dec_all,
    dec_next,
    dec_normed,
    queries,
    memory,
    square,
    kv_acc,
    keys,
    values,
    attended,
    att_out,
    att_in,
    dec_ps,
    dec_pr,
    att_ps,
    att_pr,
    sel,
    mask,
    own_out_sem,
):
    s = lax.axis_index("seq")
    m = lax.axis_index("mp")
    rows, width = enc_ref.shape
    depth = fin_ref.shape[0]
    units = fin_ref.shape[1] // n_seq
    out_width = fout_ref.shape[1]
    total_rows = rows * n_seq
    per_block = out_width // width

    order = column_order(n_seq, per_block)
    early = (n_seq - 2) * per_block

    barrier = pltpu.get_barrier_semaphore()
    for bits in range(1, n_seq):
        pl.semaphore_signal(barrier, inc=1, device_id=(flip(s, bits), m), device_id_type=MESH)
    for bits in range(1, n_mp):
        pl.semaphore_signal(barrier, inc=1, device_id=(s, flip(m, bits)), device_id_type=MESH)
    pl.semaphore_wait(barrier, n_seq + n_mp - 2)

    my_rows = pl.ds(pl.multiple_of(s * rows, rows), rows)

    def plane_gather(buf, send_sem, recv_sem):
        def copy(slot, bits, peer):
            return pltpu.make_async_remote_copy(
                src_ref=buf.at[slot],
                dst_ref=buf.at[slot],
                send_sem=send_sem.at[bits],
                recv_sem=recv_sem.at[bits],
                device_id=(s, peer),
                device_id_type=MESH,
            )

        across = [bits for bits in range(n_mp - 2, 1, -2)]
        direct = {bits: copy(m, bits, flip(m, bits)) for bits in across + [1]}
        for bits in across + [1]:
            direct[bits].start()

        def finish():
            onward = []
            for bits in reversed(across):
                direct[bits].wait_recv()
                forward = copy(flip(m, bits), bits + 1, flip(m, 1))
                forward.start()
                onward.append(forward)
            direct[1].wait_recv()
            for forward in onward:
                forward.wait()
            for bits in across + [1]:
                direct[bits].wait_send()

        return finish

    def direct_gather(buf, send_sem, recv_sem):
        def copy(bits):
            return pltpu.make_async_remote_copy(
                src_ref=buf.at[m],
                dst_ref=buf.at[m],
                send_sem=send_sem.at[bits],
                recv_sem=recv_sem.at[bits],
                device_id=(s, flip(m, bits)),
                device_id_type=MESH,
            )

        for bits in range(n_mp - 1, 0, -1):
            copy(bits).start()

        def finish():
            for bits in range(1, n_mp):
                copy(bits).wait()

        return finish

    def normalise(buf, dst, count, gain, gain_row):
        step = min(256, count)

        def body(i, carry):
            span = pl.ds(pl.multiple_of(i * step, step), step)
            squares = jnp.zeros((step, 1), jnp.float32)
            for k in range(n_mp):
                value = buf[k, span, :].astype(jnp.float32)
                squares = squares + jnp.sum(value * value, axis=1, keepdims=True)
            scale = lax.rsqrt(squares / (n_mp * width) + epsilon)
            for k in range(n_mp):
                cols = pl.ds(k * width, width)
                value = buf[k, span, :].astype(jnp.float32)
                dst[span, cols] = (value * scale * gain[pl.ds(gain_row, 1), cols]).astype(
                    jnp.bfloat16
                )
            return carry

        lax.fori_loop(0, count // step, body, 0)

    def product(left, right, layer, store):
        columns = right.shape[2]
        step = min(256, columns)

        def body(i, carry):
            cols = pl.ds(pl.multiple_of(i * step, step), step)
            store(
                cols, jnp.dot(left[...], right[layer, :, cols], preferred_element_type=jnp.float32)
            )
            return carry

        lax.fori_loop(0, columns // step, body, 0)

    def project_queries(layer, span):
        def store(cols, value):
            queries[span, cols] = (value * DH ** (-0.5)).astype(jnp.bfloat16)

        product(dec_normed.at[span], wq, layer, store)

    def project_part(cols0, count, first):
        step = min(256, wk.shape[2])
        part = pl.ds(cols0, count)

        def body(i, carry):
            cols = pl.ds(pl.multiple_of(i * step, step), step)
            for index, weight in enumerate((wk, wv)):
                value = jnp.dot(
                    memory[:, part], weight[0, part, cols], preferred_element_type=jnp.float32
                )
                if not first:
                    value = value + kv_acc[index, :, cols]
                kv_acc[index, :, cols] = value
            return carry

        lax.fori_loop(0, wk.shape[2] // step, body, 0)

    def row_scale():
        squares = jnp.sum(square[...], axis=1, keepdims=True)
        return lax.rsqrt(squares / (n_mp * width) + epsilon)

    def project_last(cols0, count):
        step = min(256, wk.shape[2])
        part = pl.ds(cols0, count)
        scale = row_scale()

        def body(i, carry):
            cols = pl.ds(pl.multiple_of(i * step, step), step)
            for index, (weight, dst) in enumerate(((wk, keys), (wv, values))):
                value = kv_acc[index, :, cols] + jnp.dot(
                    memory[:, part], weight[0, part, cols], preferred_element_type=jnp.float32
                )
                dst[:, cols] = (value * scale).astype(jnp.bfloat16)
            return carry

        lax.fori_loop(0, wk.shape[2] // step, body, 0)

    def project_memory(layer):
        scale = row_scale()

        def store_key(cols, value):
            keys[:, cols] = (value * scale).astype(jnp.bfloat16)

        def store_value(cols, value):
            values[:, cols] = (value * scale).astype(jnp.bfloat16)

        product(memory, wk, layer, store_key)
        product(memory, wv, layer, store_value)

    slot_rows = sel.shape[1]
    targets = dec_ref.shape[0]
    per_sentence = targets // n_seq
    layers = wq_ref.shape[0]
    heads = wq_ref.shape[2] // DH

    def attend(first, count):
        def body(i, carry):
            span = pl.ds(pl.multiple_of(i * per_sentence, per_sentence), per_sentence)
            slot_span = pl.ds(pl.multiple_of(i * slot_rows, slot_rows), slot_rows)
            live = mask[i] > 0.5
            columns = [pl.ds(head * DH, DH) for head in range(heads)]
            scores = [
                lax.dot_general(
                    queries[span, cols],
                    keys[slot_span, cols],
                    (((1,), (1,)), ((), ())),
                    preferred_element_type=jnp.float32,
                )
                for cols in columns
            ]
            scores = [jnp.where(live, score, -jnp.inf) for score in scores]
            tops = [jnp.max(score, axis=1, keepdims=True) for score in scores]
            powers = [jnp.exp(score - top) for score, top in zip(scores, tops)]
            sums = [jnp.sum(power, axis=1, keepdims=True) for power in powers]
            weights = [
                (power * (1.0 / total)).astype(jnp.bfloat16) for power, total in zip(powers, sums)
            ]
            for cols, weight in zip(columns, weights):
                attended[span, cols] = jnp.dot(
                    weight, values[slot_span, cols], preferred_element_type=jnp.float32
                ).astype(jnp.bfloat16)
            return carry

        lax.fori_loop(first, first + count, body, 0, unroll=True)

    parts = 2
    part_rows = targets // parts

    def rows_of(part):
        return pl.ds(part * part_rows, part_rows)

    def att_copy(layer, part, slot, source):
        return pltpu.make_async_remote_copy(
            src_ref=att_out.at[layer, part, slot],
            dst_ref=att_in.at[layer, part, source],
            send_sem=att_ps.at[layer, part, slot],
            recv_sem=att_pr.at[layer, part, source],
            device_id=(s, slot),
            device_id_type=MESH,
        )

    def scatter_output(layer, part):
        step = max(width, 256)

        def body(i, carry):
            chip = (i + m // (step // width) + 1) % (n_mp * width // step)
            cols = pl.ds(pl.multiple_of(chip * step, step), step)
            value = jnp.dot(
                attended[rows_of(part), :], wo[layer, :, cols], preferred_element_type=jnp.float32
            ).astype(jnp.bfloat16)
            for j in range(step // width):
                slot = chip * (step // width) + j
                att_out[layer, part, slot] = value[:, j * width : (j + 1) * width]

                @pl.when(slot != m)
                def _():
                    att_copy(layer, part, slot, m).start()

            return carry

        lax.fori_loop(0, n_mp * width // step, body, 0)

    def collect_output(layer, part):
        total = att_out[layer, part, m].astype(jnp.float32)
        for bits in range(1, n_mp):
            peer = flip(m, bits)
            att_copy(layer, part, peer, peer).wait_recv()
            total = total + att_in[layer, part, peer].astype(jnp.float32)
        return total

    own_enc = pltpu.make_async_copy(enc_ref, enc_all.at[m, my_rows], local_sem.at[0])
    own_enc.start()

    def enc_copy(bits):
        return pltpu.make_async_remote_copy(
            src_ref=enc_ref,
            dst_ref=enc_all.at[m, my_rows],
            send_sem=enc_zs.at[bits],
            recv_sem=enc_zr.at[bits],
            device_id=(flip(s, bits), m),
            device_id_type=MESH,
        )

    for bits in (2, 1):
        enc_copy(bits).start()
    across_rows = pl.ds(pl.multiple_of(flip(s, 2) * rows, rows), rows)
    enc_onward = pltpu.make_async_remote_copy(
        src_ref=enc_all.at[m, across_rows],
        dst_ref=enc_all.at[m, across_rows],
        send_sem=enc_zs.at[3],
        recv_sem=enc_zr.at[3],
        device_id=(flip(s, 1), m),
        device_id_type=MESH,
    )
    inner = (s % 2 + s // 2) % 2

    own_in = pltpu.make_async_copy(
        fin_ref.at[:, pl.ds(pl.multiple_of(s * units, units), units)], win.at[s], local_sem.at[1]
    )
    own_in.start()
    own_out = [
        pltpu.make_async_copy(
            fout_ref.at[
                pl.ds(pl.multiple_of(s * units, units), units), pl.ds(j * width, width)
            ],
            wout.at[s, j],
            own_out_sem.at[j],
        )
        for j in range(per_block)
    ]
    for copy in own_out:
        copy.start()
    def in_copy(bits):
        peer = flip(s, bits)
        return pltpu.make_async_remote_copy(
            src_ref=fin_ref.at[:, pl.ds(pl.multiple_of(peer * units, units), units)],
            dst_ref=win.at[s],
            send_sem=in_s.at[bits],
            recv_sem=in_r.at[bits],
            device_id=(peer, m),
            device_id_type=MESH,
        )

    @pl.when(inner == 1)
    def _():
        for bits in (2, 3):
            in_copy(bits).start()

    enc_copy(2).wait_recv()
    enc_onward.start()

    @pl.when(inner == 0)
    def _():
        for bits in (2, 3):
            in_copy(bits).start()

    in_copy(1).start()
    piece = units // 2

    def out_copy(bits, j, k):
        peer = flip_any(bits)
        return pltpu.make_async_remote_copy(
            src_ref=fout_ref.at[
                pl.ds(pl.multiple_of(peer * units + k * piece, piece), piece),
                pl.ds(j * width, width),
            ],
            dst_ref=wout.at[s, j, pl.ds(k * piece, piece)],
            send_sem=out_s.at[bits, j, k],
            recv_sem=out_r.at[bits, j, k],
            device_id=(peer, m),
            device_id_type=MESH,
        )

    def flip_any(bits):
        if isinstance(bits, int):
            return flip(s, bits)
        return flip(s, 2) * (3 - bits) + flip(s, 3) * (bits - 2)

    def across_out(j, k):
        for bits in (3, 2):
            out_copy(bits, j, k).start()

    for j in range(per_block):
        for k in range(2):
            out_copy(1, j, k).start()

    @pl.when(inner == 1)
    def _():
        for j in range(per_block):
            for k in range(2):
                across_out(j, k)

    weight_copies = []
    for index, (src, dst) in enumerate(((wq_ref, wq), (wo_ref, wo))):
        copy = pltpu.make_async_copy(src, dst, w_sem.at[index])
        copy.start()
        weight_copies.append(copy)
    for index, (src, dst) in enumerate(((wk_ref, wk), (wv_ref, wv))):
        for slot, source in enumerate(order):
            copy = pltpu.make_async_copy(
                src.at[:, pl.ds(source * width, width)],
                dst.at[:, pl.ds(slot * width, width)],
                w_sem.at[2 + index * n_mp + slot],
            )
            copy.start()
            weight_copies.append(copy)
    own_dec = pltpu.make_async_copy(dec_ref, dec_all.at[m], local_sem.at[3])
    own_dec.start()
    own_dec.wait()
    finish_dec = plane_gather(dec_all, dec_ps.at[0], dec_pr.at[0])

    own_enc.wait()
    enc_copy(1).wait_recv()
    enc_onward.wait_recv()
    for bits in (2, 1):
        enc_copy(bits).wait_send()
    enc_onward.wait_send()

    plane_gather(enc_all, enc_ps, enc_pr)()

    chunk = min(256, rows)

    normalise(enc_all, normed, total_rows, gain_ref, 0)

    for source in range(n_seq):
        start = jnp.int32(0)
        before = jnp.int32(0)
        for j in range(n_seq):
            start = start + jnp.where(table_ref[source, j] == s, before, 0)
            before = before + lengths_ref[source, j]
        slot_row = lax.broadcasted_iota(jnp.int32, (slot_rows, rows), 0)
        column = lax.broadcasted_iota(jnp.int32, (slot_rows, rows), 1)
        wanted = jnp.minimum(slot_row + start, rows - 1)
        sel[source] = jnp.where(wanted == column, 1.0, 0.0).astype(jnp.bfloat16)
    for source in range(n_seq):
        length = jnp.int32(0)
        for j in range(n_seq):
            length = length + jnp.where(table_ref[source, j] == s, lengths_ref[source, j], 0)
        slot = lax.broadcasted_iota(jnp.int32, (1, slot_rows), 1)
        mask[source] = jnp.where(slot < length, 1.0, 0.0)

    finish_dec()
    normalise(dec_all, dec_normed, targets, dec_gain_ref, 0)
    for copy in weight_copies:
        copy.wait()
    project_queries(0, pl.ds(0, targets))

    own_in.wait()
    for bits in range(1, n_seq):
        in_copy(bits).wait()

    tile = min(256, units)

    def hidden_chunk(i, carry):
        cols = pl.ds(pl.multiple_of((i % (units // tile)) * tile, tile), tile)
        span = pl.ds(pl.multiple_of((i // (units // tile)) * chunk, chunk), chunk)
        acc = jnp.zeros((chunk, tile), jnp.float32)
        for k in range(n_seq):
            acc = acc + jnp.dot(
                normed[span, pl.ds(k * depth, depth)],
                win[k, :, cols],
                preferred_element_type=jnp.float32,
            )
        hidden[span, cols] = jnp.maximum(acc, 0.0).astype(jnp.bfloat16)
        return carry

    lax.fori_loop(0, (total_rows // chunk) * (units // tile), hidden_chunk, 0)

    share = total_rows // n_mp
    per_chunk = chunk // share
    per_source = rows // share
    my_share = pl.ds(pl.multiple_of(m * share, share), share)

    def position(block, j):
        within = (block % 2 + block // 2) % 2
        outside = early + block // (n_seq - 1) + 2 * j
        return within * ((block - 1) * per_block + j) + (1 - within) * outside

    def rs_copy(p, peer, source):
        return pltpu.make_async_remote_copy(
            src_ref=part_out.at[p, pl.ds(pl.multiple_of(peer * share, share), share)],
            dst_ref=part_in.at[p, source],
            send_sem=rs_s.at[p, peer],
            recv_sem=rs_r.at[p, source],
            device_id=(s, peer),
            device_id_type=MESH,
        )

    def send_block(block, j):
        p = position(block, j)

        def rows_chunk(i, carry):
            c = (i + m // per_chunk + 1) % (total_rows // chunk)
            span = pl.ds(pl.multiple_of(c * chunk, chunk), chunk)
            part_out[p, span, :] = jnp.dot(
                hidden[span, :], wout[block, j], preferred_element_type=jnp.float32
            ).astype(jnp.bfloat16)
            for t in range(per_chunk):
                peer = c * per_chunk + t

                @pl.when(peer != m)
                def _():
                    rs_copy(p, peer, m).start()

            return carry

        lax.fori_loop(0, total_rows // chunk, rows_chunk, 0)

    def receive_block(bits, block, j):
        for k in range(2):
            out_copy(bits, j, k).wait_recv()
        send_block(block, j)

    def plane_sum(p):
        total = part_out[p, my_share, :].astype(jnp.float32)
        for bits in range(1, n_mp):
            peer = flip(m, bits)
            rs_copy(p, peer, peer).wait_recv()
            total = total + part_in[p, peer].astype(jnp.float32)
        return total

    def tree_copy(bits, p0, count):
        return pltpu.make_async_remote_copy(
            src_ref=tree_out.at[min(bits, 1), pl.ds(p0, count)],
            dst_ref=tree_in.at[min(bits, 2), pl.ds(p0, count)],
            send_sem=tree_s.at[bits, p0],
            recv_sem=tree_r.at[min(bits, 2), p0],
            device_id=(flip(s, max(bits, 1)), m),
            device_id_type=MESH,
        )

    def residual(p):
        return enc_all[order[p], my_share, :].astype(jnp.float32)

    def tree_up(p0, count):
        for p in range(p0, p0 + count):
            tree_out[0, p] = plane_sum(p).astype(jnp.bfloat16)

        @pl.when(inner == 1)
        def _():
            tree_copy(0, p0, count).start()

    def tree_across(p0, count):
        @pl.when(inner == 0)
        def _():
            tree_copy(0, p0, count).wait_recv()
            for p in range(p0, p0 + count):
                tree_out[1, p] = (
                    tree_out[0, p].astype(jnp.float32) + tree_in[0, p].astype(jnp.float32)
                ).astype(jnp.bfloat16)
            for bits in z_order(n_seq):
                tree_copy(bits, p0, count).start()

    def tree_down(p0, count, enc_buf, first=0):
        def combine(own):
            for p in range(p0, p0 + count):
                total = own[p].astype(jnp.float32) + tree_in[2, p].astype(jnp.float32)
                enc_buf[m, p - p0 + first] = (total + residual(p)).astype(jnp.bfloat16)

        tree_copy(2, p0, count).wait_recv()

        @pl.when(inner == 0)
        def _():
            combine(tree_out.at[1])

        @pl.when(inner == 1)
        def _():
            tree_copy(1, p0, count).wait_recv()
            combine(tree_in.at[1])

    def tree_finish(p0, count):
        @pl.when(inner == 1)
        def _():
            tree_copy(0, p0, count).wait_send()

        @pl.when(inner == 0)
        def _():
            for bits in z_order(n_seq):
                tree_copy(bits, p0, count).wait_send()

    last = early + 2

    def absorb(enc_buf, p0, count):
        for source in range(n_seq):
            span = pl.ds(source * slot_rows, slot_rows)
            total = jnp.zeros((slot_rows, width), jnp.float32)
            for q in range(count):
                block = enc_buf[pl.ds(source * per_source, per_source), q].reshape(rows, width)
                slot = jnp.dot(sel[source], block, preferred_element_type=jnp.float32)
                total = total + slot * slot
                memory[span, pl.ds((p0 + q) * width, width)] = (
                    slot * final_gain_ref[:, pl.ds(order[p0 + q] * width, width)]
                ).astype(jnp.bfloat16)
            if p0 == 0:
                square[span, :] = total
            else:
                square[span, :] = square[span, :] + total

    last = early + 2
    near = 2 - s // 2
    far = 3 - 3 * (s // 2)
    near_bits = 2 + inner

    for j in range(per_block):
        own_out[j].wait()
        send_block(s, j)
    for j in range(per_block):
        receive_block(1, flip(s, 1), j)
    for j in range(per_block - 1):
        receive_block(near_bits, near, j)
    out_copy(near_bits, per_block - 1, 0).wait_recv()

    @pl.when(inner == 0)
    def _():
        out_copy(2, 0, 0).start()

    out_copy(near_bits, per_block - 1, 1).wait_recv()

    @pl.when(inner == 0)
    def _():
        out_copy(2, 0, 1).start()
        for k in range(2):
            out_copy(2, 1, k).start()

    send_block(near, per_block - 1)
    tree_up(0, early)
    tree_across(0, early)

    @pl.when(inner == 0)
    def _():
        for j in range(per_block):
            for k in range(2):
                out_copy(3, j, k).start()

    @pl.when(inner == 1)
    def _():
        receive_block(2, far, 0)
        tree_up(early, 2)
        receive_block(2, far, 1)
        tree_up(last, 2)

    tree_down(0, early, enc_a)
    plane_gather(enc_a, ag_s.at[0], ag_r.at[0])()
    absorb(enc_a, 0, early)
    project_part(0, early * width, True)

    @pl.when(inner == 0)
    def _():
        receive_block(3, far, 0)
        tree_up(early, 2)
        tree_across(early, 2)
        receive_block(3, far, 1)
        tree_copy(0, last, 2).wait_recv()
        for p in (last + s // 2, last + 1 - s // 2):
            tree_out[1, p] = (plane_sum(p) + tree_in[0, p].astype(jnp.float32)).astype(jnp.bfloat16)
            for bits in z_order(n_seq):
                tree_copy(bits, p, 1).start()

    tree_down(early, 2, enc_b)
    finish_b = plane_gather(enc_b, ag_s.at[1], ag_r.at[1])
    for p in range(last, last + 2):
        tree_down(p, 1, enc_c, p - last)
    finish_c = plane_gather(enc_c, ag_s.at[2], ag_r.at[2])
    finish_b()
    absorb(enc_b, early, 2)
    project_part(early * width, 2 * width, False)
    finish_c()
    absorb(enc_c, last, 2)
    project_last(last * width, 2 * width)

    for p in range(n_mp):
        for bits in range(1, n_mp):
            rs_copy(p, flip(m, bits), m).wait_send()
    tree_finish(0, early)
    tree_finish(early, 2)
    @pl.when(inner == 1)
    def _():
        tree_copy(0, last, 2).wait_send()

    @pl.when(inner == 0)
    def _():
        for p in range(last, last + 2):
            for bits in z_order(n_seq):
                tree_copy(bits, p, 1).wait_send()

    for bits in range(1, n_seq):
        for j in range(per_block):
            for k in range(2):
                out_copy(bits, j, k).wait_send()

    state = [dec_ref[rows_of(part), :].astype(jnp.float32) for part in range(parts)]
    per_part = n_seq // parts
    finish = [None] * parts
    for layer in range(layers):
        for part in range(parts):
            if layer > 0:
                finish[part]()
                span = rows_of(part)
                normalise(
                    dec_next.at[layer - 1, part], dec_normed.at[span], part_rows, dec_gain_ref, layer
                )
                project_queries(layer, span)
            attend(part * per_part, per_part)
            scatter_output(layer, part)
        for part in range(parts):
            state[part] = state[part] + collect_output(layer, part)
            if layer + 1 < layers:
                dec_next[layer, part, m] = state[part].astype(jnp.bfloat16)
                index = 1 + layer * parts + part
                finish[part] = direct_gather(
                    dec_next.at[layer, part], dec_ps.at[index], dec_pr.at[index]
                )
                if part == 0:
                    project_memory(layer + 1)
            else:
                out_ref[rows_of(part), :] = state[part].astype(out_ref.dtype)
    for layer in range(layers):
        for part in range(parts):
            for bits in range(1, n_mp):
                att_copy(layer, part, flip(m, bits), m).wait_send()


def whole_fast(
    enc_rows,
    ffn_in,
    ffn_out,
    enc_gain,
    final_gain,
    sent_lengths,
    group_table,
    dec_rows,
    dec_gain,
    w_query,
    w_key,
    w_value,
    w_output,
):
    n_seq, n_mp = lax.axis_size("seq"), lax.axis_size("mp")
    rows, width = enc_rows.shape
    depth, units = ffn_in.shape[0], ffn_in.shape[1] // n_seq
    out_width = ffn_out.shape[1]
    total = rows * n_seq
    full = width * n_mp
    targets = dec_rows.shape[0]
    layers, _, heads_width = w_query.shape
    slot_total = 2 * rows
    per_block = out_width // width
    share = total // n_mp
    half = jnp.bfloat16
    dma = pltpu.SemaphoreType.DMA
    return pl.pallas_call(
        functools.partial(ffn_kernel, n_seq, n_mp),
        out_shape=jax.ShapeDtypeStruct(dec_rows.shape, dec_rows.dtype),
        in_specs=[pl.BlockSpec(memory_space=pltpu.VMEM)] * 3
        + [pl.BlockSpec(memory_space=pltpu.SMEM)] * 2
        + [pl.BlockSpec(memory_space=pltpu.VMEM)] * 2
        + [pl.BlockSpec(memory_space=pl.ANY)] * 6,
        out_specs=pl.BlockSpec(memory_space=pltpu.VMEM),
        scratch_shapes=[
            pltpu.VMEM((n_mp, total, width), half),
            pltpu.VMEM((total, full), half),
            pltpu.VMEM((n_seq, depth, units), half),
            pltpu.VMEM((n_seq, per_block, units, width), half),
            pltpu.VMEM((total, units), half),
            pltpu.VMEM((n_mp, total, width), half),
            pltpu.VMEM((n_mp, n_mp, share, width), half),
            pltpu.VMEM((2, n_mp, share, width), half),
            pltpu.VMEM((3, n_mp, share, width), half),
            pltpu.VMEM((n_mp, n_mp - 4, share, width), half),
            pltpu.VMEM((n_mp, 2, share, width), half),
            pltpu.VMEM((n_mp, 2, share, width), half),
            dma((n_seq,)),
            dma((n_seq,)),
            dma((n_mp,)),
            dma((n_mp,)),
            dma((n_seq,)),
            dma((n_seq,)),
            dma((n_seq, per_block, 2)),
            dma((n_seq, per_block, 2)),
            dma((n_mp, n_mp)),
            dma((n_mp, n_mp)),
            dma((4, n_mp)),
            dma((3, n_mp)),
            dma((3, n_mp)),
            dma((3, n_mp)),
            dma((4,)),
            pltpu.VMEM(w_query.shape, half),
            pltpu.VMEM(w_key.shape, half),
            pltpu.VMEM(w_value.shape, half),
            pltpu.VMEM(w_output.shape, half),
            dma((2 + 2 * n_mp,)),
            pltpu.VMEM((n_mp, targets, width), half),
            pltpu.VMEM((layers, 2, n_mp, targets // 2, width), half),
            pltpu.VMEM((targets, full), half),
            pltpu.VMEM((targets, heads_width), half),
            pltpu.VMEM((slot_total, full), half),
            pltpu.VMEM((slot_total, width), jnp.float32),
            pltpu.VMEM((2, slot_total, heads_width), jnp.float32),
            pltpu.VMEM((slot_total, heads_width), half),
            pltpu.VMEM((slot_total, heads_width), half),
            pltpu.VMEM((targets, heads_width), half),
            pltpu.VMEM((layers, 2, n_mp, targets // 2, width), half),
            pltpu.VMEM((layers, 2, n_mp, targets // 2, width), half),
            dma((2 * layers, n_mp)),
            dma((2 * layers, n_mp)),
            dma((layers, 2, n_mp)),
            dma((layers, 2, n_mp)),
            pltpu.VMEM((n_seq, slot_total // n_seq, rows), half),
            pltpu.VMEM((n_seq, 1, slot_total // n_seq), jnp.float32),
            dma((per_block,)),
        ],
        compiler_params=pltpu.CompilerParams(
            collective_id=0, has_side_effects=True, vmem_limit_bytes=60 * 1024 * 1024
        ),
    )(
        enc_rows,
        enc_gain.reshape(1, full),
        final_gain.reshape(1, full),
        sent_lengths,
        group_table,
        dec_rows,
        dec_gain,
        ffn_in,
        ffn_out,
        w_query,
        w_key,
        w_value,
        w_output,
    )


def fast_shapes(enc_rows, ffn_in, ffn_out, dec_rows, w_query):
    n_seq, n_mp = lax.axis_size("seq"), lax.axis_size("mp")
    power = n_seq == 4 and n_mp == 8 and ffn_out.shape[1] == 2 * enc_rows.shape[1]
    aligned = (
        enc_rows.shape[1] % 128 == 0
        and ffn_in.shape[0] % 128 == 0
        and (ffn_in.shape[1] // n_seq) % 256 == 0
        and ffn_out.shape[1] % enc_rows.shape[1] == 0
        and enc_rows.shape[0] % 256 == 0
        and dec_rows.shape[0] % 256 == 0
        and (2 * enc_rows.shape[0] // n_seq) % 128 == 0
        and w_query.shape[2] % 256 == 0
        and w_query.shape[1] % 256 == 0
    )
    return power and aligned


def shards(
    enc_rows,
    ffn_in,
    ffn_out,
    enc_gain,
    final_gain,
    sent_lengths,
    group_table,
    dec_rows,
    dec_gain,
    w_query,
    w_key,
    w_value,
    w_output,
):
    group_count = lax.axis_size("seq")
    my_group = lax.axis_index("seq")
    col_width = enc_rows.shape[1]
    col_start = lax.axis_index("mp") * col_width
    row_count = enc_rows.shape[0]
    max_length = 2 * row_count // group_count
    fast = fast_shapes(enc_rows, ffn_in, ffn_out, dec_rows, w_query)
    if not fast:
        whole_rows = lax.all_gather(enc_rows, "mp", axis=1, tiled=True)
        normed = rms_scale(whole_rows.astype(jnp.float32), enc_gain).astype(jnp.bfloat16)
        full_in = lax.all_gather(ffn_in, "seq", axis=0, tiled=True)
        inner = jnp.dot(normed, full_in, preferred_element_type=jnp.float32)
        hidden = jnp.maximum(inner, 0.0).astype(jnp.bfloat16)
        partial_out = jnp.dot(
            hidden,
            lax.all_gather(ffn_out, "seq", axis=1, tiled=True),
            preferred_element_type=jnp.float32,
        )
    my_lengths = lax.dynamic_index_in_dim(sent_lengths, my_group, 0, keepdims=False)
    my_targets = lax.dynamic_index_in_dim(group_table, my_group, 0, keepdims=False)
    ordinal = jnp.arange(group_count, dtype=jnp.int32)
    my_starts = jnp.sum(
        jnp.where(ordinal[None, :] < ordinal[:, None], my_lengths[None, :], 0), axis=1
    )
    group_ids = jnp.arange(group_count, dtype=jnp.int32)
    matches = my_targets[None, :] == group_ids[:, None]
    send_starts = jnp.sum(jnp.where(matches, my_starts[None, :], 0), axis=1)
    positions = jnp.arange(max_length, dtype=jnp.int32)
    row_index = jnp.minimum(send_starts[:, None] + positions[None, :], row_count - 1)
    recv_lengths = jnp.sum(jnp.where(group_table == my_group, sent_lengths, 0), axis=1)
    live_mask = positions[None, :] < recv_lengths[:, None]
    if fast:
        return whole_fast(
            enc_rows,
            ffn_in,
            ffn_out,
            enc_gain,
            final_gain,
            sent_lengths,
            group_table,
            dec_rows,
            dec_gain,
            w_query,
            w_key,
            w_value,
            w_output,
        )
    kv_width = w_key.shape[2]
    weight_list = []
    for layer_index in range(LAYERS):
        weight_list.append(w_key[layer_index])
        weight_list.append(w_value[layer_index])
    enc_share = lax.psum_scatter(partial_out, "mp", scatter_dimension=1, tiled=True)
    encoded = enc_rows.astype(jnp.float32) + enc_share
    squares = lax.psum(jnp.sum(encoded * encoded, axis=1), "mp")
    gain_part = lax.dynamic_slice_in_dim(final_gain, col_start, col_width, 0)
    memory = (encoded * lax.rsqrt(squares / D + epsilon)[:, None] * gain_part).astype(jnp.bfloat16)
    blocks = memory[row_index]
    gathered = lax.all_gather(
        lax.all_to_all(blocks, "seq", split_axis=0, concat_axis=0, tiled=True),
        "mp",
        axis=2,
        tiled=True,
    )
    projected = tuple(
        (
            jnp.einsum(
                "std,de->ste", gathered, weight_matrix, preferred_element_type=jnp.float32
            ).astype(jnp.bfloat16)
            for weight_matrix in weight_list
        )
    )
    tgt_rows = dec_rows.shape[0]
    per_sentence = tgt_rows // group_count
    local_heads = kv_width // DH
    final_state = dec_rows.astype(jnp.float32)
    for layer_index in range(LAYERS):
        state_half = lax.all_gather(final_state.astype(jnp.bfloat16), "mp", axis=1, tiled=True)
        normed_rows = rms_scale(state_half.astype(jnp.float32), dec_gain[layer_index]).astype(
            jnp.bfloat16
        )
        queries = (
            jnp.dot(normed_rows, w_query[layer_index], preferred_element_type=jnp.float32)
            * DH ** (-0.5)
        ).astype(jnp.bfloat16)
        query_heads = queries.reshape(group_count, per_sentence, local_heads, DH)
        key_heads = projected[2 * layer_index].reshape(group_count, max_length, local_heads, DH)
        value_heads = projected[2 * layer_index + 1].reshape(
            group_count, max_length, local_heads, DH
        )
        scores = jnp.einsum(
            "sqhd,sthd->shqt", query_heads, key_heads, preferred_element_type=jnp.float32
        )
        scores = jnp.where(live_mask[:, None, None, :], scores, -jnp.inf)
        weights = jax.nn.softmax(scores, axis=-1).astype(jnp.bfloat16)
        attended = jnp.einsum(
            "shqt,sthd->sqhd", weights, value_heads, preferred_element_type=jnp.float32
        ).astype(jnp.bfloat16)
        final_state = final_state + lax.psum_scatter(
            jnp.dot(
                attended.reshape(tgt_rows, kv_width),
                w_output[layer_index],
                preferred_element_type=jnp.float32,
            ).astype(jnp.bfloat16),
            "mp",
            scatter_dimension=1,
            tiled=True,
        ).astype(jnp.float32)
    return final_state.astype(jnp.bfloat16)


def solution(mesh):
    in_specs = (
        P("seq", "mp"),
        P("seq", "mp"),
        P("mp", "seq"),
        P(),
        P(),
        P(),
        P(),
        P("seq", "mp"),
        P(),
        P(None, None, "mp"),
        P(None, None, "mp"),
        P(None, None, "mp"),
        P(None, "mp", None),
    )
    out_specs = P("seq", "mp")
    return jax.shard_map(shards, mesh=mesh, in_specs=in_specs, out_specs=out_specs, check_vma=False)
```

```python
import functools

import jax
import jax.numpy as jnp
from jax import lax
from jax.experimental import pallas as pl
from jax.experimental.pallas import tpu as pltpu
from jax.sharding import PartitionSpec as P

MESH = pl.DeviceIdType.MESH

D = 1024
DH = 128
LAYERS = 2


epsilon = 1e-06


def rms_scale(values, gain_row):
    mean_square = jnp.mean(values * values, axis=-1, keepdims=True)
    return values * lax.rsqrt(mean_square + epsilon) * gain_row


def flip(index, bits):
    out = index
    for power in (1, 2, 4, 8, 16, 32):
        if bits & power:
            out = out + power - 2 * power * ((out // power) % 2)
    return out


def z_order(count):
    return sorted(range(1, count), key=lambda bits: (bits == 1, bits))


def column_order(n_seq, per_block):
    inner = [block * per_block + j for block in range(1, n_seq - 1) for j in range(per_block)]
    outer = [block * per_block + j for j in range(per_block) for block in (0, n_seq - 1)]
    return inner + outer


def ffn_kernel(
    n_seq,
    n_mp,
    enc_ref,
    gain_ref,
    final_gain_ref,
    lengths_ref,
    table_ref,
    dec_ref,
    dec_gain_ref,
    fin_ref,
    fout_ref,
    wq_ref,
    wk_ref,
    wv_ref,
    wo_ref,
    out_ref,
    enc_all,
    normed,
    win,
    wout,
    hidden,
    part_out,
    part_in,
    tree_out,
    tree_in,
    enc_a,
    enc_b,
    enc_c,
    enc_zs,
    enc_zr,
    enc_ps,
    enc_pr,
    in_s,
    in_r,
    out_s,
    out_r,
    rs_s,
    rs_r,
    tree_s,
    tree_r,
    ag_s,
    ag_r,
    local_sem,
    wq,
    wk,
    wv,
    wo,
    w_sem,
    dec_all,
    dec_next,
    dec_normed,
    queries,
    memory,
    square,
    kv_acc,
    keys,
    values,
    attended,
    att_out,
    att_in,
    dec_ps,
    dec_pr,
    att_ps,
    att_pr,
    sel,
    mask,
    own_out_sem,
):
    s = lax.axis_index("seq")
    m = lax.axis_index("mp")
    rows, width = enc_ref.shape
    depth = fin_ref.shape[0]
    units = fin_ref.shape[1] // n_seq
    out_width = fout_ref.shape[1]
    total_rows = rows * n_seq
    per_block = out_width // width

    order = column_order(n_seq, per_block)
    early = (n_seq - 2) * per_block

    barrier = pltpu.get_barrier_semaphore()
    for bits in range(1, n_seq):
        pl.semaphore_signal(barrier, inc=1, device_id=(flip(s, bits), m), device_id_type=MESH)
    for bits in range(1, n_mp):
        pl.semaphore_signal(barrier, inc=1, device_id=(s, flip(m, bits)), device_id_type=MESH)
    pl.semaphore_wait(barrier, n_seq + n_mp - 2)

    my_rows = pl.ds(pl.multiple_of(s * rows, rows), rows)

    def plane_gather(buf, send_sem, recv_sem):
        def copy(slot, bits, peer):
            return pltpu.make_async_remote_copy(
                src_ref=buf.at[slot],
                dst_ref=buf.at[slot],
                send_sem=send_sem.at[bits],
                recv_sem=recv_sem.at[bits],
                device_id=(s, peer),
                device_id_type=MESH,
            )

        across = [bits for bits in range(n_mp - 2, 1, -2)]
        direct = {bits: copy(m, bits, flip(m, bits)) for bits in across + [1]}
        for bits in across + [1]:
            direct[bits].start()

        def finish():
            onward = []
            for bits in reversed(across):
                direct[bits].wait_recv()
                forward = copy(flip(m, bits), bits + 1, flip(m, 1))
                forward.start()
                onward.append(forward)
            direct[1].wait_recv()
            for forward in onward:
                forward.wait()
            for bits in across + [1]:
                direct[bits].wait_send()

        return finish

    def direct_gather(buf, send_sem, recv_sem):
        def copy(bits):
            return pltpu.make_async_remote_copy(
                src_ref=buf.at[m],
                dst_ref=buf.at[m],
                send_sem=send_sem.at[bits],
                recv_sem=recv_sem.at[bits],
                device_id=(s, flip(m, bits)),
                device_id_type=MESH,
            )

        for bits in range(n_mp - 1, 0, -1):
            copy(bits).start()

        def finish():
            for bits in range(1, n_mp):
                copy(bits).wait()

        return finish

    def normalise(buf, dst, count, gain, gain_row):
        step = min(256, count)

        def body(i, carry):
            span = pl.ds(pl.multiple_of(i * step, step), step)
            squares = jnp.zeros((step, 1), jnp.float32)
            for k in range(n_mp):
                value = buf[k, span, :].astype(jnp.float32)
                squares = squares + jnp.sum(value * value, axis=1, keepdims=True)
            scale = lax.rsqrt(squares / (n_mp * width) + epsilon)
            for k in range(n_mp):
                cols = pl.ds(k * width, width)
                value = buf[k, span, :].astype(jnp.float32)
                dst[span, cols] = (value * scale * gain[pl.ds(gain_row, 1), cols]).astype(
                    jnp.bfloat16
                )
            return carry

        lax.fori_loop(0, count // step, body, 0)

    def product(left, right, layer, store):
        columns = right.shape[2]
        step = min(256, columns)

        def body(i, carry):
            cols = pl.ds(pl.multiple_of(i * step, step), step)
            store(
                cols, jnp.dot(left[...], right[layer, :, cols], preferred_element_type=jnp.float32)
            )
            return carry

        lax.fori_loop(0, columns // step, body, 0)

    def project_queries(layer, span):
        def store(cols, value):
            queries[span, cols] = (value * DH ** (-0.5)).astype(jnp.bfloat16)

        product(dec_normed.at[span], wq, layer, store)

    def project_part(cols0, count, first):
        step = min(256, wk.shape[2])
        part = pl.ds(cols0, count)

        def body(i, carry):
            cols = pl.ds(pl.multiple_of(i * step, step), step)
            for index, weight in enumerate((wk, wv)):
                value = jnp.dot(
                    memory[:, part], weight[0, part, cols], preferred_element_type=jnp.float32
                )
                if not first:
                    value = value + kv_acc[index, :, cols]
                kv_acc[index, :, cols] = value
            return carry

        lax.fori_loop(0, wk.shape[2] // step, body, 0)

    def row_scale():
        squares = jnp.sum(square[...], axis=1, keepdims=True)
        return lax.rsqrt(squares / (n_mp * width) + epsilon)

    def project_last(cols0, count):
        step = min(256, wk.shape[2])
        part = pl.ds(cols0, count)
        scale = row_scale()

        def body(i, carry):
            cols = pl.ds(pl.multiple_of(i * step, step), step)
            for index, (weight, dst) in enumerate(((wk, keys), (wv, values))):
                value = kv_acc[index, :, cols] + jnp.dot(
                    memory[:, part], weight[0, part, cols], preferred_element_type=jnp.float32
                )
                dst[:, cols] = (value * scale).astype(jnp.bfloat16)
            return carry

        lax.fori_loop(0, wk.shape[2] // step, body, 0)

    def project_memory(layer):
        scale = row_scale()

        def store_key(cols, value):
            keys[:, cols] = (value * scale).astype(jnp.bfloat16)

        def store_value(cols, value):
            values[:, cols] = (value * scale).astype(jnp.bfloat16)

        product(memory, wk, layer, store_key)
        product(memory, wv, layer, store_value)

    slot_rows = sel.shape[1]
    targets = dec_ref.shape[0]
    per_sentence = targets // n_seq
    layers = wq_ref.shape[0]
    heads = wq_ref.shape[2] // DH

    def attend(first, count):
        def body(i, carry):
            span = pl.ds(pl.multiple_of(i * per_sentence, per_sentence), per_sentence)
            slot_span = pl.ds(pl.multiple_of(i * slot_rows, slot_rows), slot_rows)
            live = mask[i] > 0.5
            columns = [pl.ds(head * DH, DH) for head in range(heads)]
            scores = [
                lax.dot_general(
                    queries[span, cols],
                    keys[slot_span, cols],
                    (((1,), (1,)), ((), ())),
                    preferred_element_type=jnp.float32,
                )
                for cols in columns
            ]
            scores = [jnp.where(live, score, -jnp.inf) for score in scores]
            tops = [jnp.max(score, axis=1, keepdims=True) for score in scores]
            powers = [jnp.exp(score - top) for score, top in zip(scores, tops)]
            sums = [jnp.sum(power, axis=1, keepdims=True) for power in powers]
            weights = [
                (power * (1.0 / total)).astype(jnp.bfloat16) for power, total in zip(powers, sums)
            ]
            for cols, weight in zip(columns, weights):
                attended[span, cols] = jnp.dot(
                    weight, values[slot_span, cols], preferred_element_type=jnp.float32
                ).astype(jnp.bfloat16)
            return carry

        lax.fori_loop(first, first + count, body, 0, unroll=True)

    parts = 2
    part_rows = targets // parts

    def rows_of(part):
        return pl.ds(part * part_rows, part_rows)

    def att_copy(layer, part, slot, source):
        return pltpu.make_async_remote_copy(
            src_ref=att_out.at[layer, part, slot],
            dst_ref=att_in.at[layer, part, source],
            send_sem=att_ps.at[layer, part, slot],
            recv_sem=att_pr.at[layer, part, source],
            device_id=(s, slot),
            device_id_type=MESH,
        )

    def scatter_output(layer, part):
        step = max(width, 256)

        def body(i, carry):
            chip = (i + m // (step // width) + 1) % (n_mp * width // step)
            cols = pl.ds(pl.multiple_of(chip * step, step), step)
            value = jnp.dot(
                attended[rows_of(part), :], wo[layer, :, cols], preferred_element_type=jnp.float32
            ).astype(jnp.bfloat16)
            for j in range(step // width):
                slot = chip * (step // width) + j
                att_out[layer, part, slot] = value[:, j * width : (j + 1) * width]

                @pl.when(slot != m)
                def _():
                    att_copy(layer, part, slot, m).start()

            return carry

        lax.fori_loop(0, n_mp * width // step, body, 0)

    def collect_output(layer, part):
        total = att_out[layer, part, m].astype(jnp.float32)
        for bits in range(1, n_mp):
            peer = flip(m, bits)
            att_copy(layer, part, peer, peer).wait_recv()
            total = total + att_in[layer, part, peer].astype(jnp.float32)
        return total

    own_enc = pltpu.make_async_copy(enc_ref, enc_all.at[m, my_rows], local_sem.at[0])
    own_enc.start()

    def enc_copy(bits):
        return pltpu.make_async_remote_copy(
            src_ref=enc_ref,
            dst_ref=enc_all.at[m, my_rows],
            send_sem=enc_zs.at[bits],
            recv_sem=enc_zr.at[bits],
            device_id=(flip(s, bits), m),
            device_id_type=MESH,
        )

    for bits in (2, 1):
        enc_copy(bits).start()
    across_rows = pl.ds(pl.multiple_of(flip(s, 2) * rows, rows), rows)
    enc_onward = pltpu.make_async_remote_copy(
        src_ref=enc_all.at[m, across_rows],
        dst_ref=enc_all.at[m, across_rows],
        send_sem=enc_zs.at[3],
        recv_sem=enc_zr.at[3],
        device_id=(flip(s, 1), m),
        device_id_type=MESH,
    )
    inner = (s % 2 + s // 2) % 2

    own_in = pltpu.make_async_copy(
        fin_ref.at[:, pl.ds(pl.multiple_of(s * units, units), units)], win.at[s], local_sem.at[1]
    )
    own_in.start()
    own_out = [
        pltpu.make_async_copy(
            fout_ref.at[
                pl.ds(pl.multiple_of(s * units, units), units), pl.ds(j * width, width)
            ],
            wout.at[s, j],
            own_out_sem.at[j],
        )
        for j in range(per_block)
    ]
    for copy in own_out:
        copy.start()
    def in_copy(bits):
        peer = flip(s, bits)
        return pltpu.make_async_remote_copy(
            src_ref=fin_ref.at[:, pl.ds(pl.multiple_of(peer * units, units), units)],
            dst_ref=win.at[s],
            send_sem=in_s.at[bits],
            recv_sem=in_r.at[bits],
            device_id=(peer, m),
            device_id_type=MESH,
        )

    @pl.when(inner == 1)
    def _():
        for bits in (2, 3):
            in_copy(bits).start()

    enc_copy(2).wait_recv()
    enc_onward.start()

    @pl.when(inner == 0)
    def _():
        for bits in (2, 3):
            in_copy(bits).start()

    in_copy(1).start()
    piece = units // 2

    def out_copy(bits, j, k):
        peer = flip_any(bits)
        return pltpu.make_async_remote_copy(
            src_ref=fout_ref.at[
                pl.ds(pl.multiple_of(peer * units + k * piece, piece), piece),
                pl.ds(j * width, width),
            ],
            dst_ref=wout.at[s, j, pl.ds(k * piece, piece)],
            send_sem=out_s.at[bits, j, k],
            recv_sem=out_r.at[bits, j, k],
            device_id=(peer, m),
            device_id_type=MESH,
        )

    def flip_any(bits):
        if isinstance(bits, int):
            return flip(s, bits)
        return flip(s, 2) * (3 - bits) + flip(s, 3) * (bits - 2)

    def across_out(j, k):
        for bits in (3, 2):
            out_copy(bits, j, k).start()

    for j in range(per_block):
        for k in range(2):
            out_copy(1, j, k).start()

    @pl.when(inner == 1)
    def _():
        for j in range(per_block):
            for k in range(2):
                across_out(j, k)

    weight_copies = []
    for index, (src, dst) in enumerate(((wq_ref, wq), (wo_ref, wo))):
        copy = pltpu.make_async_copy(src, dst, w_sem.at[index])
        copy.start()
        weight_copies.append(copy)
    for index, (src, dst) in enumerate(((wk_ref, wk), (wv_ref, wv))):
        for slot, source in enumerate(order):
            copy = pltpu.make_async_copy(
                src.at[:, pl.ds(source * width, width)],
                dst.at[:, pl.ds(slot * width, width)],
                w_sem.at[2 + index * n_mp + slot],
            )
            copy.start()
            weight_copies.append(copy)
    own_dec = pltpu.make_async_copy(dec_ref, dec_all.at[m], local_sem.at[3])
    own_dec.start()
    own_dec.wait()
    finish_dec = plane_gather(dec_all, dec_ps.at[0], dec_pr.at[0])

    own_enc.wait()
    enc_copy(1).wait_recv()
    enc_onward.wait_recv()
    for bits in (2, 1):
        enc_copy(bits).wait_send()
    enc_onward.wait_send()

    plane_gather(enc_all, enc_ps, enc_pr)()

    chunk = min(256, rows)

    normalise(enc_all, normed, total_rows, gain_ref, 0)

    for source in range(n_seq):
        start = jnp.int32(0)
        before = jnp.int32(0)
        for j in range(n_seq):
            start = start + jnp.where(table_ref[source, j] == s, before, 0)
            before = before + lengths_ref[source, j]
        slot_row = lax.broadcasted_iota(jnp.int32, (slot_rows, rows), 0)
        column = lax.broadcasted_iota(jnp.int32, (slot_rows, rows), 1)
        wanted = jnp.minimum(slot_row + start, rows - 1)
        sel[source] = jnp.where(wanted == column, 1.0, 0.0).astype(jnp.bfloat16)
    for source in range(n_seq):
        length = jnp.int32(0)
        for j in range(n_seq):
            length = length + jnp.where(table_ref[source, j] == s, lengths_ref[source, j], 0)
        slot = lax.broadcasted_iota(jnp.int32, (1, slot_rows), 1)
        mask[source] = jnp.where(slot < length, 1.0, 0.0)

    finish_dec()
    normalise(dec_all, dec_normed, targets, dec_gain_ref, 0)
    for copy in weight_copies:
        copy.wait()
    project_queries(0, pl.ds(0, targets))

    own_in.wait()
    for bits in range(1, n_seq):
        in_copy(bits).wait()

    tile = min(256, units)

    def hidden_chunk(i, carry):
        cols = pl.ds(pl.multiple_of((i % (units // tile)) * tile, tile), tile)
        span = pl.ds(pl.multiple_of((i // (units // tile)) * chunk, chunk), chunk)
        acc = jnp.zeros((chunk, tile), jnp.float32)
        for k in range(n_seq):
            acc = acc + jnp.dot(
                normed[span, pl.ds(k * depth, depth)],
                win[k, :, cols],
                preferred_element_type=jnp.float32,
            )
        hidden[span, cols] = jnp.maximum(acc, 0.0).astype(jnp.bfloat16)
        return carry

    lax.fori_loop(0, (total_rows // chunk) * (units // tile), hidden_chunk, 0)

    share = total_rows // n_mp
    per_chunk = chunk // share
    per_source = rows // share
    my_share = pl.ds(pl.multiple_of(m * share, share), share)

    def position(block, j):
        within = (block % 2 + block // 2) % 2
        outside = early + block // (n_seq - 1) + 2 * j
        return within * ((block - 1) * per_block + j) + (1 - within) * outside

    def rs_copy(p, peer, source):
        return pltpu.make_async_remote_copy(
            src_ref=part_out.at[p, pl.ds(pl.multiple_of(peer * share, share), share)],
            dst_ref=part_in.at[p, source],
            send_sem=rs_s.at[p, peer],
            recv_sem=rs_r.at[p, source],
            device_id=(s, peer),
            device_id_type=MESH,
        )

    def send_block(block, j):
        p = position(block, j)

        def rows_chunk(i, carry):
            c = (i + m // per_chunk + 1) % (total_rows // chunk)
            span = pl.ds(pl.multiple_of(c * chunk, chunk), chunk)
            part_out[p, span, :] = jnp.dot(
                hidden[span, :], wout[block, j], preferred_element_type=jnp.float32
            ).astype(jnp.bfloat16)
            for t in range(per_chunk):
                peer = c * per_chunk + t

                @pl.when(peer != m)
                def _():
                    rs_copy(p, peer, m).start()

            return carry

        lax.fori_loop(0, total_rows // chunk, rows_chunk, 0)

    def receive_block(bits, block, j):
        for k in range(2):
            out_copy(bits, j, k).wait_recv()
        send_block(block, j)

    def plane_sum(p):
        total = part_out[p, my_share, :].astype(jnp.float32)
        for bits in range(1, n_mp):
            peer = flip(m, bits)
            rs_copy(p, peer, peer).wait_recv()
            total = total + part_in[p, peer].astype(jnp.float32)
        return total

    def tree_copy(bits, p0, count):
        return pltpu.make_async_remote_copy(
            src_ref=tree_out.at[min(bits, 1), pl.ds(p0, count)],
            dst_ref=tree_in.at[min(bits, 2), pl.ds(p0, count)],
            send_sem=tree_s.at[bits, p0],
            recv_sem=tree_r.at[min(bits, 2), p0],
            device_id=(flip(s, max(bits, 1)), m),
            device_id_type=MESH,
        )

    def residual(p):
        return enc_all[order[p], my_share, :].astype(jnp.float32)

    def tree_up(p0, count):
        for p in range(p0, p0 + count):
            tree_out[0, p] = plane_sum(p).astype(jnp.bfloat16)

        @pl.when(inner == 1)
        def _():
            tree_copy(0, p0, count).start()

    def tree_across(p0, count):
        @pl.when(inner == 0)
        def _():
            tree_copy(0, p0, count).wait_recv()
            for p in range(p0, p0 + count):
                tree_out[1, p] = (
                    tree_out[0, p].astype(jnp.float32) + tree_in[0, p].astype(jnp.float32)
                ).astype(jnp.bfloat16)
            for bits in z_order(n_seq):
                tree_copy(bits, p0, count).start()

    def tree_down(p0, count, enc_buf, first=0):
        def combine(own):
            for p in range(p0, p0 + count):
                total = own[p].astype(jnp.float32) + tree_in[2, p].astype(jnp.float32)
                enc_buf[m, p - p0 + first] = (total + residual(p)).astype(jnp.bfloat16)

        tree_copy(2, p0, count).wait_recv()

        @pl.when(inner == 0)
        def _():
            combine(tree_out.at[1])

        @pl.when(inner == 1)
        def _():
            tree_copy(1, p0, count).wait_recv()
            combine(tree_in.at[1])

    def tree_finish(p0, count):
        @pl.when(inner == 1)
        def _():
            tree_copy(0, p0, count).wait_send()

        @pl.when(inner == 0)
        def _():
            for bits in z_order(n_seq):
                tree_copy(bits, p0, count).wait_send()

    last = early + 2

    def absorb(enc_buf, p0, count):
        for source in range(n_seq):
            span = pl.ds(source * slot_rows, slot_rows)
            total = jnp.zeros((slot_rows, width), jnp.float32)
            for q in range(count):
                block = enc_buf[pl.ds(source * per_source, per_source), q].reshape(rows, width)
                slot = jnp.dot(sel[source], block, preferred_element_type=jnp.float32)
                total = total + slot * slot
                memory[span, pl.ds((p0 + q) * width, width)] = (
                    slot * final_gain_ref[:, pl.ds(order[p0 + q] * width, width)]
                ).astype(jnp.bfloat16)
            if p0 == 0:
                square[span, :] = total
            else:
                square[span, :] = square[span, :] + total

    last = early + 2
    near = 2 - s // 2
    far = 3 - 3 * (s // 2)
    near_bits = 2 + inner

    for j in range(per_block):
        own_out[j].wait()
        send_block(s, j)
    for j in range(per_block):
        receive_block(1, flip(s, 1), j)
    for j in range(per_block - 1):
        receive_block(near_bits, near, j)
    out_copy(near_bits, per_block - 1, 0).wait_recv()

    @pl.when(inner == 0)
    def _():
        out_copy(2, 0, 0).start()

    out_copy(near_bits, per_block - 1, 1).wait_recv()

    @pl.when(inner == 0)
    def _():
        out_copy(2, 0, 1).start()
        for k in range(2):
            out_copy(2, 1, k).start()

    send_block(near, per_block - 1)
    tree_up(0, early)
    tree_across(0, early)

    @pl.when(inner == 0)
    def _():
        for j in range(per_block):
            for k in range(2):
                out_copy(3, j, k).start()

    @pl.when(inner == 1)
    def _():
        receive_block(2, far, 0)
        tree_up(early, 2)
        receive_block(2, far, 1)
        tree_up(last, 2)

    tree_down(0, early, enc_a)
    plane_gather(enc_a, ag_s.at[0], ag_r.at[0])()
    absorb(enc_a, 0, early)
    project_part(0, early * width, True)

    @pl.when(inner == 0)
    def _():
        receive_block(3, far, 0)
        tree_up(early, 2)
        tree_across(early, 2)
        tree_out[0, last + s // 2] = plane_sum(last + s // 2).astype(jnp.bfloat16)
        receive_block(3, far, 1)
        tree_copy(0, last, 2).wait_recv()
        ready = True
        for p in (last + s // 2, last + 1 - s // 2):
            if ready:
                value = tree_out[0, p].astype(jnp.float32)
            else:
                value = plane_sum(p)
            ready = False
            tree_out[1, p] = (value + tree_in[0, p].astype(jnp.float32)).astype(jnp.bfloat16)
            for bits in z_order(n_seq):
                tree_copy(bits, p, 1).start()

    tree_down(early, 2, enc_b)
    finish_b = plane_gather(enc_b, ag_s.at[1], ag_r.at[1])
    for p in range(last, last + 2):
        tree_down(p, 1, enc_c, p - last)
    finish_c = plane_gather(enc_c, ag_s.at[2], ag_r.at[2])
    finish_b()
    absorb(enc_b, early, 2)
    project_part(early * width, 2 * width, False)
    finish_c()
    absorb(enc_c, last, 2)
    project_last(last * width, 2 * width)

    for p in range(n_mp):
        for bits in range(1, n_mp):
            rs_copy(p, flip(m, bits), m).wait_send()
    tree_finish(0, early)
    tree_finish(early, 2)
    @pl.when(inner == 1)
    def _():
        tree_copy(0, last, 2).wait_send()

    @pl.when(inner == 0)
    def _():
        for p in range(last, last + 2):
            for bits in z_order(n_seq):
                tree_copy(bits, p, 1).wait_send()

    for bits in range(1, n_seq):
        for j in range(per_block):
            for k in range(2):
                out_copy(bits, j, k).wait_send()

    state = [dec_ref[rows_of(part), :].astype(jnp.float32) for part in range(parts)]
    per_part = n_seq // parts
    finish = [None] * parts
    for layer in range(layers):
        for part in range(parts):
            if layer > 0:
                finish[part]()
                span = rows_of(part)
                normalise(
                    dec_next.at[layer - 1, part], dec_normed.at[span], part_rows, dec_gain_ref, layer
                )
                project_queries(layer, span)
            attend(part * per_part, per_part)
            scatter_output(layer, part)
        for part in range(parts):
            state[part] = state[part] + collect_output(layer, part)
            if layer + 1 < layers:
                dec_next[layer, part, m] = state[part].astype(jnp.bfloat16)
                index = 1 + layer * parts + part
                finish[part] = direct_gather(
                    dec_next.at[layer, part], dec_ps.at[index], dec_pr.at[index]
                )
                if part == 0:
                    project_memory(layer + 1)
            else:
                out_ref[rows_of(part), :] = state[part].astype(out_ref.dtype)
    for layer in range(layers):
        for part in range(parts):
            for bits in range(1, n_mp):
                att_copy(layer, part, flip(m, bits), m).wait_send()


def whole_fast(
    enc_rows,
    ffn_in,
    ffn_out,
    enc_gain,
    final_gain,
    sent_lengths,
    group_table,
    dec_rows,
    dec_gain,
    w_query,
    w_key,
    w_value,
    w_output,
):
    n_seq, n_mp = lax.axis_size("seq"), lax.axis_size("mp")
    rows, width = enc_rows.shape
    depth, units = ffn_in.shape[0], ffn_in.shape[1] // n_seq
    out_width = ffn_out.shape[1]
    total = rows * n_seq
    full = width * n_mp
    targets = dec_rows.shape[0]
    layers, _, heads_width = w_query.shape
    slot_total = 2 * rows
    per_block = out_width // width
    share = total // n_mp
    half = jnp.bfloat16
    dma = pltpu.SemaphoreType.DMA
    return pl.pallas_call(
        functools.partial(ffn_kernel, n_seq, n_mp),
        out_shape=jax.ShapeDtypeStruct(dec_rows.shape, dec_rows.dtype),
        in_specs=[pl.BlockSpec(memory_space=pltpu.VMEM)] * 3
        + [pl.BlockSpec(memory_space=pltpu.SMEM)] * 2
        + [pl.BlockSpec(memory_space=pltpu.VMEM)] * 2
        + [pl.BlockSpec(memory_space=pl.ANY)] * 6,
        out_specs=pl.BlockSpec(memory_space=pltpu.VMEM),
        scratch_shapes=[
            pltpu.VMEM((n_mp, total, width), half),
            pltpu.VMEM((total, full), half),
            pltpu.VMEM((n_seq, depth, units), half),
            pltpu.VMEM((n_seq, per_block, units, width), half),
            pltpu.VMEM((total, units), half),
            pltpu.VMEM((n_mp, total, width), half),
            pltpu.VMEM((n_mp, n_mp, share, width), half),
            pltpu.VMEM((2, n_mp, share, width), half),
            pltpu.VMEM((3, n_mp, share, width), half),
            pltpu.VMEM((n_mp, n_mp - 4, share, width), half),
            pltpu.VMEM((n_mp, 2, share, width), half),
            pltpu.VMEM((n_mp, 2, share, width), half),
            dma((n_seq,)),
            dma((n_seq,)),
            dma((n_mp,)),
            dma((n_mp,)),
            dma((n_seq,)),
            dma((n_seq,)),
            dma((n_seq, per_block, 2)),
            dma((n_seq, per_block, 2)),
            dma((n_mp, n_mp)),
            dma((n_mp, n_mp)),
            dma((4, n_mp)),
            dma((3, n_mp)),
            dma((3, n_mp)),
            dma((3, n_mp)),
            dma((4,)),
            pltpu.VMEM(w_query.shape, half),
            pltpu.VMEM(w_key.shape, half),
            pltpu.VMEM(w_value.shape, half),
            pltpu.VMEM(w_output.shape, half),
            dma((2 + 2 * n_mp,)),
            pltpu.VMEM((n_mp, targets, width), half),
            pltpu.VMEM((layers, 2, n_mp, targets // 2, width), half),
            pltpu.VMEM((targets, full), half),
            pltpu.VMEM((targets, heads_width), half),
            pltpu.VMEM((slot_total, full), half),
            pltpu.VMEM((slot_total, width), jnp.float32),
            pltpu.VMEM((2, slot_total, heads_width), jnp.float32),
            pltpu.VMEM((slot_total, heads_width), half),
            pltpu.VMEM((slot_total, heads_width), half),
            pltpu.VMEM((targets, heads_width), half),
            pltpu.VMEM((layers, 2, n_mp, targets // 2, width), half),
            pltpu.VMEM((layers, 2, n_mp, targets // 2, width), half),
            dma((2 * layers, n_mp)),
            dma((2 * layers, n_mp)),
            dma((layers, 2, n_mp)),
            dma((layers, 2, n_mp)),
            pltpu.VMEM((n_seq, slot_total // n_seq, rows), half),
            pltpu.VMEM((n_seq, 1, slot_total // n_seq), jnp.float32),
            dma((per_block,)),
        ],
        compiler_params=pltpu.CompilerParams(
            collective_id=0, has_side_effects=True, vmem_limit_bytes=60 * 1024 * 1024
        ),
    )(
        enc_rows,
        enc_gain.reshape(1, full),
        final_gain.reshape(1, full),
        sent_lengths,
        group_table,
        dec_rows,
        dec_gain,
        ffn_in,
        ffn_out,
        w_query,
        w_key,
        w_value,
        w_output,
    )


def fast_shapes(enc_rows, ffn_in, ffn_out, dec_rows, w_query):
    n_seq, n_mp = lax.axis_size("seq"), lax.axis_size("mp")
    power = n_seq == 4 and n_mp == 8 and ffn_out.shape[1] == 2 * enc_rows.shape[1]
    aligned = (
        enc_rows.shape[1] % 128 == 0
        and ffn_in.shape[0] % 128 == 0
        and (ffn_in.shape[1] // n_seq) % 256 == 0
        and ffn_out.shape[1] % enc_rows.shape[1] == 0
        and enc_rows.shape[0] % 256 == 0
        and dec_rows.shape[0] % 256 == 0
        and (2 * enc_rows.shape[0] // n_seq) % 128 == 0
        and w_query.shape[2] % 256 == 0
        and w_query.shape[1] % 256 == 0
    )
    return power and aligned


def shards(
    enc_rows,
    ffn_in,
    ffn_out,
    enc_gain,
    final_gain,
    sent_lengths,
    group_table,
    dec_rows,
    dec_gain,
    w_query,
    w_key,
    w_value,
    w_output,
):
    group_count = lax.axis_size("seq")
    my_group = lax.axis_index("seq")
    col_width = enc_rows.shape[1]
    col_start = lax.axis_index("mp") * col_width
    row_count = enc_rows.shape[0]
    max_length = 2 * row_count // group_count
    fast = fast_shapes(enc_rows, ffn_in, ffn_out, dec_rows, w_query)
    if not fast:
        whole_rows = lax.all_gather(enc_rows, "mp", axis=1, tiled=True)
        normed = rms_scale(whole_rows.astype(jnp.float32), enc_gain).astype(jnp.bfloat16)
        full_in = lax.all_gather(ffn_in, "seq", axis=0, tiled=True)
        inner = jnp.dot(normed, full_in, preferred_element_type=jnp.float32)
        hidden = jnp.maximum(inner, 0.0).astype(jnp.bfloat16)
        partial_out = jnp.dot(
            hidden,
            lax.all_gather(ffn_out, "seq", axis=1, tiled=True),
            preferred_element_type=jnp.float32,
        )
    my_lengths = lax.dynamic_index_in_dim(sent_lengths, my_group, 0, keepdims=False)
    my_targets = lax.dynamic_index_in_dim(group_table, my_group, 0, keepdims=False)
    ordinal = jnp.arange(group_count, dtype=jnp.int32)
    my_starts = jnp.sum(
        jnp.where(ordinal[None, :] < ordinal[:, None], my_lengths[None, :], 0), axis=1
    )
    group_ids = jnp.arange(group_count, dtype=jnp.int32)
    matches = my_targets[None, :] == group_ids[:, None]
    send_starts = jnp.sum(jnp.where(matches, my_starts[None, :], 0), axis=1)
    positions = jnp.arange(max_length, dtype=jnp.int32)
    row_index = jnp.minimum(send_starts[:, None] + positions[None, :], row_count - 1)
    recv_lengths = jnp.sum(jnp.where(group_table == my_group, sent_lengths, 0), axis=1)
    live_mask = positions[None, :] < recv_lengths[:, None]
    if fast:
        return whole_fast(
            enc_rows,
            ffn_in,
            ffn_out,
            enc_gain,
            final_gain,
            sent_lengths,
            group_table,
            dec_rows,
            dec_gain,
            w_query,
            w_key,
            w_value,
            w_output,
        )
    kv_width = w_key.shape[2]
    weight_list = []
    for layer_index in range(LAYERS):
        weight_list.append(w_key[layer_index])
        weight_list.append(w_value[layer_index])
    enc_share = lax.psum_scatter(partial_out, "mp", scatter_dimension=1, tiled=True)
    encoded = enc_rows.astype(jnp.float32) + enc_share
    squares = lax.psum(jnp.sum(encoded * encoded, axis=1), "mp")
    gain_part = lax.dynamic_slice_in_dim(final_gain, col_start, col_width, 0)
    memory = (encoded * lax.rsqrt(squares / D + epsilon)[:, None] * gain_part).astype(jnp.bfloat16)
    blocks = memory[row_index]
    gathered = lax.all_gather(
        lax.all_to_all(blocks, "seq", split_axis=0, concat_axis=0, tiled=True),
        "mp",
        axis=2,
        tiled=True,
    )
    projected = tuple(
        (
            jnp.einsum(
                "std,de->ste", gathered, weight_matrix, preferred_element_type=jnp.float32
            ).astype(jnp.bfloat16)
            for weight_matrix in weight_list
        )
    )
    tgt_rows = dec_rows.shape[0]
    per_sentence = tgt_rows // group_count
    local_heads = kv_width // DH
    final_state = dec_rows.astype(jnp.float32)
    for layer_index in range(LAYERS):
        state_half = lax.all_gather(final_state.astype(jnp.bfloat16), "mp", axis=1, tiled=True)
        normed_rows = rms_scale(state_half.astype(jnp.float32), dec_gain[layer_index]).astype(
            jnp.bfloat16
        )
        queries = (
            jnp.dot(normed_rows, w_query[layer_index], preferred_element_type=jnp.float32)
            * DH ** (-0.5)
        ).astype(jnp.bfloat16)
        query_heads = queries.reshape(group_count, per_sentence, local_heads, DH)
        key_heads = projected[2 * layer_index].reshape(group_count, max_length, local_heads, DH)
        value_heads = projected[2 * layer_index + 1].reshape(
            group_count, max_length, local_heads, DH
        )
        scores = jnp.einsum(
            "sqhd,sthd->shqt", query_heads, key_heads, preferred_element_type=jnp.float32
        )
        scores = jnp.where(live_mask[:, None, None, :], scores, -jnp.inf)
        weights = jax.nn.softmax(scores, axis=-1).astype(jnp.bfloat16)
        attended = jnp.einsum(
            "shqt,sthd->sqhd", weights, value_heads, preferred_element_type=jnp.float32
        ).astype(jnp.bfloat16)
        final_state = final_state + lax.psum_scatter(
            jnp.dot(
                attended.reshape(tgt_rows, kv_width),
                w_output[layer_index],
                preferred_element_type=jnp.float32,
            ).astype(jnp.bfloat16),
            "mp",
            scatter_dimension=1,
            tiled=True,
        ).astype(jnp.float32)
    return final_state.astype(jnp.bfloat16)


def solution(mesh):
    in_specs = (
        P("seq", "mp"),
        P("seq", "mp"),
        P("mp", "seq"),
        P(),
        P(),
        P(),
        P(),
        P("seq", "mp"),
        P(),
        P(None, None, "mp"),
        P(None, None, "mp"),
        P(None, None, "mp"),
        P(None, "mp", None),
    )
    out_specs = P("seq", "mp")
    return jax.shard_map(shards, mesh=mesh, in_specs=in_specs, out_specs=out_specs, check_vma=False)
```
